32 devices in a mesh: tok: 32 (over z, y, x, core).
Axes of the slice: x: 2, y: 2, z: 4, core: 2. Of those that a mesh axis runs over, the one named last changes fastest.
Arguments:
- tokens: bfloat16 [2, 36864, 768], P(None, 'tok'), may hold values from -6 to 6
- segments: int32 [2, 32, 1152], P(None, 'tok'), may hold values from 0 to 23, never falling along the last dimension, each value on 1 to 1024 neighbouring positions
- cotangent: bfloat16 [2, 36864, 768], P(None, 'tok'), may hold values from -6 to 6
- w_proj: bfloat16 [768, 1536], P('tok'), may hold values from -0.21875 to 0.21875
- w_depth: bfloat16 [768, 9], P('tok'), may hold values from -2 to 2
- w_point: bfloat16 [768, 384], P('tok'), may hold values from -0.21875 to 0.21875
- w_kernel: bfloat16 [384, 54], P('tok'), may hold values from -0.4375 to 0.4375
- w_out: bfloat16 [768, 768], P('tok'), may hold values from -0.625 to 0.625
- attn_gain: bfloat16 [768], P('tok'), may hold values from 0.5 to 1.5
- attn_shift: bfloat16 [768], P('tok'), may hold values from -3 to 3
- w_in: bfloat16 [768, 1536], P('tok'), may hold values from -0.3125 to 0.3125
- w_down: bfloat16 [3072, 384], P('tok'), may hold values from -0.21875 to 0.21875
- ffn_gain: bfloat16 [768], P('tok'), may hold values from 0.5 to 1.5
- ffn_shift: bfloat16 [768], P('tok'), may hold values from -3 to 3
Outputs:
- output: bfloat16 [2, 36864, 768], P(None, 'tok')
- grad_tokens: float32 [2, 36864, 768], P(None, 'tok')
- grad_proj: float32 [768, 1536], P('tok')
- grad_depth: float32 [768, 9], P('tok')
- grad_point: float32 [768, 384], P('tok')
- grad_kernel: float32 [384, 54], P('tok')
- grad_out: float32 [768, 768], P('tok')
- grad_attn_gain: float32 [768], P('tok')
- grad_attn_shift: float32 [768], P('tok')
- grad_in: float32 [768, 1536], P('tok')
- grad_down: float32 [3072, 384], P('tok')
- grad_ffn_gain: float32 [768], P('tok')
- grad_ffn_shift: float32 [768], P('tok')
The draws below stay inside these ranges and needn't reach their ends.
Inputs may be any that keep to these rules, and one draw needn't show every extreme that they name: `segments`: each block of 1152 tokens holds 24 whole sequences, numbered in order and never falling along the block; each sequence has 1 to 1024 tokens, and one in every block has exactly 1024.
All inputs are finite; a program needn't handle non-finite values.
Results may differ from the reference program's by a relative error of at most 0.012.
The reference program's roundings to bfloat16 on the way count: a program that leaves them out, or rounds other values in their place, can miss the bound.
Values may be sent and summed in bfloat16 or wider, within the bound.
A program may use at most 384 MiB of HBM per device.

```python
import math
import jax
import jax.numpy as jnp
import numpy as np
from jax import lax

D = 768
FF = 3072
HEADS = 6
KERNEL = 9
TOK_DEV = 1152
SEG_MOST = 1024
SEGS_DEV = 24
MB = 2
TOKENS = 36864
N_TOK = 32


def block_scale(rng, shape, cuts, least, largest):
    def one(axis_at, blocks):
        heights = jax.random.uniform(jax.random.fold_in(jax.random.fold_in(rng, 6), axis_at), (blocks,), jnp.float32, least / len(cuts), largest / len(cuts))
        return jnp.repeat(jnp.exp(heights), shape[axis_at] // blocks).reshape((-1,) + (1,) * (len(shape) - axis_at - 1))

    level = one(*cuts[0])
    for cut in cuts[1:]:
        level = level * one(*cut)
    return level


def profile(number_of, total, bound, slope):
    portions = [(1 << 20) // math.isqrt(rank ** slope) + 1 for rank in range(2, number_of + 1)]
    rest, given = total - bound - (number_of - 1), [1] * (number_of - 1)
    while rest > 0:
        free = [i for i in range(number_of - 1) if given[i] < bound]
        mass, remaining = sum([portions[i] for i in free]), rest
        for i in free:
            more = min(bound - given[i], max(1, remaining * portions[i] // mass), rest)
            given[i] = given[i] + more
            rest = rest - more
    return np.array([bound] + given)


def ragged_sizes(rng, count, total, most, lean):
    if count == 2:
        one = jax.random.randint(rng, (), max(1, total - most), min(most, total - 1) + 1)
        return jnp.stack([one, total - one])
    sizes = jnp.asarray(profile(count, total, most, lean), jnp.int32)
    twos = (count - 1) // 2
    giver, sink = sizes[1:1 + 2 * twos:2], sizes[2:2 + 2 * twos:2]
    slack = jnp.minimum(giver - 1, most - sink)
    shifted = jax.random.randint(jax.random.fold_in(rng, 1), (twos,), 0, 1 << 20) % (slack + 1)
    sizes = sizes.at[1:1 + 2 * twos:2].set(giver - shifted).at[2:2 + 2 * twos:2].set(sink + shifted)
    return sizes[jax.random.permutation(jax.random.fold_in(rng, 2), count)]


def gaussian(key, shape, deviation, most, cuts=(), kind=jnp.bfloat16):
    level = block_scale(key, shape, cuts, -0.22, 0.18) if cuts else 1.0
    entries = jax.random.normal(key, shape, jnp.float32) * deviation * level
    return jnp.minimum(jnp.maximum(entries, -most), most).astype(kind)


def setup_inputs(seed: int = 0) -> dict:
    keys = jax.random.split(jax.random.key(seed), 15)
    return {
        "tokens": gaussian(keys[0], (MB, TOKENS, D), 1.0, 6.0, ((1, 32),)),
        "segments": jax.vmap(lambda own: jnp.searchsorted(jnp.cumsum(ragged_sizes(own, SEGS_DEV, TOK_DEV, SEG_MOST, 2)), jnp.arange(TOK_DEV), side="right"))(jax.random.split(keys[1], MB * N_TOK)).reshape((MB, N_TOK, TOK_DEV)).astype(jnp.int32),
        "cotangent": gaussian(keys[2], (MB, TOKENS, D), 1.0, 6.0, ((1, 32),)),
        "w_proj": gaussian(keys[3], (D, 2 * D), D ** -0.5, 0.21875, ((0, 32),)),
        "w_depth": gaussian(keys[4], (D, KERNEL), KERNEL ** -0.5, 2.0, ((0, 32),)),
        "w_point": gaussian(keys[5], (D, D // 2), D ** -0.5, 0.21875, ((0, 32),)),
        "w_kernel": gaussian(keys[6], (D // 2, HEADS * KERNEL), (D // 4) ** -0.5, 0.4375, ((0, 32),)),
        "w_out": gaussian(keys[7], (D, D), (D // 8) ** -0.5, 0.625, ((0, 32),)),
        "attn_gain": jnp.clip(1.0 + 0.1 * jax.random.normal(keys[8], (D,), jnp.float32), 0.5, 1.5).astype(jnp.bfloat16),
        "attn_shift": gaussian(keys[9], (D,), 0.5, 3.0, ((0, 32),)),
        "w_in": gaussian(keys[10], (D, FF // 2), (D // 2) ** -0.5, 0.3125, ((0, 32),)),
        "w_down": gaussian(keys[11], (FF, D // 2), (FF // 4) ** -0.5, 0.21875, ((0, 32),)),
        "ffn_gain": jnp.clip(1.0 + 0.1 * jax.random.normal(keys[12], (D,), jnp.float32), 0.5, 1.5).astype(jnp.bfloat16),
        "ffn_shift": gaussian(keys[13], (D,), 0.5, 3.0, ((0, 32),)),
    }


norm_eps = 1e-12
HIGH = lax.Precision.HIGHEST

@jax.custom_vjp
def low(v):
    return lax.optimization_barrier(v.astype(jnp.bfloat16)).astype(jnp.float32)

@jax.custom_vjp
def low_back(v):
    return v

def low_keep(v):
    return (low(v), None)

def low_pass(kept, grad):
    return (grad,)

def back_keep(v):
    return (v, None)

def back_low(kept, grad):
    return (low(grad),)
low.defvjp(low_keep, low_pass)
low_back.defvjp(back_keep, back_low)

def both_ways(value):
    return low(low_back(value))

def matmul(left, right):
    return jnp.dot(left, right, precision=HIGH, preferred_element_type=jnp.float32)

def window_mask(seg_ids):
    n_rows = seg_ids.shape[0]
    reach = KERNEL // 2
    padded = jnp.pad(seg_ids, (reach, reach), constant_values=-1)
    return jnp.stack([padded[offset:offset + n_rows] == seg_ids for offset in range(KERNEL)], 1).astype(jnp.float32)

def window_stack(field):
    n_rows = field.shape[0]
    reach = KERNEL // 2
    padded = jnp.pad(field, ((reach, reach), (0, 0)))
    return jnp.stack([padded[offset:offset + n_rows] for offset in range(KERNEL)], 0)

def layer_norm(values, gain, shift):
    centre = values - lax.optimization_barrier(jnp.mean(values, -1, keepdims=True))
    inv_std = lax.rsqrt(lax.optimization_barrier(jnp.mean(centre * centre, -1, keepdims=True)) + norm_eps)
    return centre * inv_std * gain + shift

def forward(x_rows, seg_ids, weights):
    w_proj, w_depth, w_point, w_kernel, w_out, attn_gain, attn_shift, w_in, w_down, ffn_gain, ffn_shift = weights
    n_rows, d_model = x_rows.shape
    d_half = d_model // 2
    head_dim = d_half // HEADS
    valid = window_mask(seg_ids)
    merged = both_ways(matmul(x_rows, w_proj))
    q_rows = merged[:, :d_half]
    k_rows = merged[:, d_half:2 * d_half]
    v_rows = merged[:, 2 * d_half:3 * d_half]
    c_rows = merged[:, 3 * d_half:]
    depth = jnp.einsum('jnc,nj,cj->nc', window_stack(x_rows), valid, w_depth, precision=HIGH)
    depth_low = low(depth)
    span_key = low_back(matmul(depth_low, w_point))
    mixed = low(span_key * q_rows)
    logits = low_back(matmul(mixed, w_kernel)).reshape(n_rows, HEADS, KERNEL)
    taps = jax.nn.softmax(logits, -1) * valid[:, None, :]
    c_wins = window_stack(c_rows).reshape(KERNEL, n_rows, HEADS, head_dim)
    conv_out = jnp.einsum('jnhd,nhj->nhd', c_wins, taps, precision=HIGH).reshape(n_rows, d_half)
    q_heads = q_rows.reshape(n_rows, HEADS, head_dim)
    k_heads = k_rows.reshape(n_rows, HEADS, head_dim)
    v_heads = v_rows.reshape(n_rows, HEADS, head_dim)
    scores = low_back(jnp.einsum('qhd,khd->hqk', q_heads, k_heads, precision=HIGH) * head_dim ** (-0.5))
    same_seq = seg_ids[:, None] == seg_ids[None, :]
    probs = jax.nn.softmax(jnp.where(same_seq[None], scores, -1e+30), -1)
    context = jnp.einsum('hqk,khd->qhd', low(probs), v_heads, precision=HIGH).reshape(n_rows, d_half)
    context = low_back(context)
    joined = low(jnp.concatenate([context, conv_out], 1))
    attended = low_back(matmul(joined, w_out))
    hidden = layer_norm(attended + x_rows, attn_gain, attn_shift)
    hidden_low = low(hidden)
    inner = jnp.einsum('ngi,gio->ngo', hidden_low.reshape(n_rows, 2, d_half), w_in.reshape(2, d_half, -1), precision=HIGH)
    inner = low_back(inner)
    active = low(jax.nn.gelu(inner, approximate=False))
    outer = jnp.einsum('ngh,gho->ngo', active, w_down.reshape(2, -1, d_half), precision=HIGH).reshape(n_rows, d_model)
    outer = low_back(outer)
    return layer_norm(outer + hidden, ffn_gain, ffn_shift)

def reference(tokens, segments, cotangent, w_proj, w_depth, w_point, w_kernel, w_out, attn_gain, attn_shift, w_in, w_down, ffn_gain, ffn_shift):
    weights = tuple((weight.astype(jnp.float32) for weight in (w_proj, w_depth, w_point, w_kernel, w_out, attn_gain, attn_shift, w_in, w_down, ffn_gain, ffn_shift)))
    x_blocks = tokens.reshape(MB * N_TOK, TOK_DEV, D)
    s_blocks = segments.reshape(MB * N_TOK, TOK_DEV)
    c_blocks = cotangent.reshape(MB * N_TOK, TOK_DEV, D)

    def one_block(totals, item):
        x_rows, seg_ids, cot_rows = item
        out_rows, pullback = jax.vjp(lambda x_in, p_in: forward(x_in, seg_ids, p_in), x_rows.astype(jnp.float32), weights)
        d_rows, d_params = pullback(cot_rows.astype(jnp.float32))
        summed = tuple((acc_part + new_part for acc_part, new_part in zip(totals, d_params)))
        return (summed, (out_rows.astype(jnp.bfloat16), d_rows))
    start = tuple((jnp.zeros(weight.shape, jnp.float32) for weight in weights))
    totals, (outs, d_inputs) = lax.scan(one_block, start, (x_blocks, s_blocks, c_blocks))
    return (outs.reshape(MB, TOKENS, D), d_inputs.reshape(MB, TOKENS, D), totals[0], totals[1], totals[2], totals[3], totals[4], totals[5], totals[6], totals[7], totals[8], totals[9], totals[10])
```

```python
from functools import partial

import jax
import jax.numpy as jnp
from jax import lax
from jax.experimental import pallas as pl
from jax.experimental.pallas import tpu as pltpu
from jax.sharding import PartitionSpec as P

HEADS = 6
KERNEL = 9
REACH = 4
SEG_MOST = 1024
NORM_EPS = 1e-12
F32 = jnp.float32
BF16 = jnp.bfloat16
NT = (((1,), (1,)), ((), ()))
NN = (((1,), (0,)), ((), ()))
TN = (((0,), (0,)), ((), ()))
VMEM_CAP = 62 * 1024 * 1024


def mm(a, b, dims=NN):
    return lax.dot_general(a, b, dims, preferred_element_type=F32)


def lanes(shape):
    return lax.broadcasted_iota(jnp.int32, shape, 1)


def split2(v):
    hi = v.astype(BF16)
    return hi, (v - hi.astype(F32)).astype(BF16)


def split3(v):
    hi = v.astype(BF16)
    rest = v - hi.astype(F32)
    mid = rest.astype(BF16)
    return hi, mid, (rest - mid.astype(F32)).astype(BF16)


def expand_taps(tap_rows, e_ref):
    hi, lo = split2(tap_rows)
    both = jnp.concatenate([hi, lo], 0)
    return mm(both, e_ref[...], TN)


def fill_expander(e_ref):
    shape = e_ref.shape
    half = shape[1] // KERNEL
    row = lax.broadcasted_iota(jnp.int32, shape, 0) % 72
    col = lax.broadcasted_iota(jnp.int32, shape, 1)
    want = (col // half) * 8 + (col % half) // 64
    e_ref[...] = jnp.where(row == want, 1.0, 0.0).astype(BF16)


def mask_rows(segb_ref, r0, rows):
    own = segb_ref[pl.ds(8 + r0, rows), :]
    return [
        jnp.where(segb_ref[pl.ds(8 + r0 + o - REACH, rows), :] == own, 1.0, 0.0)
        for o in range(KERNEL)
    ]


def fill_segments(seg_ref, segb_ref, vt_ref):
    t = seg_ref.shape[-1]
    row = seg_ref[...]
    wide = jnp.broadcast_to(row, (128, t))
    segb_ref[0:8, :] = jnp.full((8, 128), -1.0, F32)
    segb_ref[t + 8 : t + 16, :] = jnp.full((8, 128), -1.0, F32)
    segb_ref[8 : t + 8, :] = wide.T
    tall = jnp.broadcast_to(row, (8, t))
    pos = lanes((8, t))
    for o in range(KERNEL):
        d = o - REACH
        moved = pltpu.roll(tall, (-d) % t, 1) if d else tall
        inside = (pos + d >= 0) & (pos + d < t)
        vt_ref[o] = jnp.where(inside & (moved == tall), 1.0, 0.0)


def masked_tiles(t, body):
    full = SEG_MOST // 128

    def inner(i, c):
        body(pl.multiple_of(i * 128, 128), False)
        return c

    lax.fori_loop(1, full - 1, inner, 0)

    def edge(i, c):
        idx = jnp.where(i == 0, 0, i + full - 2)
        body(pl.multiple_of(idx * 128, 128), True)
        return c

    lax.fori_loop(0, t // 128 - full + 2, edge, 0)


def kernel_a(
    s_ref, x_ref, cot_ref, seg_ref, wp_ref, wd_ref, wpt_ref, wk_ref,
    xr_ref, cotr_ref, q_ref, k_ref, v_ref, c_ref, depth_ref, span_ref, mixed_ref, taps_ref, conv_ref,
    raw, xs, segb, vt, cs, lt, e_ref, texp,
):
    t, d = x_ref.shape[1:]
    half = d // 2
    nch = d // 128
    b = pl.program_id(0)
    s = s_ref[b]

    @pl.when(b == 0)
    def _():
        fill_expander(e_ref)
        xs[:, 0:8, :] = jnp.zeros((nch, 8, 128), F32)
        xs[:, t + 8 : t + 16, :] = jnp.zeros((nch, 8, 128), F32)
        cs[:, 0:8, :] = jnp.zeros((nch // 2, 8, 128), F32)
        cs[:, t + 8 : t + 16, :] = jnp.zeros((nch // 2, 8, 128), F32)

    fill_segments(seg_ref, segb, vt)
    for src, dst in ((cot_ref, cotr_ref), (x_ref, xr_ref)):
        for j in range(nch):
            col = pl.ds(j * 128, 128)
            raw[0:t, :] = src[0, :, col].astype(F32)
            raw[t : t + 128, :] = src[0, 0:128, col].astype(F32)
            moved = raw[pl.ds(s, t), :]
            if dst is xr_ref:
                xs[j, 8 : t + 8, :] = moved
            dst[0, :, col] = moved.astype(BF16)

    def depth_tile(r0, masked):
        masks = mask_rows(segb, r0, 128) if masked else None
        for j in range(nch):
            acc = None
            for o in range(KERNEL):
                part = xs[j, pl.ds(8 + r0 + o - REACH, 128), :]
                w = wd_ref[o : o + 1, pl.ds(j * 128, 128)]
                part = part * (masks[o] * w) if masked else part * w
                acc = part if acc is None else acc + part
            depth_ref[0, pl.ds(r0, 128), pl.ds(j * 128, 128)] = acc.astype(BF16)

    masked_tiles(t, depth_tile)

    def proj_tile(i, carry):
        r0 = pl.multiple_of(i * 384, 128)
        rows = pl.ds(r0, 384)
        merged = mm(xr_ref[0, rows, :], wp_ref[...]).astype(BF16)
        q = merged[:, 0:half]
        q_ref[0, rows, :] = q
        k_ref[0, rows, :] = merged[:, half : 2 * half]
        v_ref[0, rows, :] = merged[:, 2 * half : 3 * half]
        c = merged[:, 3 * half :]
        c_ref[0, rows, :] = c
        for j in range(nch // 2):
            cs[j, pl.ds(8 + r0, 384), :] = c[:, j * 128 : (j + 1) * 128].astype(F32)
        span = mm(depth_ref[0, rows, :], wpt_ref[...])
        span_ref[0, rows, :] = span
        mixed = (span * q.astype(F32)).astype(BF16)
        mixed_ref[0, rows, :] = mixed
        lt[:, rows] = mm(wk_ref[...], mixed, NT)
        return carry

    lax.fori_loop(0, t // 384, proj_tile, 0)

    logits = [lt[o * 8 : o * 8 + 8, :] for o in range(KERNEL)]
    top = logits[0]
    for o in range(1, KERNEL):
        top = jnp.maximum(top, logits[o])
    exps = [jnp.exp(v - top) for v in logits]
    total = exps[0]
    for o in range(1, KERNEL):
        total = total + exps[o]
    inv = 1.0 / total
    for o in range(KERNEL):
        tap = exps[o] * inv
        taps_ref[0, o * 8 : o * 8 + 8, :] = tap
        lt[o * 8 : o * 8 + 8, :] = tap * vt[o]

    def conv_tile(i, carry):
        r0 = pl.multiple_of(i * 128, 128)
        rows = pl.ds(r0, 128)
        texp[...] = expand_taps(lt[:, rows], e_ref)
        for j in range(nch // 2):
            acc = None
            for o in range(KERNEL):
                part = cs[j, pl.ds(8 + r0 + o - REACH, 128), :] * texp[:, o * half + j * 128 : o * half + (j + 1) * 128]
                acc = part if acc is None else acc + part
            conv_ref[0, rows, pl.ds(j * 128, 128)] = acc.astype(BF16)
        return carry

    lax.fori_loop(0, t // 128, conv_tile, 0)


def whole(*shape):
    return pl.BlockSpec(shape, lambda *_: (0,) * len(shape), pipeline_mode=pl.Buffered(1))


def per_block(*shape):
    return pl.BlockSpec((1,) + shape, lambda b, *_: (b,) + (0,) * len(shape))


def params(n):
    return pltpu.CompilerParams(dimension_semantics=("arbitrary",) * n, vmem_limit_bytes=VMEM_CAP)


def stage_a(s, x, cot, segr, wp, wd, wpt, wk):
    mb, t, d = x.shape
    half = d // 2
    sds = jax.ShapeDtypeStruct
    out = [
        ((t, d), BF16), ((t, d), BF16), ((t, half), BF16), ((t, half), BF16), ((t, half), BF16), ((t, half), BF16),
        ((t, d), BF16), ((t, half), F32), ((t, half), BF16), ((72, t), F32), ((t, half), BF16),
    ]
    return pl.pallas_call(
        kernel_a,
        out_shape=[sds((mb,) + sh, dt) for sh, dt in out],
        grid_spec=pltpu.PrefetchScalarGridSpec(
            num_scalar_prefetch=1,
            grid=(mb,),
            in_specs=[
                per_block(t, d), per_block(t, d),
                pl.BlockSpec((pl.Squeezed(), 1, t), lambda b, *_: (b, 0, 0)),
                whole(*wp.shape), whole(*wd.shape), whole(*wpt.shape), whole(*wk.shape),
            ],
            out_specs=[per_block(*sh) for sh, _ in out],
            scratch_shapes=[
                pltpu.VMEM((t + 128, 128), F32),
                pltpu.VMEM((d // 128, t + 16, 128), F32),
                pltpu.VMEM((t + 16, 128), F32),
                pltpu.VMEM((KERNEL, 8, t), F32),
                pltpu.VMEM((half // 128, t + 16, 128), F32),
                pltpu.VMEM((72, t), F32),
                pltpu.VMEM((144, KERNEL * half), BF16),
                pltpu.VMEM((128, KERNEL * half), F32),
            ],
        ),
        compiler_params=params(1),
        name="mix_fwd",
    )(s, x, cot, segr, wp, wd, wpt, wk)


QT = 256


def seg_codes(segb, first):
    lane = lanes(segb.shape) - first
    hot = segb == lane.astype(F32)
    inside = (lane >= 0) & (lane < 24)
    return jnp.where(hot & inside, 1.0, 0.0), jnp.where(inside & ~hot, -1e30, 0.0)


def kernel_b(segt_ref, q_ref, k_ref, v_ref, ctx_ref, lse_ref):
    t = q_ref.shape[1]
    tail = t - SEG_MOST
    low_half = lanes((1, 128)) < 64

    def finish(rows, outs, tops):
        both = jnp.where(low_half, outs[0], outs[1])
        sums = jnp.where(low_half, outs[1], outs[0])
        ctx_ref[0, rows, :] = (both / pltpu.roll(sums, 64, 1)).astype(BF16)
        lse_ref[0, rows, :] = jnp.where(low_half, tops[1], tops[0]) + jnp.log(sums)

    def one(q, k, v):
        scores = mm(q, k, NT)
        top = jnp.max(scores, -1, keepdims=True)
        return mm(jnp.exp(scores - top).astype(BF16), v), top

    k = k_ref[0, 0:SEG_MOST, :]
    v = v_ref[0, 0:SEG_MOST, :]
    one_b = jnp.ones((), BF16)
    vs = (jnp.where(low_half, v, one_b), jnp.where(low_half, one_b, v))

    def tile(i, carry):
        rows = pl.ds(pl.multiple_of(i * QT, QT), QT)
        q = q_ref[0, rows, :] * 0.125
        zero = jnp.zeros((), BF16)
        outs = [one(jnp.where(low_half, q, zero), k, vs[0]), one(jnp.where(low_half, zero, q), k, vs[1])]
        finish(rows, [o[0] for o in outs], [o[1] for o in outs])
        return carry

    lax.fori_loop(0, SEG_MOST // QT, tile, 0)
    rows = pl.ds(SEG_MOST, tail)
    q = q_ref[0, rows, :] * 0.125
    kt = k_ref[0, rows, :]
    vt = v_ref[0, rows, :]
    segb = jnp.broadcast_to(segt_ref[...], (128, tail)).T
    outs = []
    for h in range(2):
        hot, pen = seg_codes(segb, 64 - 64 * h)
        mine = low_half if h == 0 else ~low_half
        outs.append(
            one(
                jnp.where(mine, q, pen.astype(BF16)),
                jnp.where(mine, kt, hot.astype(BF16)),
                jnp.where(mine, vt, one_b),
            )
        )
    finish(rows, [o[0] for o in outs], [o[1] for o in outs])


def pair(t):
    return pl.BlockSpec((1, t, 128), lambda b, j: (b, 0, j))


def seg_tail(tail):
    return pl.BlockSpec((pl.Squeezed(), 1, tail), lambda b, *_: (b, 0, 0))


def stage_b(segt, q, k, v):
    mb, t, half = q.shape
    sds = jax.ShapeDtypeStruct
    return pl.pallas_call(
        kernel_b,
        out_shape=[sds((mb, t, half), BF16), sds((mb, t, half), F32)],
        grid=(mb, half // 128),
        in_specs=[seg_tail(t - SEG_MOST), pair(t), pair(t), pair(t)],
        out_specs=[pair(t), pair(t)],
        compiler_params=params(2),
        name="att_fwd",
    )(segt, q, k, v)


ROWS = 384


def norm_fwd(values):
    centre = values - jnp.mean(values, -1, keepdims=True)
    inv_std = lax.rsqrt(jnp.mean(centre * centre, -1, keepdims=True) + NORM_EPS)
    return centre * inv_std, inv_std


def norm_back(grad, normed, inv_std):
    one = jnp.mean(grad, -1, keepdims=True)
    two = jnp.mean(grad * normed, -1, keepdims=True)
    return inv_std * (grad - one - normed * two)


def gelu_both(x):
    z = jnp.abs(x) * 0.7071067811865476
    r = 1.0 / (1.0 + 0.3275911 * z)
    e = jnp.exp(-0.5 * (x * x))
    poly = r * (0.254829592 + r * (-0.284496736 + r * (1.421413741 + r * (-1.453152027 + r * 1.061405429))))
    tail = 0.5 * (poly * e)
    cdf = jnp.where(x < 0, tail, 1.0 - tail)
    return x * cdf, cdf + x * (e * 0.3989422804014327)


def col_sum(v):
    return jnp.sum(v, 0, keepdims=True)


def kernel_c(
    ctx_ref, conv_ref, x_ref, cot_ref, wo_ref, wi_ref, wdn_ref, ln_ref,
    out_ref, dres_ref, dctx_ref, dconv_ref, go_ref, gi_ref, gd_ref, gs_ref,
    joined, act, slope, dinner,
):
    first = (pl.program_id(0) == 0) & (pl.program_id(1) == 0)
    d = x_ref.shape[-1]
    half = d // 2
    hid = wi_ref.shape[1]

    @pl.when(first)
    def _():
        go_ref[...] = jnp.zeros_like(go_ref)
        gi_ref[...] = jnp.zeros_like(gi_ref)
        gd_ref[...] = jnp.zeros_like(gd_ref)
        gs_ref[...] = jnp.zeros_like(gs_ref)

    joined[:, 0:half] = ctx_ref[0]
    joined[:, half:] = conv_ref[0]
    gain1, shift1, gain2, shift2 = (ln_ref[i : i + 1, :] for i in range(4))
    normed1, inv1 = norm_fwd(mm(joined[...], wo_ref[...]) + x_ref[0].astype(F32))
    hidden = normed1 * gain1 + shift1
    hidden_low = hidden.astype(BF16)
    outers = []
    for g in range(2):
        cols = pl.ds(g * hid, hid)
        inner = mm(hidden_low[:, g * half : (g + 1) * half], wi_ref[g * half : (g + 1) * half, :])
        value, deriv = gelu_both(inner)
        act[:, cols] = value.astype(BF16)
        slope[:, cols] = deriv
        outers.append(mm(act[:, cols], wdn_ref[g * hid : (g + 1) * hid, :]))
    normed2, inv2 = norm_fwd(jnp.concatenate(outers, 1) + hidden)
    out_ref[0] = (normed2 * gain2 + shift2).astype(BF16)
    cot = cot_ref[0].astype(F32)
    gs_ref[2:3, :] += col_sum(cot * normed2)
    gs_ref[3:4, :] += col_sum(cot)
    d_sum = norm_back(cot * gain2, normed2, inv2)
    d_outer = d_sum.astype(BF16)
    d_hid = []
    for g in range(2):
        cols = pl.ds(g * hid, hid)
        mine = d_outer[:, g * half : (g + 1) * half]
        d_act = mm(mine, wdn_ref[g * hid : (g + 1) * hid, :], NT)
        gd_ref[:, cols] += mm(mine, act[:, cols], TN)
        dinner[:, cols] = (d_act * slope[:, cols]).astype(BF16)
        d_hid.append(mm(dinner[:, cols], wi_ref[g * half : (g + 1) * half, :], NT))
        gi_ref[g * half : (g + 1) * half, :] += mm(hidden_low[:, g * half : (g + 1) * half], dinner[:, cols], TN)
    d_hidden = jnp.concatenate(d_hid, 1) + d_sum
    gs_ref[0:1, :] += col_sum(d_hidden * normed1)
    gs_ref[1:2, :] += col_sum(d_hidden)
    d_res = norm_back(d_hidden * gain1, normed1, inv1)
    dres_ref[0] = d_res
    d_attn = d_res.astype(BF16)
    d_joined = mm(d_attn, wo_ref[...], NT)
    dctx_ref[0] = d_joined[:, 0:half].astype(BF16)
    dconv_ref[0] = d_joined[:, half:]
    go_ref[...] += mm(joined[...], d_attn, TN)


def stage_c(ctx, conv, x, cot, wo, wi, wdn, ln):
    mb, t, d = x.shape
    half = d // 2
    hid = wi.shape[1]
    sds = jax.ShapeDtypeStruct

    def tile(cols):
        return pl.BlockSpec((1, ROWS, cols), lambda b, i: (b, i, 0))

    return pl.pallas_call(
        kernel_c,
        out_shape=[
            sds((mb, t, d), BF16), sds((mb, t, d), F32), sds((mb, t, half), BF16), sds((mb, t, half), F32),
            sds((d, d), F32), sds((d, hid), F32), sds((half, 2 * hid), F32), sds((8, d), F32),
        ],
        grid=(mb, t // ROWS),
        in_specs=[
            tile(half), tile(half), tile(d), tile(d),
            whole(*wo.shape), whole(*wi.shape), whole(*wdn.shape), whole(*ln.shape),
        ],
        out_specs=[
            tile(d), tile(d), tile(half), tile(half),
            whole(d, d), whole(d, hid), whole(half, 2 * hid), whole(8, d),
        ],
        scratch_shapes=[
            pltpu.VMEM((ROWS, d), BF16),
            pltpu.VMEM((ROWS, 2 * hid), BF16),
            pltpu.VMEM((ROWS, 2 * hid), F32),
            pltpu.VMEM((ROWS, 2 * hid), BF16),
        ],
        compiler_params=params(2),
        name="ffn",
    )(ctx, conv, x, cot, wo, wi, wdn, ln)


KT = 256


def kernel_d(segt_ref, q_ref, k_ref, v_ref, ctx_ref, lse_ref, do_ref, dq_ref, dk_ref, dv_ref, qa, da, dqt):
    t = q_ref.shape[1]
    tail = t - SEG_MOST
    lane = lanes((1, 128))
    low_half = lane < 64
    one_b = jnp.ones((), BF16)
    zero_b = jnp.zeros((), BF16)

    r = lax.broadcasted_iota(jnp.int32, (256, 128), 0) % 128
    c = lax.broadcasted_iota(jnp.int32, (256, 128), 1)
    swap = jnp.where((r < 64) != (c < 64), 1.0, 0.0).astype(BF16)
    prod = do_ref[0].astype(F32) * ctx_ref[0].astype(F32)
    hi, lo = split2(prod)
    dsum = mm(jnp.concatenate([hi, lo], 1), swap)
    q8 = q_ref[0] * 0.125
    do = do_ref[0]
    for stat, src, dst in ((lse_ref[0], q8, qa), (dsum, do, da)):
        pieces = split3(-stat)
        code = jnp.where(
            (lane & 63) == 0, pieces[0], jnp.where((lane & 63) == 1, pieces[1], jnp.where((lane & 63) == 2, pieces[2], zero_b))
        )
        dst[0] = jnp.where(low_half, src, code)
        dst[1] = jnp.where(low_half, code, src)

    def run(key_rows, q_rows, h, codes):
        mark = (lane & 63) < 3
        mine = low_half if h == 0 else ~low_half
        k = k_ref[0, key_rows, :]
        v = v_ref[0, key_rows, :]
        ka = jnp.where(mine, k, jnp.where(mark, one_b, zero_b))
        va = jnp.where(mine, v, jnp.where(mark, one_b, zero_b))
        qh = qa[h, q_rows, :]
        if codes is not None:
            hot, pen = codes
            qh = qh + pen
            ka = ka + hot
        p = jnp.exp(mm(ka, qh, NT))
        dp = mm(va, da[h, q_rows, :], NT)
        ds = (p * dp).astype(BF16)
        dv = mm(p.astype(BF16), do_ref[0, q_rows, :])
        dk = mm(ds, q_ref[0, q_rows, :] * 0.125)
        return ds, dk, dv, k

    main = pl.ds(0, SEG_MOST)

    def tile(i, carry):
        rows = pl.ds(pl.multiple_of(i * KT, KT), KT)
        halves = []
        for h in range(2):
            ds, dk, dv, k = run(rows, main, h, None)
            part = mm(k[:, 64 * h : 64 * h + 64], ds, TN)
            dqt[64 * h : 64 * h + 64, :] = jnp.where(i == 0, part, dqt[64 * h : 64 * h + 64, :] + part)
            halves.append((dk, dv))
        dk_ref[0, rows, :] = jnp.where(low_half, halves[0][0], halves[1][0]).astype(BF16)
        dv_ref[0, rows, :] = jnp.where(low_half, halves[0][1], halves[1][1]).astype(BF16)
        return carry

    dqt[...] = jnp.zeros_like(dqt)
    lax.fori_loop(0, SEG_MOST // KT, tile, 0)
    dq_ref[0, main, :] = dqt[...].T * 0.125

    rows = pl.ds(SEG_MOST, tail)
    segb = jnp.broadcast_to(segt_ref[...], (128, tail)).T
    halves = []
    for h in range(2):
        hot, pen = seg_codes(segb, 64 - 64 * h + 8)
        ds, dk, dv, k = run(rows, rows, h, (hot.astype(BF16), pen.astype(BF16)))
        halves.append((dk, dv, mm(ds, k, TN)))
    for ref, i in ((dk_ref, 0), (dv_ref, 1)):
        ref[0, rows, :] = jnp.where(low_half, halves[0][i], halves[1][i]).astype(BF16)
    dq_ref[0, rows, :] = jnp.where(low_half, halves[0][2], halves[1][2]) * 0.125


def stage_d(segt, q, k, v, ctx, lse, dctx):
    mb, t, half = q.shape
    sds = jax.ShapeDtypeStruct
    return pl.pallas_call(
        kernel_d,
        out_shape=[sds((mb, t, half), F32), sds((mb, t, half), BF16), sds((mb, t, half), BF16)],
        grid=(mb, half // 128),
        in_specs=[seg_tail(t - SEG_MOST)] + [pair(t)] * 6,
        out_specs=[pair(t)] * 3,
        scratch_shapes=[
            pltpu.VMEM((2, t, 128), BF16), pltpu.VMEM((2, t, 128), BF16), pltpu.VMEM((128, SEG_MOST), F32),
        ],
        compiler_params=params(2),
        name="att_bwd",
    )(segt, q, k, v, ctx, lse, dctx)


def kernel_e(
    s_ref, seg_ref, x_ref, out_ref_in, dres_ref, dconv_ref, dq_ref, dk_ref, dv_ref,
    q_ref, c_ref, depth_ref, span_ref, mixed_ref, taps_ref, wp_ref, wd_ref, wpt_ref, wk_ref,
    gx_ref, out_ref, gp_ref, gpt_ref, gk_ref, gdep_ref,
    pad, xs, segb, vt, dcs, dts, e_ref, er_ref, texp, dlt, rt, dm, dl, gacc,
):
    t, d = x_ref.shape[1:]
    half = d // 2
    nch = d // 128
    b = pl.program_id(0)
    s = s_ref[b]

    @pl.when(b == 0)
    def _():
        fill_expander(e_ref)
        row = lax.broadcasted_iota(jnp.int32, er_ref.shape, 0)
        col = lax.broadcasted_iota(jnp.int32, er_ref.shape, 1)
        head = ((row % 768) % half) // 64
        er_ref[...] = jnp.where(col == (row // 768) * 8 + head, 1.0, 0.0).astype(BF16)
        for ref in (xs, dts, dcs):
            n = ref.shape[0]
            ref[:, 0:8, :] = jnp.zeros((n, 8, 128), F32)
            ref[:, t + 8 : t + 16, :] = jnp.zeros((n, 8, 128), F32)
        gp_ref[...] = jnp.zeros_like(gp_ref)
        gpt_ref[...] = jnp.zeros_like(gpt_ref)
        gk_ref[...] = jnp.zeros_like(gk_ref)
        gacc[...] = jnp.zeros_like(gacc)

    fill_segments(seg_ref, segb, vt)
    cw = xs
    for j in range(nch // 2):
        cols = pl.ds(j * 128, 128)
        cw[j, 8 : t + 8, :] = c_ref[0, :, cols].astype(F32)
        dcs[j, 8 : t + 8, :] = dconv_ref[0, :, cols]

    def dtap_tile(i, carry):
        r0 = pl.multiple_of(i * 128, 128)
        rows = pl.ds(r0, 128)
        acc = None
        for o in range(KERNEL):
            his, los = [], []
            for j in range(nch // 2):
                prod = cw[j, pl.ds(8 + r0 + o - REACH, 128), :] * dcs[j, pl.ds(8 + r0, 128), :]
                hi, lo = split2(prod)
                his.append(hi)
                los.append(lo)
            part = mm(jnp.concatenate(his + los, 1), er_ref[o * 768 : (o + 1) * 768, :])
            acc = part if acc is None else acc + part
        dlt[:, rows] = acc.T[0:72, :]
        return carry

    lax.fori_loop(0, t // 128, dtap_tile, 0)

    taps = [taps_ref[0, o * 8 : o * 8 + 8, :] for o in range(KERNEL)]
    dtaps = [dlt[o * 8 : o * 8 + 8, :] * vt[o] for o in range(KERNEL)]
    mean = taps[0] * dtaps[0]
    for o in range(1, KERNEL):
        mean = mean + taps[o] * dtaps[o]
    for o in range(KERNEL):
        dl[o * 8 : o * 8 + 8, :] = taps[o] * (dtaps[o] - mean)
        tv = taps[o] * vt[o]
        move = (o - REACH) % t
        rt[o * 8 : o * 8 + 8, :] = pltpu.roll(tv, move, 1) if move else tv

    def point_tile(i, carry):
        r0 = pl.multiple_of(i * 384, 128)
        rows = pl.ds(r0, 384)
        dlog = dl[:, rows].astype(BF16)
        d_mixed = mm(dlog, wk_ref[...], TN)
        gk_ref[...] += mm(dlog, mixed_ref[0, rows, :])
        d_span = (d_mixed * q_ref[0, rows, :].astype(F32)).astype(BF16)
        dm[rows, 0:half] = (dq_ref[0, rows, :] + d_mixed * span_ref[0, rows, :]).astype(BF16)
        dm[rows, half : 2 * half] = dk_ref[0, rows, :]
        dm[rows, 2 * half : 3 * half] = dv_ref[0, rows, :]
        gpt_ref[...] += mm(depth_ref[0, rows, :], d_span, TN)
        d_depth = mm(d_span, wpt_ref[...], NT)
        for j in range(nch):
            dts[j, pl.ds(8 + r0, 384), :] = d_depth[:, j * 128 : (j + 1) * 128]
        return carry

    lax.fori_loop(0, t // 384, point_tile, 0)

    def dc_tile(i, carry):
        r0 = pl.multiple_of(i * 128, 128)
        rows = pl.ds(r0, 128)
        texp[...] = expand_taps(rt[:, rows], e_ref)
        for j in range(nch // 2):
            acc = None
            for o in range(KERNEL):
                part = dcs[j, pl.ds(8 + r0 - o + REACH, 128), :] * texp[:, o * half + j * 128 : o * half + (j + 1) * 128]
                acc = part if acc is None else acc + part
            dm[rows, pl.ds(3 * half + j * 128, 128)] = acc.astype(BF16)
        return carry

    lax.fori_loop(0, t // 128, dc_tile, 0)

    for j in range(nch):
        xs[j, 8 : t + 8, :] = x_ref[0, :, pl.ds(j * 128, 128)].astype(F32)

    def proj_tile(i, carry):
        r0 = pl.multiple_of(i * 384, 128)
        rows = pl.ds(r0, 384)
        gp_ref[...] += mm(x_ref[0, rows, :], dm[rows, :], TN)
        gx = mm(dm[rows, :], wp_ref[...], NT) + dres_ref[0, rows, :]
        for j in range(nch):
            pad[j, pl.ds(r0, 384), :] = gx[:, j * 128 : (j + 1) * 128]
        return carry

    lax.fori_loop(0, t // 384, proj_tile, 0)

    def depth_tile(r0, masked):
        masks = mask_rows(segb, r0, 128) if masked else None
        for j in range(nch):
            acc = pad[j, pl.ds(r0, 128), :]
            own = dts[j, pl.ds(8 + r0, 128), :]
            for o in range(KERNEL):
                w = wd_ref[KERNEL - 1 - o : KERNEL - o, pl.ds(j * 128, 128)]
                near = dts[j, pl.ds(8 + r0 + o - REACH, 128), :]
                xw = xs[j, pl.ds(8 + r0 + o - REACH, 128), :]
                if masked:
                    near = near * masks[o]
                    xw = xw * masks[o]
                acc = acc + near * w
                term = (own * xw).reshape(16, 8, 128)
                gacc[o, :, pl.ds(j * 128, 128)] += jnp.sum(term, 0)
            pad[j, pl.ds(r0, 128), :] = acc

    masked_tiles(t, depth_tile)

    for j in range(nch):
        cols = pl.ds(j * 128, 128)
        pad[j, pl.ds(t, 128), :] = pad[j, 0:128, :]
        back = t - s
        first = pl.ds(back, 128)
        gx_ref[0, :, cols] = xs[j, 8 : t + 8, :]
        xs[j, 0:128, :] = pad[j, first, :]
        gx_ref[0, 0:128, cols] = xs[j, 0:128, :]
        gx_ref[0, 128:, cols] = pad[j, pl.ds(128 - s, t - 128), :]
        pad[j, 0:t, :] = out_ref_in[0, :, cols].astype(F32)
        pad[j, pl.ds(t, 128), :] = pad[j, 0:128, :]
        out_ref[0, 0:128, cols] = pad[j, first, :].astype(BF16)
        out_ref[0, 128:, cols] = pad[j, pl.ds(128 - s, t - 128), :].astype(BF16)

    @pl.when(b == pl.num_programs(0) - 1)
    def _():
        for o in range(KERNEL):
            gdep_ref[o : o + 1, :] = jnp.sum(gacc[o], 0, keepdims=True)


def stage_e(s, segr, x, out_r, dres, dconv, dq, dk, dv, q, c, depth, span, mixed, taps, wp, wd, wpt, wk):
    mb, t, d = x.shape
    half = d // 2
    sds = jax.ShapeDtypeStruct

    def slow(*shape):
        return pl.BlockSpec((1,) + shape, lambda b, *_: (b,) + (0,) * len(shape), pipeline_mode=pl.Buffered(1))

    return pl.pallas_call(
        kernel_e,
        out_shape=[
            sds((mb, t, d), F32), sds((mb, t, d), BF16), sds(wp.shape, F32), sds(wpt.shape, F32), sds((72, half), F32),
            sds((16, d), F32),
        ],
        grid_spec=pltpu.PrefetchScalarGridSpec(
            num_scalar_prefetch=1,
            grid=(mb,),
            in_specs=[pl.BlockSpec((pl.Squeezed(), 1, t), lambda b, *_: (b, 0, 0))]
            + [slow(t, d), slow(t, d), slow(t, d), slow(t, half), slow(t, half), slow(t, half), slow(t, half)]
            + [slow(t, half), slow(t, half), slow(t, d), slow(t, half), slow(t, half), slow(72, t)]
            + [whole(*w.shape) for w in (wp, wd, wpt, wk)],
            out_specs=[slow(t, d), slow(t, d), whole(*wp.shape), whole(*wpt.shape), whole(72, half), whole(16, d)],
            scratch_shapes=[
                pltpu.VMEM((d // 128, t + 128, 128), F32),
                pltpu.VMEM((d // 128, t + 16, 128), F32),
                pltpu.VMEM((t + 16, 128), F32),
                pltpu.VMEM((KERNEL, 8, t), F32),
                pltpu.VMEM((half // 128, t + 16, 128), F32),
                pltpu.VMEM((d // 128, t + 16, 128), F32),
                pltpu.VMEM((144, KERNEL * half), BF16),
                pltpu.VMEM((KERNEL * 768, 128), BF16),
                pltpu.VMEM((128, KERNEL * half), F32),
                pltpu.VMEM((72, t), F32),
                pltpu.VMEM((72, t), F32),
                pltpu.VMEM((t, 2 * d), BF16),
                pltpu.VMEM((72, t), F32),
                pltpu.VMEM((KERNEL, 8, d), F32),
            ],
        ),
        compiler_params=params(1),
        name="mix_bwd",
    )(s, segr, x, out_r, dres, dconv, dq, dk, dv, q, c, depth, span, mixed, taps, wp, wd, wpt, wk)


def rolled_segments(segments):
    mb, t = segments.shape
    span = t - SEG_MOST + 1
    hit = segments[:, :span] == segments[:, SEG_MOST - 1 :]
    s = jnp.sum(jnp.where(hit, jnp.arange(span, dtype=jnp.int32)[None, :], 0), 1).astype(jnp.int32)
    twice = jnp.concatenate([segments, segments[:, : t - SEG_MOST]], 1).astype(F32)
    rows = [lax.dynamic_slice(twice[b], (s[b],), (t,)) for b in range(mb)]
    return s, jnp.stack(rows)[:, None, :]


def kernel_rows(w_kernel):
    half = w_kernel.shape[0]
    heads = w_kernel.reshape(half, HEADS, KERNEL).transpose(2, 1, 0)
    return jnp.pad(heads, ((0, 0), (0, 8 - HEADS), (0, 0))).reshape(72, half)


def local_step(tokens, segments, cotangent, full):
    wp, wd, wpt, wk, wo, g1, b1, wi, wdn, g2, b2 = full
    d = tokens.shape[-1]
    s, segr = rolled_segments(segments)
    segt = segr[:, :, SEG_MOST:]
    wd_rows = jnp.pad(wd.T.astype(F32), ((0, 16 - KERNEL), (0, 0)))
    wk_rows = kernel_rows(wk)
    ln = jnp.pad(jnp.stack([g1, b1, g2, b2]).astype(F32), ((0, 4), (0, 0)))
    xr, cotr, q, k, v, c, depth, span, mixed, taps, conv = stage_a(s, tokens, cotangent, segr, wp, wd_rows, wpt, wk_rows)
    ctx, lse = stage_b(segt, q, k, v)
    out_r, dres, dctx, dconv, g_out, g_in, g_down_t, g_small = stage_c(ctx, conv, xr, cotr, wo, wi, wdn, ln)
    dq, dk, dv = stage_d(segt, q, k, v, ctx, lse, dctx)
    gx, out, g_proj, g_point, g_kernel_t, g_depth_t = stage_e(
        s, segr, xr, out_r, dres, dconv, dq, dk, dv, q, c, depth, span, mixed, taps, wp, wd_rows, wpt, wk_rows
    )
    g_kernel = g_kernel_t.reshape(KERNEL, 8, -1)[:, :HEADS].transpose(2, 1, 0).reshape(-1, HEADS * KERNEL)
    grads = (
        g_proj, g_depth_t[:KERNEL].T, g_point, g_kernel, g_out, g_small[0], g_small[1], g_in, g_down_t.T,
        g_small[2], g_small[3],
    )
    return out, gx, grads


def shards(tokens, segments, cotangent, *weights):
    full = tuple(lax.all_gather(w, "tok", axis=0, tiled=True) for w in weights)
    out, gx, grads = local_step(tokens, segments[:, 0], cotangent, full)
    owned = tuple(lax.psum_scatter(g, "tok", scatter_dimension=0, tiled=True) for g in grads)
    return (out, gx) + owned


def solution(mesh):
    rows, vec, act = P("tok", None), P("tok"), P(None, "tok", None)
    in_specs = (act, act, act, rows, rows, rows, rows, rows, vec, vec, rows, rows, vec, vec)
    out_specs = (act, act, rows, rows, rows, rows, rows, vec, vec, rows, rows, vec, vec)
    return jax.shard_map(shards, mesh=mesh, in_specs=in_specs, out_specs=out_specs, check_vma=False)
```

```python
from functools import partial

import jax
import jax.numpy as jnp
from jax import lax
from jax.experimental import pallas as pl
from jax.experimental.pallas import tpu as pltpu
from jax.sharding import PartitionSpec as P

HEADS = 6
KERNEL = 9
REACH = 4
SEG_MOST = 1024
NORM_EPS = 1e-12
F32 = jnp.float32
BF16 = jnp.bfloat16
NT = (((1,), (1,)), ((), ()))
NN = (((1,), (0,)), ((), ()))
TN = (((0,), (0,)), ((), ()))
VMEM_CAP = 62 * 1024 * 1024
MESH = pl.DeviceIdType.MESH
PIECE = 24


def mm(a, b, dims=NN):
    return lax.dot_general(a, b, dims, preferred_element_type=F32)


def lanes(shape):
    return lax.broadcasted_iota(jnp.int32, shape, 1)


def split2(v):
    hi = v.astype(BF16)
    return hi, (v - hi.astype(F32)).astype(BF16)


def split3(v):
    hi = v.astype(BF16)
    rest = v - hi.astype(F32)
    mid = rest.astype(BF16)
    return hi, mid, (rest - mid.astype(F32)).astype(BF16)


def partner(me, bit):
    return me + (1 - 2 * lax.rem(lax.div(me, bit), 2)) * bit


def flipped(me, bits, k):
    at = me
    for j, bit in enumerate(bits):
        at = at + (partner(me, bit) - me) * lax.rem(lax.div(k, 1 << j), 2)
    return at


def bit_orders(n):
    one = [1 << b for b in range(n.bit_length() - 1)]
    two = one[:1] + one[2:3] + one[1:2] + one[3:] if len(one) > 2 else one
    return one, two


def greet(n):
    me = lax.axis_index("tok")
    barrier = pltpu.get_barrier_semaphore()
    bits = bit_orders(n)[0]
    for bit in bits:
        pl.semaphore_signal(barrier, inc=1, device_id=(partner(me, bit),), device_id_type=MESH)
    pl.semaphore_wait(barrier, len(bits))


def many(count, body):
    if count <= 4:
        for k in range(count):
            body(k)
    else:
        lax.fori_loop(0, count, lambda k, c: (body(k), c)[1], 0)


class Gather:
    def __init__(self, n, src, dst, order, send, recv, own):
        self.src, self.dst, self.order = src, dst, order[::-1]
        self.send, self.recv, self.own = send, recv, own
        self.me = lax.axis_index("tok")

    def start(self):
        pltpu.make_async_copy(self.src, self.dst.at[self.me], self.own).start()
        self.stage(0)

    def stage(self, s):
        to = partner(self.me, self.order[s])

        def one(k):
            at = flipped(self.me, self.order[:s], k)
            pltpu.make_async_remote_copy(
                src_ref=self.dst.at[at] if s else self.src,
                dst_ref=self.dst.at[at],
                send_sem=self.send.at[s],
                recv_sem=self.recv.at[s],
                device_id=(to,),
                device_id_type=MESH,
            ).start()

        many(1 << s, one)

    def wait(self, sem, s):
        whole = self.dst.at[pl.ds(0, 1 << s)]
        pltpu.make_async_copy(whole, whole, sem.at[s]).wait()

    def step(self, s):
        if s == 1:
            pltpu.make_async_copy(self.src, self.dst.at[self.me], self.own).wait()
        self.wait(self.recv, s - 1)
        self.stage(s)

    def finish(self):
        last = len(self.order) - 1
        self.wait(self.recv, last)
        for s in range(last + 1):
            self.wait(self.send, s)


class Scatter:
    def __init__(self, n, src, first, acc, got, order, send, recv, own):
        self.n, self.src, self.acc, self.got, self.order = n, src, acc, got, order
        self.rows = pl.ds(first, acc.shape[1])
        self.send, self.recv, self.own = send, recv, own
        self.me = lax.axis_index("tok")

    def term(self, k):
        at = flipped(self.me, self.order[::-1], k)
        return self.src.at[at, self.rows]

    def start(self):
        half = self.n // 2
        to = partner(self.me, self.order[0])

        def one(k):
            pltpu.make_async_remote_copy(
                src_ref=self.term(half + k),
                dst_ref=self.got.at[half + k],
                send_sem=self.send.at[0],
                recv_sem=self.recv.at[0],
                device_id=(to,),
                device_id_type=MESH,
            ).start()

        def mine(k):
            pltpu.make_async_copy(self.term(k), self.acc.at[k], self.own).start()

        many(half, one)
        many(half, mine)

    def held(self, s):
        return pl.ds(self.n >> (s + 1), self.n >> (s + 1))

    def wait(self, sem, s):
        ref = self.got.at[self.held(s)]
        pltpu.make_async_copy(ref, ref, sem.at[s]).wait()

    def add(self, s):
        if s == 0:
            pltpu.make_async_copy(self.acc, self.acc, self.own).wait()
        self.wait(self.recv, s)
        count = self.n >> (s + 1)

        def one(k):
            total = self.acc[k].astype(F32) + self.got[count + k].astype(F32)
            self.acc[k] = total.astype(BF16)

        many(count, one)

    def step(self, s):
        self.add(s - 1)
        part = self.acc.at[self.held(s)]
        pltpu.make_async_remote_copy(
            src_ref=part,
            dst_ref=self.got.at[self.held(s)],
            send_sem=self.send.at[s],
            recv_sem=self.recv.at[s],
            device_id=(partner(self.me, self.order[s]),),
            device_id_type=MESH,
        ).start()

    def finish(self, out):
        last = len(self.order) - 1
        self.wait(self.recv, last)
        out[self.rows, :] = self.acc[0].astype(F32) + self.got[1].astype(F32)
        for s in range(last + 1):
            self.wait(self.send, s)


ANY = pl.BlockSpec(memory_space=pl.ANY)


def remote(cid):
    return pltpu.CompilerParams(collective_id=cid, has_side_effects=True, vmem_limit_bytes=VMEM_CAP)


def gather_all(n, shards):
    count = len(shards)
    stages = n.bit_length() - 1
    orders = bit_orders(n)

    def kernel(*refs):
        srcs, dsts, (send, recv, own) = refs[:count], refs[count : 2 * count], refs[2 * count :]
        greet(n)
        plans = [
            Gather(n, srcs[i], dsts[i], orders[i % 2], send.at[i], recv.at[i], own.at[i]) for i in range(count)
        ]
        for g in plans:
            g.start()
        for s in range(1, stages):
            for g in plans:
                g.step(s)
        for g in plans:
            g.finish()

    return pl.pallas_call(
        kernel,
        out_shape=[jax.ShapeDtypeStruct((n,) + w.shape, w.dtype) for w in shards],
        in_specs=[ANY] * count,
        out_specs=[ANY] * count,
        scratch_shapes=[
            pltpu.SemaphoreType.DMA((count, stages)), pltpu.SemaphoreType.DMA((count, stages)),
            pltpu.SemaphoreType.DMA((count,)),
        ],
        compiler_params=remote(0),
        name="gather",
    )(*shards)


def split_rows(rows, parts):
    tiles = rows // 16
    cuts = [tiles * i // parts * 16 for i in range(parts + 1)]
    return [(a, b - a) for a, b in zip(cuts, cuts[1:]) if b > a]


def scatter_all(n, cid, packed, parts):
    stages = n.bit_length() - 1
    orders = bit_orders(n)
    cuts = [(i, a, r) for i, w in enumerate(packed) for a, r in split_rows(w.shape[1], parts)]
    count = len(packed)
    total = len(cuts)

    def kernel(*refs):
        srcs, outs, rest = refs[:count], refs[count : 2 * count], refs[2 * count :]
        accs, gots, (send, recv, own) = rest[:total], rest[total : 2 * total], rest[2 * total :]
        greet(n)
        plans = [
            Scatter(n, srcs[i], a, accs[j], gots[j], orders[j % 2], send.at[j], recv.at[j], own.at[j])
            for j, (i, a, r) in enumerate(cuts)
        ]
        for p in plans:
            p.start()
        for s in range(1, stages):
            for p in plans:
                p.step(s)
        for p, (i, a, r) in zip(plans, cuts):
            p.finish(outs[i])

    bufs = [(r, packed[i].shape[2]) for i, a, r in cuts]
    return pl.pallas_call(
        kernel,
        out_shape=[jax.ShapeDtypeStruct(w.shape[1:], F32) for w in packed],
        in_specs=[ANY] * count,
        out_specs=[pl.BlockSpec(memory_space=pltpu.VMEM)] * count,
        scratch_shapes=[pltpu.VMEM((n // 2,) + b, BF16) for b in bufs]
        + [pltpu.VMEM((n,) + b, BF16) for b in bufs]
        + [
            pltpu.SemaphoreType.DMA((total, stages)), pltpu.SemaphoreType.DMA((total, stages)),
            pltpu.SemaphoreType.DMA((total,)),
        ],
        compiler_params=remote(cid),
        name="scatter",
    )(*packed)


def expand_taps(tap_rows, e_ref):
    hi, lo = split2(tap_rows)
    both = jnp.concatenate([hi, lo], 0)
    return mm(both, e_ref[...], TN)


def fill_expander(e_ref):
    shape = e_ref.shape
    half = shape[1] // KERNEL
    row = lax.broadcasted_iota(jnp.int32, shape, 0) % 72
    col = lax.broadcasted_iota(jnp.int32, shape, 1)
    want = (col // half) * 8 + (col % half) // 64
    e_ref[...] = jnp.where(row == want, 1.0, 0.0).astype(BF16)


def mask_rows(segb_ref, r0, rows):
    own = segb_ref[pl.ds(8 + r0, rows), :]
    return [
        jnp.where(segb_ref[pl.ds(8 + r0 + o - REACH, rows), :] == own, 1.0, 0.0)
        for o in range(KERNEL)
    ]


def fill_segments(seg_ref, segb_ref, vt_ref):
    t = seg_ref.shape[-1]
    row = seg_ref[...]
    wide = jnp.broadcast_to(row, (128, t))
    segb_ref[0:8, :] = jnp.full((8, 128), -1.0, F32)
    segb_ref[t + 8 : t + 16, :] = jnp.full((8, 128), -1.0, F32)
    segb_ref[8 : t + 8, :] = wide.T
    tall = jnp.broadcast_to(row, (8, t))
    pos = lanes((8, t))
    for o in range(KERNEL):
        d = o - REACH
        moved = pltpu.roll(tall, (-d) % t, 1) if d else tall
        inside = (pos + d >= 0) & (pos + d < t)
        vt_ref[o] = jnp.where(inside & (moved == tall), 1.0, 0.0)


def masked_tiles(t, body):
    full = SEG_MOST // 128

    def inner(i, c):
        body(pl.multiple_of(i * 128, 128), False)
        return c

    lax.fori_loop(1, full - 1, inner, 0)

    def edge(i, c):
        idx = jnp.where(i == 0, 0, i + full - 2)
        body(pl.multiple_of(idx * 128, 128), True)
        return c

    lax.fori_loop(0, t // 128 - full + 2, edge, 0)


def unpack_small(sm_ref, wd_ref, wk_ref):
    d = sm_ref.shape[0]
    for j in range(d // 128):
        rows = pl.ds(j * 128, 128)
        wd_ref[:, rows] = sm_ref[rows, 0:128].astype(F32).T[0:24, :]
    row = lax.broadcasted_iota(jnp.int32, (d, d // 2), 0)
    col = lax.broadcasted_iota(jnp.int32, (d, d // 2), 1)
    piece = row % PIECE
    pick = jnp.where((piece < PIECE // 2) & (row // PIECE * (PIECE // 2) + piece == col), 1.0, 0.0).astype(BF16)
    wk_ref[...] = mm(sm_ref[:, 128:256], pick, TN)[0:72, :].astype(BF16)


def kernel_a(
    s_ref, x_ref, cot_ref, seg_ref, wp_ref, sm_ref, wpt_ref,
    xr_ref, cotr_ref, q_ref, k_ref, v_ref, c_ref, depth_ref, span_ref, mixed_ref, taps_ref, conv_ref, wd_ref, wk_ref,
    raw, xs, segb, vt, cs, lt, e_ref, texp,
):
    t, d = x_ref.shape[1:]
    half = d // 2
    nch = d // 128
    b = pl.program_id(0)
    s = s_ref[b]

    @pl.when(b == 0)
    def _():
        fill_expander(e_ref)
        unpack_small(sm_ref, wd_ref, wk_ref)
        xs[:, 0:8, :] = jnp.zeros((nch, 8, 128), F32)
        xs[:, t + 8 : t + 16, :] = jnp.zeros((nch, 8, 128), F32)
        cs[:, 0:8, :] = jnp.zeros((nch // 2, 8, 128), F32)
        cs[:, t + 8 : t + 16, :] = jnp.zeros((nch // 2, 8, 128), F32)

    fill_segments(seg_ref, segb, vt)
    for src, dst in ((cot_ref, cotr_ref), (x_ref, xr_ref)):
        for j in range(nch):
            col = pl.ds(j * 128, 128)
            raw[0:t, :] = src[0, :, col].astype(F32)
            raw[t : t + 128, :] = src[0, 0:128, col].astype(F32)
            moved = raw[pl.ds(s, t), :]
            if dst is xr_ref:
                xs[j, 8 : t + 8, :] = moved
            dst[0, :, col] = moved.astype(BF16)

    def depth_tile(r0, masked):
        masks = mask_rows(segb, r0, 128) if masked else None
        for j in range(nch):
            acc = None
            for o in range(KERNEL):
                part = xs[j, pl.ds(8 + r0 + o - REACH, 128), :]
                w = wd_ref[o : o + 1, pl.ds(j * 128, 128)]
                part = part * (masks[o] * w) if masked else part * w
                acc = part if acc is None else acc + part
            depth_ref[0, pl.ds(r0, 128), pl.ds(j * 128, 128)] = acc.astype(BF16)

    masked_tiles(t, depth_tile)

    def proj_tile(i, carry):
        r0 = pl.multiple_of(i * 384, 128)
        rows = pl.ds(r0, 384)
        merged = mm(xr_ref[0, rows, :], wp_ref[...]).astype(BF16)
        q = merged[:, 0:half]
        q_ref[0, rows, :] = q
        k_ref[0, rows, :] = merged[:, half : 2 * half]
        v_ref[0, rows, :] = merged[:, 2 * half : 3 * half]
        c = merged[:, 3 * half :]
        c_ref[0, rows, :] = c
        for j in range(nch // 2):
            cs[j, pl.ds(8 + r0, 384), :] = c[:, j * 128 : (j + 1) * 128].astype(F32)
        span = mm(depth_ref[0, rows, :], wpt_ref[...])
        span_ref[0, rows, :] = span
        mixed = (span * q.astype(F32)).astype(BF16)
        mixed_ref[0, rows, :] = mixed
        lt[:, rows] = mm(wk_ref[...], mixed, NT)
        return carry

    lax.fori_loop(0, t // 384, proj_tile, 0)

    logits = [lt[o * 8 : o * 8 + 8, :] for o in range(KERNEL)]
    top = logits[0]
    for o in range(1, KERNEL):
        top = jnp.maximum(top, logits[o])
    exps = [jnp.exp(v - top) for v in logits]
    total = exps[0]
    for o in range(1, KERNEL):
        total = total + exps[o]
    inv = 1.0 / total
    for o in range(KERNEL):
        tap = exps[o] * inv
        taps_ref[0, o * 8 : o * 8 + 8, :] = tap
        lt[o * 8 : o * 8 + 8, :] = tap * vt[o]

    def conv_tile(i, carry):
        r0 = pl.multiple_of(i * 128, 128)
        rows = pl.ds(r0, 128)
        texp[...] = expand_taps(lt[:, rows], e_ref)
        for j in range(nch // 2):
            acc = None
            for o in range(KERNEL):
                part = cs[j, pl.ds(8 + r0 + o - REACH, 128), :] * texp[:, o * half + j * 128 : o * half + (j + 1) * 128]
                acc = part if acc is None else acc + part
            conv_ref[0, rows, pl.ds(j * 128, 128)] = acc.astype(BF16)
        return carry

    lax.fori_loop(0, t // 128, conv_tile, 0)


def whole(*shape):
    return pl.BlockSpec(shape, lambda *_: (0,) * len(shape), pipeline_mode=pl.Buffered(1))


def per_block(*shape):
    return pl.BlockSpec((1,) + shape, lambda b, *_: (b,) + (0,) * len(shape))


def params(n):
    return pltpu.CompilerParams(dimension_semantics=("arbitrary",) * n, vmem_limit_bytes=VMEM_CAP)


def stage_a(s, x, cot, segr, wp, sm, wpt):
    mb, t, d = x.shape
    half = d // 2
    sds = jax.ShapeDtypeStruct
    out = [
        ((t, d), BF16), ((t, d), BF16), ((t, half), BF16), ((t, half), BF16), ((t, half), BF16), ((t, half), BF16),
        ((t, d), BF16), ((t, half), F32), ((t, half), BF16), ((72, t), F32), ((t, half), BF16),
    ]
    return pl.pallas_call(
        kernel_a,
        out_shape=[sds((mb,) + sh, dt) for sh, dt in out] + [sds((24, d), F32), sds((72, half), BF16)],
        grid_spec=pltpu.PrefetchScalarGridSpec(
            num_scalar_prefetch=1,
            grid=(mb,),
            in_specs=[
                per_block(t, d), per_block(t, d),
                pl.BlockSpec((pl.Squeezed(), 1, t), lambda b, *_: (b, 0, 0)),
                whole(*wp.shape), whole(*sm.shape), whole(*wpt.shape),
            ],
            out_specs=[per_block(*sh) for sh, _ in out] + [whole(24, d), whole(72, half)],
            scratch_shapes=[
                pltpu.VMEM((t + 128, 128), F32),
                pltpu.VMEM((d // 128, t + 16, 128), F32),
                pltpu.VMEM((t + 16, 128), F32),
                pltpu.VMEM((KERNEL, 8, t), F32),
                pltpu.VMEM((half // 128, t + 16, 128), F32),
                pltpu.VMEM((72, t), F32),
                pltpu.VMEM((144, KERNEL * half), BF16),
                pltpu.VMEM((128, KERNEL * half), F32),
            ],
        ),
        compiler_params=params(1),
        name="mix_fwd",
    )(s, x, cot, segr, wp, sm, wpt)


QT = 256


def seg_codes(segb, first):
    lane = lanes(segb.shape) - first
    hot = segb == lane.astype(F32)
    inside = (lane >= 0) & (lane < 24)
    return jnp.where(hot & inside, 1.0, 0.0), jnp.where(inside & ~hot, -1e30, 0.0)


def kernel_b(segt_ref, q_ref, k_ref, v_ref, ctx_ref, lse_ref):
    t = q_ref.shape[1]
    tail = t - SEG_MOST
    low_half = lanes((1, 128)) < 64

    def finish(rows, outs, tops):
        both = jnp.where(low_half, outs[0], outs[1])
        sums = jnp.where(low_half, outs[1], outs[0])
        ctx_ref[0, rows, :] = (both / pltpu.roll(sums, 64, 1)).astype(BF16)
        lse_ref[0, rows, :] = jnp.where(low_half, tops[1], tops[0]) + jnp.log(sums)

    def one(q, k, v):
        scores = mm(q, k, NT)
        top = jnp.max(scores, -1, keepdims=True)
        return mm(jnp.exp(scores - top).astype(BF16), v), top

    k = k_ref[0, 0:SEG_MOST, :]
    v = v_ref[0, 0:SEG_MOST, :]
    one_b = jnp.ones((), BF16)
    vs = (jnp.where(low_half, v, one_b), jnp.where(low_half, one_b, v))

    def tile(i, carry):
        rows = pl.ds(pl.multiple_of(i * QT, QT), QT)
        q = q_ref[0, rows, :] * 0.125
        zero = jnp.zeros((), BF16)
        outs = [one(jnp.where(low_half, q, zero), k, vs[0]), one(jnp.where(low_half, zero, q), k, vs[1])]
        finish(rows, [o[0] for o in outs], [o[1] for o in outs])
        return carry

    lax.fori_loop(0, SEG_MOST // QT, tile, 0)
    rows = pl.ds(SEG_MOST, tail)
    q = q_ref[0, rows, :] * 0.125
    kt = k_ref[0, rows, :]
    vt = v_ref[0, rows, :]
    segb = jnp.broadcast_to(segt_ref[...], (128, tail)).T
    outs = []
    for h in range(2):
        hot, pen = seg_codes(segb, 64 - 64 * h)
        mine = low_half if h == 0 else ~low_half
        outs.append(
            one(
                jnp.where(mine, q, pen.astype(BF16)),
                jnp.where(mine, kt, hot.astype(BF16)),
                jnp.where(mine, vt, one_b),
            )
        )
    finish(rows, [o[0] for o in outs], [o[1] for o in outs])


def pair(t):
    return pl.BlockSpec((1, t, 128), lambda b, j: (b, 0, j))


def seg_tail(tail):
    return pl.BlockSpec((pl.Squeezed(), 1, tail), lambda b, *_: (b, 0, 0))


def stage_b(segt, q, k, v):
    mb, t, half = q.shape
    sds = jax.ShapeDtypeStruct
    return pl.pallas_call(
        kernel_b,
        out_shape=[sds((mb, t, half), BF16), sds((mb, t, half), F32)],
        grid=(mb, half // 128),
        in_specs=[seg_tail(t - SEG_MOST), pair(t), pair(t), pair(t)],
        out_specs=[pair(t), pair(t)],
        compiler_params=params(2),
        name="att_fwd",
    )(segt, q, k, v)


ROWS = 384


def norm_fwd(values):
    centre = values - jnp.mean(values, -1, keepdims=True)
    inv_std = lax.rsqrt(jnp.mean(centre * centre, -1, keepdims=True) + NORM_EPS)
    return centre * inv_std, inv_std


def norm_back(grad, normed, inv_std):
    one = jnp.mean(grad, -1, keepdims=True)
    two = jnp.mean(grad * normed, -1, keepdims=True)
    return inv_std * (grad - one - normed * two)


def gelu_both(x):
    z = jnp.abs(x) * 0.7071067811865476
    r = 1.0 / (1.0 + 0.3275911 * z)
    e = jnp.exp(-0.5 * (x * x))
    poly = r * (0.254829592 + r * (-0.284496736 + r * (1.421413741 + r * (-1.453152027 + r * 1.061405429))))
    tail = 0.5 * (poly * e)
    cdf = jnp.where(x < 0, tail, 1.0 - tail)
    return x * cdf, cdf + x * (e * 0.3989422804014327)


def col_sum(v):
    return jnp.sum(v, 0, keepdims=True)


def kernel_c(
    ctx_ref, conv_ref, x_ref, cot_ref, wo_ref, wi_ref, wdn_ref, ln_ref,
    out_ref, dres_ref, dctx_ref, dconv_ref, gf_ref, gs_ref,
    joined, act, slope, dinner, go_ref, gi_ref, gd_ref,
):
    first = (pl.program_id(0) == 0) & (pl.program_id(1) == 0)
    last = (pl.program_id(0) == pl.num_programs(0) - 1) & (pl.program_id(1) == pl.num_programs(1) - 1)
    d = x_ref.shape[-1]
    half = d // 2
    hid = wi_ref.shape[1]

    @pl.when(first)
    def _():
        go_ref[...] = jnp.zeros_like(go_ref)
        gi_ref[...] = jnp.zeros_like(gi_ref)
        gd_ref[...] = jnp.zeros_like(gd_ref)
        gs_ref[...] = jnp.zeros_like(gs_ref)

    joined[:, 0:half] = ctx_ref[0]
    joined[:, half:] = conv_ref[0]
    gain1, shift1, gain2, shift2 = (ln_ref[16 + i : 17 + i, :] for i in range(4))
    normed1, inv1 = norm_fwd(mm(joined[...], wo_ref[...]) + x_ref[0].astype(F32))
    hidden = normed1 * gain1 + shift1
    hidden_low = hidden.astype(BF16)
    outers = []
    for g in range(2):
        cols = pl.ds(g * hid, hid)
        inner = mm(hidden_low[:, g * half : (g + 1) * half], wi_ref[g * half : (g + 1) * half, :])
        value, deriv = gelu_both(inner)
        act[:, cols] = value.astype(BF16)
        slope[:, cols] = deriv
        outers.append(mm(act[:, cols], wdn_ref[g * hid : (g + 1) * hid, :]))
    normed2, inv2 = norm_fwd(jnp.concatenate(outers, 1) + hidden)
    out_ref[0] = (normed2 * gain2 + shift2).astype(BF16)
    cot = cot_ref[0].astype(F32)
    gs_ref[2:3, :] += col_sum(cot * normed2)
    gs_ref[3:4, :] += col_sum(cot)
    d_sum = norm_back(cot * gain2, normed2, inv2)
    d_outer = d_sum.astype(BF16)
    d_hid = []
    for g in range(2):
        cols = pl.ds(g * hid, hid)
        mine = d_outer[:, g * half : (g + 1) * half]
        d_act = mm(mine, wdn_ref[g * hid : (g + 1) * hid, :], NT)
        gd_ref[:, cols] += mm(mine, act[:, cols], TN)
        dinner[:, cols] = (d_act * slope[:, cols]).astype(BF16)
        d_hid.append(mm(dinner[:, cols], wi_ref[g * half : (g + 1) * half, :], NT))
        gi_ref[g * half : (g + 1) * half, :] += mm(hidden_low[:, g * half : (g + 1) * half], dinner[:, cols], TN)
    d_hidden = jnp.concatenate(d_hid, 1) + d_sum
    gs_ref[0:1, :] += col_sum(d_hidden * normed1)
    gs_ref[1:2, :] += col_sum(d_hidden)
    d_res = norm_back(d_hidden * gain1, normed1, inv1)
    dres_ref[0] = d_res
    d_attn = d_res.astype(BF16)
    d_joined = mm(d_attn, wo_ref[...], NT)
    dctx_ref[0] = d_joined[:, 0:half].astype(BF16)
    dconv_ref[0] = d_joined[:, half:]
    go_ref[...] += mm(joined[...], d_attn, TN)

    @pl.when(last)
    def _():
        n, _, _ = gf_ref.shape
        rows = d // n
        tall = 2 * hid // n

        def emit(p, c):
            at = pl.ds(pl.multiple_of(p * rows, 8), rows)
            gi = gi_ref[at, :]
            go = go_ref[at, :]
            parts = [gi[:, j * half : (j + 1) * half] for j in range(hid // half)] + [go[:, 0:half], go[:, half:]]
            gf_ref[p, tall : tall + rows * len(parts), :] = jnp.concatenate(parts, 0).astype(BF16)
            return c

        lax.fori_loop(0, n, emit, 0)

        step = 4
        wide = step * tall

        def emit_down(i, c):
            block = gd_ref[:, pl.ds(pl.multiple_of(i * wide, 128), wide)].T.astype(BF16)
            for j in range(step):
                gf_ref[i * step + j, 0:tall, :] = block[j * tall : (j + 1) * tall, :]
            return c

        lax.fori_loop(0, n // step, emit_down, 0)


def stage_c(n, ctx, conv, x, cot, wo, wi, wdn, ln):
    mb, t, d = x.shape
    half = d // 2
    hid = wi.shape[1]
    packed = (d * d + d * hid + 2 * hid * half) // (n * half)
    sds = jax.ShapeDtypeStruct

    def tile(cols):
        return pl.BlockSpec((1, ROWS, cols), lambda b, i: (b, i, 0))

    return pl.pallas_call(
        kernel_c,
        out_shape=[
            sds((mb, t, d), BF16), sds((mb, t, d), F32), sds((mb, t, half), BF16), sds((mb, t, half), F32),
            sds((n, packed, half), BF16), sds((8, d), F32),
        ],
        grid=(mb, t // ROWS),
        in_specs=[
            tile(half), tile(half), tile(d), tile(d),
            whole(*wo.shape), whole(*wi.shape), whole(*wdn.shape), whole(*ln.shape),
        ],
        out_specs=[
            tile(d), tile(d), tile(half), tile(half),
            whole(n, packed, half), whole(8, d),
        ],
        scratch_shapes=[
            pltpu.VMEM((ROWS, d), BF16),
            pltpu.VMEM((ROWS, 2 * hid), BF16),
            pltpu.VMEM((ROWS, 2 * hid), F32),
            pltpu.VMEM((ROWS, 2 * hid), BF16),
            pltpu.VMEM((d, d), F32),
            pltpu.VMEM((d, hid), F32),
            pltpu.VMEM((half, 2 * hid), F32),
        ],
        compiler_params=params(2),
        name="ffn",
    )(ctx, conv, x, cot, wo, wi, wdn, ln)


KT = 256


def kernel_d(segt_ref, q_ref, k_ref, v_ref, ctx_ref, lse_ref, do_ref, dq_ref, dk_ref, dv_ref, qa, da, dqt):
    t = q_ref.shape[1]
    tail = t - SEG_MOST
    lane = lanes((1, 128))
    low_half = lane < 64
    one_b = jnp.ones((), BF16)
    zero_b = jnp.zeros((), BF16)

    r = lax.broadcasted_iota(jnp.int32, (256, 128), 0) % 128
    c = lax.broadcasted_iota(jnp.int32, (256, 128), 1)
    swap = jnp.where((r < 64) != (c < 64), 1.0, 0.0).astype(BF16)
    prod = do_ref[0].astype(F32) * ctx_ref[0].astype(F32)
    hi, lo = split2(prod)
    dsum = mm(jnp.concatenate([hi, lo], 1), swap)
    q8 = q_ref[0] * 0.125
    do = do_ref[0]
    for stat, src, dst in ((lse_ref[0], q8, qa), (dsum, do, da)):
        pieces = split3(-stat)
        code = jnp.where(
            (lane & 63) == 0, pieces[0], jnp.where((lane & 63) == 1, pieces[1], jnp.where((lane & 63) == 2, pieces[2], zero_b))
        )
        dst[0] = jnp.where(low_half, src, code)
        dst[1] = jnp.where(low_half, code, src)

    def run(key_rows, q_rows, h, codes):
        mark = (lane & 63) < 3
        mine = low_half if h == 0 else ~low_half
        k = k_ref[0, key_rows, :]
        v = v_ref[0, key_rows, :]
        ka = jnp.where(mine, k, jnp.where(mark, one_b, zero_b))
        va = jnp.where(mine, v, jnp.where(mark, one_b, zero_b))
        qh = qa[h, q_rows, :]
        if codes is not None:
            hot, pen = codes
            qh = qh + pen
            ka = ka + hot
        p = jnp.exp(mm(ka, qh, NT))
        dp = mm(va, da[h, q_rows, :], NT)
        ds = (p * dp).astype(BF16)
        dv = mm(p.astype(BF16), do_ref[0, q_rows, :])
        dk = mm(ds, q_ref[0, q_rows, :] * 0.125)
        return ds, dk, dv, k

    main = pl.ds(0, SEG_MOST)

    def tile(i, carry):
        rows = pl.ds(pl.multiple_of(i * KT, KT), KT)
        halves = []
        for h in range(2):
            ds, dk, dv, k = run(rows, main, h, None)
            part = mm(k[:, 64 * h : 64 * h + 64], ds, TN)
            dqt[64 * h : 64 * h + 64, :] = jnp.where(i == 0, part, dqt[64 * h : 64 * h + 64, :] + part)
            halves.append((dk, dv))
        dk_ref[0, rows, :] = jnp.where(low_half, halves[0][0], halves[1][0]).astype(BF16)
        dv_ref[0, rows, :] = jnp.where(low_half, halves[0][1], halves[1][1]).astype(BF16)
        return carry

    dqt[...] = jnp.zeros_like(dqt)
    lax.fori_loop(0, SEG_MOST // KT, tile, 0)
    dq_ref[0, main, :] = dqt[...].T * 0.125

    rows = pl.ds(SEG_MOST, tail)
    segb = jnp.broadcast_to(segt_ref[...], (128, tail)).T
    halves = []
    for h in range(2):
        hot, pen = seg_codes(segb, 64 - 64 * h + 8)
        ds, dk, dv, k = run(rows, rows, h, (hot.astype(BF16), pen.astype(BF16)))
        halves.append((dk, dv, mm(ds, k, TN)))
    for ref, i in ((dk_ref, 0), (dv_ref, 1)):
        ref[0, rows, :] = jnp.where(low_half, halves[0][i], halves[1][i]).astype(BF16)
    dq_ref[0, rows, :] = jnp.where(low_half, halves[0][2], halves[1][2]) * 0.125


def stage_d(segt, q, k, v, ctx, lse, dctx):
    mb, t, half = q.shape
    sds = jax.ShapeDtypeStruct
    return pl.pallas_call(
        kernel_d,
        out_shape=[sds((mb, t, half), F32), sds((mb, t, half), BF16), sds((mb, t, half), BF16)],
        grid=(mb, half // 128),
        in_specs=[seg_tail(t - SEG_MOST)] + [pair(t)] * 6,
        out_specs=[pair(t)] * 3,
        scratch_shapes=[
            pltpu.VMEM((2, t, 128), BF16), pltpu.VMEM((2, t, 128), BF16), pltpu.VMEM((128, SEG_MOST), F32),
        ],
        compiler_params=params(2),
        name="att_bwd",
    )(segt, q, k, v, ctx, lse, dctx)


def kernel_e(
    s_ref, seg_ref, x_ref, out_ref_in, dres_ref, dconv_ref, dq_ref, dk_ref, dv_ref,
    q_ref, c_ref, depth_ref, span_ref, mixed_ref, taps_ref, wp_ref, wd_ref, wpt_ref, wk_ref, gs_ref,
    gx_ref, out_ref, gm_ref,
    pad, xs, segb, vt, dcs, dts, e_ref, er_ref, texp, dlt, rt, dm, dl, gacc, gp_ref, gpt_ref, gk_ref, small,
):
    t, d = x_ref.shape[1:]
    half = d // 2
    nch = d // 128
    b = pl.program_id(0)
    s = s_ref[b]

    @pl.when(b == 0)
    def _():
        fill_expander(e_ref)
        row = lax.broadcasted_iota(jnp.int32, er_ref.shape, 0)
        col = lax.broadcasted_iota(jnp.int32, er_ref.shape, 1)
        head = ((row % 768) % half) // 64
        er_ref[...] = jnp.where(col == (row // 768) * 8 + head, 1.0, 0.0).astype(BF16)
        for ref in (xs, dts, dcs):
            n = ref.shape[0]
            ref[:, 0:8, :] = jnp.zeros((n, 8, 128), F32)
            ref[:, t + 8 : t + 16, :] = jnp.zeros((n, 8, 128), F32)
        gp_ref[...] = jnp.zeros_like(gp_ref)
        gpt_ref[...] = jnp.zeros_like(gpt_ref)
        gk_ref[...] = jnp.zeros_like(gk_ref)
        gacc[...] = jnp.zeros_like(gacc)

    fill_segments(seg_ref, segb, vt)
    cw = xs
    for j in range(nch // 2):
        cols = pl.ds(j * 128, 128)
        cw[j, 8 : t + 8, :] = c_ref[0, :, cols].astype(F32)
        dcs[j, 8 : t + 8, :] = dconv_ref[0, :, cols]

    def dtap_tile(i, carry):
        r0 = pl.multiple_of(i * 128, 128)
        rows = pl.ds(r0, 128)
        acc = None
        for o in range(KERNEL):
            his, los = [], []
            for j in range(nch // 2):
                prod = cw[j, pl.ds(8 + r0 + o - REACH, 128), :] * dcs[j, pl.ds(8 + r0, 128), :]
                hi, lo = split2(prod)
                his.append(hi)
                los.append(lo)
            part = mm(jnp.concatenate(his + los, 1), er_ref[o * 768 : (o + 1) * 768, :])
            acc = part if acc is None else acc + part
        dlt[:, rows] = acc.T[0:72, :]
        return carry

    lax.fori_loop(0, t // 128, dtap_tile, 0)

    taps = [taps_ref[0, o * 8 : o * 8 + 8, :] for o in range(KERNEL)]
    dtaps = [dlt[o * 8 : o * 8 + 8, :] * vt[o] for o in range(KERNEL)]
    mean = taps[0] * dtaps[0]
    for o in range(1, KERNEL):
        mean = mean + taps[o] * dtaps[o]
    for o in range(KERNEL):
        dl[o * 8 : o * 8 + 8, :] = taps[o] * (dtaps[o] - mean)
        tv = taps[o] * vt[o]
        move = (o - REACH) % t
        rt[o * 8 : o * 8 + 8, :] = pltpu.roll(tv, move, 1) if move else tv

    def point_tile(i, carry):
        r0 = pl.multiple_of(i * 384, 128)
        rows = pl.ds(r0, 384)
        dlog = dl[:, rows].astype(BF16)
        d_mixed = mm(dlog, wk_ref[...], TN)
        gk_ref[...] += mm(dlog, mixed_ref[0, rows, :])
        d_span = (d_mixed * q_ref[0, rows, :].astype(F32)).astype(BF16)
        dm[rows, 0:half] = (dq_ref[0, rows, :] + d_mixed * span_ref[0, rows, :]).astype(BF16)
        dm[rows, half : 2 * half] = dk_ref[0, rows, :]
        dm[rows, 2 * half : 3 * half] = dv_ref[0, rows, :]
        gpt_ref[...] += mm(depth_ref[0, rows, :], d_span, TN)
        d_depth = mm(d_span, wpt_ref[...], NT)
        for j in range(nch):
            dts[j, pl.ds(8 + r0, 384), :] = d_depth[:, j * 128 : (j + 1) * 128]
        return carry

    lax.fori_loop(0, t // 384, point_tile, 0)

    def dc_tile(i, carry):
        r0 = pl.multiple_of(i * 128, 128)
        rows = pl.ds(r0, 128)
        texp[...] = expand_taps(rt[:, rows], e_ref)
        for j in range(nch // 2):
            acc = None
            for o in range(KERNEL):
                part = dcs[j, pl.ds(8 + r0 - o + REACH, 128), :] * texp[:, o * half + j * 128 : o * half + (j + 1) * 128]
                acc = part if acc is None else acc + part
            dm[rows, pl.ds(3 * half + j * 128, 128)] = acc.astype(BF16)
        return carry

    lax.fori_loop(0, t // 128, dc_tile, 0)

    for j in range(nch):
        xs[j, 8 : t + 8, :] = x_ref[0, :, pl.ds(j * 128, 128)].astype(F32)

    def proj_tile(i, carry):
        r0 = pl.multiple_of(i * 384, 128)
        rows = pl.ds(r0, 384)
        gp_ref[...] += mm(x_ref[0, rows, :], dm[rows, :], TN)
        gx = mm(dm[rows, :], wp_ref[...], NT) + dres_ref[0, rows, :]
        for j in range(nch):
            pad[j, pl.ds(r0, 384), :] = gx[:, j * 128 : (j + 1) * 128]
        return carry

    lax.fori_loop(0, t // 384, proj_tile, 0)

    def depth_tile(r0, masked):
        masks = mask_rows(segb, r0, 128) if masked else None
        for j in range(nch):
            acc = pad[j, pl.ds(r0, 128), :]
            own = dts[j, pl.ds(8 + r0, 128), :]
            for o in range(KERNEL):
                w = wd_ref[KERNEL - 1 - o : KERNEL - o, pl.ds(j * 128, 128)]
                near = dts[j, pl.ds(8 + r0 + o - REACH, 128), :]
                xw = xs[j, pl.ds(8 + r0 + o - REACH, 128), :]
                if masked:
                    near = near * masks[o]
                    xw = xw * masks[o]
                acc = acc + near * w
                term = (own * xw).reshape(16, 8, 128)
                gacc[o, :, pl.ds(j * 128, 128)] += jnp.sum(term, 0)
            pad[j, pl.ds(r0, 128), :] = acc

    masked_tiles(t, depth_tile)

    for j in range(nch):
        cols = pl.ds(j * 128, 128)
        pad[j, pl.ds(t, 128), :] = pad[j, 0:128, :]
        back = t - s
        first = pl.ds(back, 128)
        gx_ref[0, :, cols] = xs[j, 8 : t + 8, :]
        xs[j, 0:128, :] = pad[j, first, :]
        gx_ref[0, 0:128, cols] = xs[j, 0:128, :]
        gx_ref[0, 128:, cols] = pad[j, pl.ds(128 - s, t - 128), :]
        pad[j, 0:t, :] = out_ref_in[0, :, cols].astype(F32)
        pad[j, pl.ds(t, 128), :] = pad[j, 0:128, :]
        out_ref[0, 0:128, cols] = pad[j, first, :].astype(BF16)
        out_ref[0, 128:, cols] = pad[j, pl.ds(128 - s, t - 128), :].astype(BF16)

    @pl.when(b == pl.num_programs(0) - 1)
    def _():
        n = gm_ref.shape[0]
        rows = d // n
        small[...] = jnp.zeros_like(small)
        for o in range(KERNEL):
            small[o : o + 1, :] = jnp.sum(gacc[o], 0, keepdims=True)
        small[16:24, :] = gs_ref[...]
        row = lax.broadcasted_iota(jnp.int32, (128, 72), 0)
        col = lax.broadcasted_iota(jnp.int32, (128, 72), 1)
        order = jnp.where((row < HEADS * KERNEL) & (row % KERNEL * 8 + row // KERNEL == col), 1.0, 0.0).astype(BF16)
        gk = mm(order, gk_ref[...].astype(BF16)).astype(BF16)
        row = lax.broadcasted_iota(jnp.int32, (half, d), 0)
        col = lax.broadcasted_iota(jnp.int32, (half, d), 1)
        piece = col % PIECE
        put = jnp.where((piece < PIECE // 2) & (col // PIECE * (PIECE // 2) + piece == row), 1.0, 0.0).astype(BF16)
        gk = mm(gk, put)
        for j in range(nch):
            cols = pl.ds(j * 128, 128)
            pad[0, cols, :] = small[:, cols].T
            pad[1, cols, :] = gk[:, j * 128 : (j + 1) * 128].T

        def emit(p, c):
            at = pl.ds(pl.multiple_of(p * rows, 8), rows)
            gp = gp_ref[at, :]
            parts = [gp[:, j * half : (j + 1) * half] for j in range(gp.shape[1] // half)] + [gpt_ref[at, :]]
            parts.append(jnp.concatenate([pad[0, at, :], pad[1, at, :], jnp.zeros((rows, half - 256), F32)], 1))
            gm_ref[p] = jnp.concatenate(parts, 0).astype(BF16)
            return c

        lax.fori_loop(0, n, emit, 0)


def stage_e(n, s, segr, x, out_r, dres, dconv, dq, dk, dv, q, c, depth, span, mixed, taps, wp, wd, wpt, wk, gs):
    mb, t, d = x.shape
    half = d // 2
    packed = (d * 2 * d + d * half) // (n * half) + d // n
    sds = jax.ShapeDtypeStruct

    def slow(*shape):
        return pl.BlockSpec((1,) + shape, lambda b, *_: (b,) + (0,) * len(shape), pipeline_mode=pl.Buffered(1))

    return pl.pallas_call(
        kernel_e,
        out_shape=[
            sds((mb, t, d), F32), sds((mb, t, d), BF16), sds((n, packed, half), BF16),
        ],
        grid_spec=pltpu.PrefetchScalarGridSpec(
            num_scalar_prefetch=1,
            grid=(mb,),
            in_specs=[pl.BlockSpec((pl.Squeezed(), 1, t), lambda b, *_: (b, 0, 0))]
            + [slow(t, d), slow(t, d), slow(t, d), slow(t, half), slow(t, half), slow(t, half), slow(t, half)]
            + [slow(t, half), slow(t, half), slow(t, d), slow(t, half), slow(t, half), slow(72, t)]
            + [whole(*w.shape) for w in (wp, wd, wpt, wk, gs)],
            out_specs=[slow(t, d), slow(t, d), whole(n, packed, half)],
            scratch_shapes=[
                pltpu.VMEM((d // 128, t + 128, 128), F32),
                pltpu.VMEM((d // 128, t + 16, 128), F32),
                pltpu.VMEM((t + 16, 128), F32),
                pltpu.VMEM((KERNEL, 8, t), F32),
                pltpu.VMEM((half // 128, t + 16, 128), F32),
                pltpu.VMEM((d // 128, t + 16, 128), F32),
                pltpu.VMEM((144, KERNEL * half), BF16),
                pltpu.VMEM((KERNEL * 768, 128), BF16),
                pltpu.VMEM((128, KERNEL * half), F32),
                pltpu.VMEM((72, t), F32),
                pltpu.VMEM((72, t), F32),
                pltpu.VMEM((t, 2 * d), BF16),
                pltpu.VMEM((72, t), F32),
                pltpu.VMEM((KERNEL, 8, d), F32),
                pltpu.VMEM(wp.shape, F32),
                pltpu.VMEM(wpt.shape, F32),
                pltpu.VMEM((72, half), F32),
                pltpu.VMEM((128, d), F32),
            ],
        ),
        compiler_params=params(1),
        name="mix_bwd",
    )(s, segr, x, out_r, dres, dconv, dq, dk, dv, q, c, depth, span, mixed, taps, wp, wd, wpt, wk, gs)


def rolled_segments(segments):
    mb, t = segments.shape
    span = t - SEG_MOST + 1
    hit = segments[:, :span] == segments[:, SEG_MOST - 1 :]
    s = jnp.sum(jnp.where(hit, jnp.arange(span, dtype=jnp.int32)[None, :], 0), 1).astype(jnp.int32)
    twice = jnp.concatenate([segments, segments[:, : t - SEG_MOST]], 1).astype(F32)
    rows = [lax.dynamic_slice(twice[b], (s[b],), (t,)) for b in range(mb)]
    return s, jnp.stack(rows)[:, None, :]


def pack_small(w_depth, w_kernel, g1, b1, g2, b2):
    rows = w_depth.shape[0]
    units = rows // PIECE
    heads = w_kernel.reshape(units, PIECE // 2, HEADS, KERNEL).transpose(0, 1, 3, 2)
    heads = jnp.pad(heads, ((0, 0), (0, PIECE // 2), (0, 0), (0, 8 - HEADS))).reshape(rows, 8 * KERNEL)
    norms = jnp.stack([g1, b1, g2, b2], 1)
    gap = jnp.zeros((rows, 16 - KERNEL), BF16)
    return jnp.concatenate(
        [w_depth, gap, norms, jnp.zeros((rows, 128 - 20), BF16), heads, jnp.zeros((rows, 128 - 8 * KERNEL), BF16)], 1
    )


def finish_kernel(f_ref, m_ref, gp_ref, gdep_ref, gpt_ref, gk_ref, go_ref, gi_ref, gd_ref, gs_ref):
    half = f_ref.shape[1]
    rows = gp_ref.shape[0]
    tall = gd_ref.shape[0]
    gd_ref[...] = f_ref[0:tall, :]
    for j in range(gi_ref.shape[1] // half):
        gi_ref[:, j * half : (j + 1) * half] = f_ref[tall + j * rows : tall + (j + 1) * rows, :]
    tall = tall + rows * (gi_ref.shape[1] // half)
    for j in range(2):
        go_ref[:, j * half : (j + 1) * half] = f_ref[tall + j * rows : tall + (j + 1) * rows, :]
    wide = gp_ref.shape[1] // half
    for j in range(wide):
        gp_ref[:, j * half : (j + 1) * half] = m_ref[j * rows : (j + 1) * rows, :]
    gpt_ref[...] = m_ref[wide * rows : (wide + 1) * rows, :]
    small = m_ref[(wide + 1) * rows : (wide + 2) * rows, 0:256]
    gdep_ref[...] = small[:, 0:KERNEL]
    gk_ref[...] = small[0 : rows // 2, 128 : 128 + HEADS * KERNEL]
    gs_ref[...] = small[:, 16:24]


def finish(n, d, hid, f, m):
    half = d // 2
    sds = jax.ShapeDtypeStruct
    rows = d // n
    return pl.pallas_call(
        finish_kernel,
        out_shape=[
            sds((rows, 2 * d), F32), sds((rows, KERNEL), F32), sds((rows, half), F32), sds((half // n, HEADS * KERNEL), F32),
            sds((rows, d), F32), sds((rows, hid), F32), sds((2 * hid // n, half), F32), sds((rows, 8), F32),
        ],
        name="finish",
    )(f, m)


def side_by_side(block, parts):
    units, _, cols = block.shape
    return block.reshape(units, parts, PIECE, cols).transpose(0, 2, 1, 3).reshape(units * PIECE, parts * cols)


def native_sums(gf, gm, d, hid):
    gf, gm = gf.astype(F32), gm.astype(F32)
    half = d // 2
    tall = 2 * hid * PIECE // d
    wide = hid // half * PIECE
    many_p = 2 * d // half
    g_down = gf[:, :tall].reshape(-1, half)
    g_in = side_by_side(gf[:, tall : tall + wide], hid // half)
    g_out = side_by_side(gf[:, tall + wide :], 2)
    g_proj = side_by_side(gm[:, : many_p * PIECE], many_p)
    g_point = gm[:, many_p * PIECE : (many_p + 1) * PIECE].reshape(-1, half)
    small = gm[:, (many_p + 1) * PIECE :]
    g_kernel = small[:, : PIECE // 2, 128 : 128 + HEADS * KERNEL].reshape(half, -1)
    small = small[:, :, 0:24].reshape(d, -1)
    grads = [g_proj, small[:, :KERNEL], g_point, g_kernel, g_out, g_in, g_down, small[:, 16:]]
    return [lax.psum_scatter(g, "tok", scatter_dimension=0, tiled=True) for g in grads]


def shards(n, tokens, segments, cotangent, w_proj, w_depth, w_point, w_kernel, w_out, g1, b1, w_in, w_down, g2, b2):
    d = tokens.shape[-1]
    hid = w_in.shape[1]
    units = d // PIECE
    own = n == units
    if own:
        small = pack_small(w_depth, w_kernel, g1, b1, g2, b2)
        full = gather_all(n, [w_proj, w_in, small, w_down, w_point, w_out])
        wp, wi, sm, wdn, wpt, wo = [w.reshape(-1, w.shape[2]) for w in full]
    else:
        given = [w_proj, w_in, w_down, w_point, w_out, w_depth, w_kernel, g1, b1, g2, b2]
        wp, wi, wdn, wpt, wo, *rest = [lax.all_gather(w, "tok", axis=0, tiled=True) for w in given]
        sm = pack_small(*rest)
    s, segr = rolled_segments(segments[:, 0])
    segt = segr[:, :, SEG_MOST:]
    xr, cotr, q, k, v, c, depth, span, mixed, taps, conv, wd_rows, wk_rows = stage_a(
        s, tokens, cotangent, segr, wp, sm, wpt
    )
    ctx, lse = stage_b(segt, q, k, v)
    out_r, dres, dctx, dconv, gf, g_small = stage_c(units, ctx, conv, xr, cotr, wo, wi, wdn, wd_rows)
    dq, dk, dv = stage_d(segt, q, k, v, ctx, lse, dctx)
    gx, out, gm = stage_e(
        units, s, segr, xr, out_r, dres, dconv, dq, dk, dv, q, c, depth, span, mixed, taps, wp, wd_rows, wpt, wk_rows,
        g_small,
    )
    if own:
        f, m = scatter_all(n, 1, [gf, gm], 2)
        sums = finish(n, d, hid, f, m)
    else:
        sums = native_sums(gf, gm, d, hid)
    g_proj, g_depth, g_point, g_kernel, g_out, g_in, g_down, g_vec = sums
    return (
        out, gx, g_proj, g_depth, g_point, g_kernel, g_out, g_vec[:, 0], g_vec[:, 1], g_in, g_down,
        g_vec[:, 2], g_vec[:, 3],
    )


def solution(mesh):
    rows, vec, act = P("tok", None), P("tok"), P(None, "tok", None)
    in_specs = (act, act, act, rows, rows, rows, rows, rows, vec, vec, rows, rows, vec, vec)
    out_specs = (act, act, rows, rows, rows, rows, rows, vec, vec, rows, rows, vec, vec)
    run = partial(shards, mesh.shape["tok"])
    return jax.shard_map(run, mesh=mesh, in_specs=in_specs, out_specs=out_specs, check_vma=False)
```

```python
from functools import partial

import jax
import jax.numpy as jnp
from jax import lax
from jax.experimental import pallas as pl
from jax.experimental.pallas import tpu as pltpu
from jax.sharding import PartitionSpec as P

HEADS = 6
KERNEL = 9
REACH = 4
SEG_MOST = 1024
NORM_EPS = 1e-12
F32 = jnp.float32
BF16 = jnp.bfloat16
NT = (((1,), (1,)), ((), ()))
NN = (((1,), (0,)), ((), ()))
TN = (((0,), (0,)), ((), ()))
VMEM_CAP = 62 * 1024 * 1024
MESH = pl.DeviceIdType.MESH
PIECE = 24


def mm(a, b, dims=NN):
    return lax.dot_general(a, b, dims, preferred_element_type=F32)


def lanes(shape):
    return lax.broadcasted_iota(jnp.int32, shape, 1)


def split2(v):
    hi = v.astype(BF16)
    return hi, (v - hi.astype(F32)).astype(BF16)


def split3(v):
    hi = v.astype(BF16)
    rest = v - hi.astype(F32)
    mid = rest.astype(BF16)
    return hi, mid, (rest - mid.astype(F32)).astype(BF16)


def partner(me, bit):
    return me + (1 - 2 * lax.rem(lax.div(me, bit), 2)) * bit


def flipped(me, bits, k):
    at = me
    for j, bit in enumerate(bits):
        at = at + (partner(me, bit) - me) * lax.rem(lax.div(k, 1 << j), 2)
    return at


def bit_orders(n):
    one = [1 << b for b in range(n.bit_length() - 1)]
    two = one[:1] + one[2:3] + one[1:2] + one[3:] if len(one) > 2 else one
    return one, two


def greet(n):
    me = lax.axis_index("tok")
    barrier = pltpu.get_barrier_semaphore()
    bits = bit_orders(n)[0]
    for bit in bits:
        pl.semaphore_signal(barrier, inc=1, device_id=(partner(me, bit),), device_id_type=MESH)
    pl.semaphore_wait(barrier, len(bits))


def many(count, body):
    if count <= 4:
        for k in range(count):
            body(k)
    else:
        lax.fori_loop(0, count, lambda k, c: (body(k), c)[1], 0)


class Gather:
    def __init__(self, src, dst, cols, order, send, recv, own):
        self.src, self.all, self.cols, self.order = src.at[:, cols], dst, cols, order[::-1]
        self.send, self.recv, self.own = send, recv, own
        self.me = lax.axis_index("tok")

    def dst(self, at):
        return self.all.at[at, :, self.cols]

    def start(self):
        pltpu.make_async_copy(self.src, self.dst(self.me), self.own).start()
        self.stage(0)

    def stage(self, s):
        to = partner(self.me, self.order[s])

        def one(k):
            at = flipped(self.me, self.order[:s], k)
            pltpu.make_async_remote_copy(
                src_ref=self.dst(at) if s else self.src,
                dst_ref=self.dst(at),
                send_sem=self.send.at[s],
                recv_sem=self.recv.at[s],
                device_id=(to,),
                device_id_type=MESH,
            ).start()

        many(1 << s, one)

    def wait(self, sem, s):
        whole = self.dst(pl.ds(0, 1 << s))
        pltpu.make_async_copy(whole, whole, sem.at[s]).wait()

    def step(self, s):
        if s == 1:
            pltpu.make_async_copy(self.src, self.dst(self.me), self.own).wait()
        self.wait(self.recv, s - 1)
        self.stage(s)

    def finish(self):
        last = len(self.order) - 1
        self.wait(self.recv, last)
        for s in range(last + 1):
            self.wait(self.send, s)


class Scatter:
    def __init__(self, n, src, first, acc, got, order, send, recv, own):
        self.n, self.src, self.acc, self.got, self.order = n, src, acc, got, order
        self.rows = pl.ds(first, acc.shape[1])
        self.send, self.recv, self.own = send, recv, own
        self.me = lax.axis_index("tok")

    def term(self, k):
        at = flipped(self.me, self.order[::-1], k)
        return self.src.at[at, self.rows]

    def start(self):
        half = self.n // 2
        to = partner(self.me, self.order[0])

        def one(k):
            pltpu.make_async_remote_copy(
                src_ref=self.term(half + k),
                dst_ref=self.got.at[half + k],
                send_sem=self.send.at[0],
                recv_sem=self.recv.at[0],
                device_id=(to,),
                device_id_type=MESH,
            ).start()

        def mine(k):
            pltpu.make_async_copy(self.term(k), self.acc.at[k], self.own).start()

        many(half, one)
        many(half, mine)

    def held(self, s):
        return pl.ds(self.n >> (s + 1), self.n >> (s + 1))

    def wait(self, sem, s):
        ref = self.got.at[self.held(s)]
        pltpu.make_async_copy(ref, ref, sem.at[s]).wait()

    def add(self, s):
        if s == 0:
            pltpu.make_async_copy(self.acc, self.acc, self.own).wait()
        self.wait(self.recv, s)
        count = self.n >> (s + 1)

        def one(k):
            total = self.acc[k].astype(F32) + self.got[count + k].astype(F32)
            self.acc[k] = total.astype(BF16)

        many(count, one)

    def step(self, s):
        self.add(s - 1)
        part = self.acc.at[self.held(s)]
        pltpu.make_async_remote_copy(
            src_ref=part,
            dst_ref=self.got.at[self.held(s)],
            send_sem=self.send.at[s],
            recv_sem=self.recv.at[s],
            device_id=(partner(self.me, self.order[s]),),
            device_id_type=MESH,
        ).start()

    def finish(self, out):
        last = len(self.order) - 1
        self.wait(self.recv, last)
        out[self.rows, :] = self.acc[0].astype(F32) + self.got[1].astype(F32)
        for s in range(last + 1):
            self.wait(self.send, s)


ANY = pl.BlockSpec(memory_space=pl.ANY)


def remote(cid):
    return pltpu.CompilerParams(collective_id=cid, has_side_effects=True, vmem_limit_bytes=VMEM_CAP)


class Gathers:
    def __init__(self, n, srcs, dsts, send, recv, own):
        self.parts = []
        self.last = n.bit_length() - 1
        for src, dst in zip(srcs, dsts):
            wide = src.shape[1]
            cut = wide // 256 * 128
            for cols, order in zip((pl.ds(0, cut), pl.ds(cut, wide - cut)), bit_orders(n)):
                i = len(self.parts)
                self.parts.append(Gather(src, dst, cols, order, send.at[i], recv.at[i], own.at[i]))

    def step(self, s):
        for g in self.parts:
            if s == 0:
                g.start()
            elif s < self.last:
                g.step(s)
            else:
                g.finish()

    @staticmethod
    def sems(n, count):
        stages = n.bit_length() - 1
        dma = pltpu.SemaphoreType.DMA
        return [dma((2 * count, stages)), dma((2 * count, stages)), dma((2 * count,))]


def gathered(n, shards):
    return [jax.ShapeDtypeStruct((n,) + w.shape, w.dtype) for w in shards]


def gather_all(n, shards):
    count = len(shards)

    def kernel(*refs):
        greet(n)
        plan = Gathers(n, refs[:count], refs[count : 2 * count], *refs[2 * count :])
        for s in range(plan.last + 1):
            plan.step(s)

    return pl.pallas_call(
        kernel,
        out_shape=gathered(n, shards),
        in_specs=[ANY] * count,
        out_specs=[ANY] * count,
        scratch_shapes=Gathers.sems(n, count),
        compiler_params=remote(0),
        name="gather",
    )(*shards)


def split_rows(rows, parts):
    tiles = rows // 16
    cuts = [tiles * i // parts * 16 for i in range(parts + 1)]
    return [(a, b - a) for a, b in zip(cuts, cuts[1:]) if b > a]


class Scatters:
    def __init__(self, n, cuts, srcs, outs, refs):
        total = len(cuts)
        accs, gots, (send, recv, own) = refs[:total], refs[total : 2 * total], refs[2 * total :]
        orders = bit_orders(n)
        self.last = n.bit_length() - 1
        self.outs = [outs[i] for i, a, r in cuts]
        self.parts = [
            Scatter(n, srcs[i], a, accs[j], gots[j], orders[j % 2], send.at[j], recv.at[j], own.at[j])
            for j, (i, a, r) in enumerate(cuts)
        ]

    def step(self, s):
        for p, out in zip(self.parts, self.outs):
            if s == 0:
                p.start()
            elif s < self.last:
                p.step(s)
            else:
                p.finish(out)

    @staticmethod
    def cuts(packed, parts):
        return [(i, a, r) for i, w in enumerate(packed) for a, r in split_rows(w.shape[1], parts)]

    @staticmethod
    def scratch(n, cuts, packed):
        total, stages = len(cuts), n.bit_length() - 1
        dma = pltpu.SemaphoreType.DMA
        bufs = [(r, packed[i].shape[2]) for i, a, r in cuts]
        return (
            [pltpu.VMEM((n // 2,) + b, BF16) for b in bufs]
            + [pltpu.VMEM((n,) + b, BF16) for b in bufs]
            + [dma((total, stages)), dma((total, stages)), dma((total,))]
        )


def scatter_all(n, cid, packed, parts):
    cuts = Scatters.cuts(packed, parts)
    count = len(packed)

    def kernel(*refs):
        greet(n)
        plan = Scatters(n, cuts, refs[:count], refs[count : 2 * count], refs[2 * count :])
        for s in range(plan.last + 1):
            plan.step(s)

    return pl.pallas_call(
        kernel,
        out_shape=[jax.ShapeDtypeStruct(w.shape[1:], F32) for w in packed],
        in_specs=[ANY] * count,
        out_specs=[pl.BlockSpec(memory_space=pltpu.VMEM)] * count,
        scratch_shapes=Scatters.scratch(n, cuts, packed),
        compiler_params=remote(cid),
        name="scatter",
    )(*packed)


def expand_taps(tap_rows, e_ref):
    hi, lo = split2(tap_rows)
    both = jnp.concatenate([hi, lo], 0)
    return mm(both, e_ref[...], TN)


def fill_expander(e_ref):
    shape = e_ref.shape
    half = shape[1] // KERNEL
    row = lax.broadcasted_iota(jnp.int32, shape, 0) % 72
    col = lax.broadcasted_iota(jnp.int32, shape, 1)
    want = (col // half) * 8 + (col % half) // 64
    e_ref[...] = jnp.where(row == want, 1.0, 0.0).astype(BF16)


def mask_rows(segb_ref, r0, rows):
    own = segb_ref[pl.ds(8 + r0, rows), :]
    return [
        jnp.where(segb_ref[pl.ds(8 + r0 + o - REACH, rows), :] == own, 1.0, 0.0)
        for o in range(KERNEL)
    ]


def fill_segments(seg_ref, segb_ref, vt_ref):
    t = seg_ref.shape[-1]
    row = seg_ref[...]
    wide = jnp.broadcast_to(row, (128, t))
    segb_ref[0:8, :] = jnp.full((8, 128), -1.0, F32)
    segb_ref[t + 8 : t + 16, :] = jnp.full((8, 128), -1.0, F32)
    segb_ref[8 : t + 8, :] = wide.T
    tall = jnp.broadcast_to(row, (8, t))
    pos = lanes((8, t))
    for o in range(KERNEL):
        d = o - REACH
        moved = pltpu.roll(tall, (-d) % t, 1) if d else tall
        inside = (pos + d >= 0) & (pos + d < t)
        vt_ref[o] = jnp.where(inside & (moved == tall), 1.0, 0.0)


def masked_tiles(t, body):
    full = SEG_MOST // 128

    def inner(i, c):
        body(pl.multiple_of(i * 128, 128), False)
        return c

    lax.fori_loop(1, full - 1, inner, 0)

    def edge(i, c):
        idx = jnp.where(i == 0, 0, i + full - 2)
        body(pl.multiple_of(idx * 128, 128), True)
        return c

    lax.fori_loop(0, t // 128 - full + 2, edge, 0)


def unpack_small(sm_ref, wd_ref, wk_ref):
    d = sm_ref.shape[0]
    for j in range(d // 128):
        rows = pl.ds(j * 128, 128)
        wd_ref[:, rows] = sm_ref[rows, 0:128].astype(F32).T[0:24, :]
    row = lax.broadcasted_iota(jnp.int32, (d, d // 2), 0)
    col = lax.broadcasted_iota(jnp.int32, (d, d // 2), 1)
    piece = row % PIECE
    pick = jnp.where((piece < PIECE // 2) & (row // PIECE * (PIECE // 2) + piece == col), 1.0, 0.0).astype(BF16)
    wk_ref[...] = mm(sm_ref[:, 128:256], pick, TN)[0:72, :].astype(BF16)


def kernel_a(n, count, *refs):
    s_ref, x_ref, cot_ref, seg_ref, wp_ref, sm_ref, wpt_ref = refs[:7]
    srcs, refs = refs[7 : 7 + count], refs[7 + count :]
    xr_ref, cotr_ref, q_ref, k_ref, v_ref, c_ref, depth_ref, span_ref, mixed_ref, taps_ref, conv_ref = refs[:11]
    wd_ref, wk_ref = refs[11:13]
    dsts, refs = refs[13 : 13 + count], refs[13 + count :]
    raw, xs, segb, vt, cs, lt, e_ref, texp, *sems = refs
    plan = Gathers(n, srcs, dsts, *sems) if count else None
    t, d = x_ref.shape[1:]
    half = d // 2
    nch = d // 128
    b = pl.program_id(0)
    s = s_ref[b]
    point(b == 0, lambda: greet(n), plan, 0)

    @pl.when(b == 0)
    def _():
        fill_expander(e_ref)
        unpack_small(sm_ref, wd_ref, wk_ref)
        xs[:, 0:8, :] = jnp.zeros((nch, 8, 128), F32)
        xs[:, t + 8 : t + 16, :] = jnp.zeros((nch, 8, 128), F32)
        cs[:, 0:8, :] = jnp.zeros((nch // 2, 8, 128), F32)
        cs[:, t + 8 : t + 16, :] = jnp.zeros((nch // 2, 8, 128), F32)

    fill_segments(seg_ref, segb, vt)
    for src, dst in ((cot_ref, cotr_ref), (x_ref, xr_ref)):
        for j in range(nch):
            col = pl.ds(j * 128, 128)
            raw[0:t, :] = src[0, :, col].astype(F32)
            raw[t : t + 128, :] = src[0, 0:128, col].astype(F32)
            moved = raw[pl.ds(s, t), :]
            if dst is xr_ref:
                xs[j, 8 : t + 8, :] = moved
            dst[0, :, col] = moved.astype(BF16)

    def depth_tile(r0, masked):
        masks = mask_rows(segb, r0, 128) if masked else None
        for j in range(nch):
            acc = None
            for o in range(KERNEL):
                part = xs[j, pl.ds(8 + r0 + o - REACH, 128), :]
                w = wd_ref[o : o + 1, pl.ds(j * 128, 128)]
                part = part * (masks[o] * w) if masked else part * w
                acc = part if acc is None else acc + part
            depth_ref[0, pl.ds(r0, 128), pl.ds(j * 128, 128)] = acc.astype(BF16)

    point(b == 0, None, plan, 1)
    masked_tiles(t, depth_tile)
    point(b == 0, None, plan, 2)

    def proj_tile(i, carry):
        r0 = pl.multiple_of(i * 384, 128)
        rows = pl.ds(r0, 384)
        merged = mm(xr_ref[0, rows, :], wp_ref[...]).astype(BF16)
        q = merged[:, 0:half]
        q_ref[0, rows, :] = q
        k_ref[0, rows, :] = merged[:, half : 2 * half]
        v_ref[0, rows, :] = merged[:, 2 * half : 3 * half]
        c = merged[:, 3 * half :]
        c_ref[0, rows, :] = c
        for j in range(nch // 2):
            cs[j, pl.ds(8 + r0, 384), :] = c[:, j * 128 : (j + 1) * 128].astype(F32)
        span = mm(depth_ref[0, rows, :], wpt_ref[...])
        span_ref[0, rows, :] = span
        mixed = (span * q.astype(F32)).astype(BF16)
        mixed_ref[0, rows, :] = mixed
        lt[:, rows] = mm(wk_ref[...], mixed, NT)
        return carry

    lax.fori_loop(0, t // 384, proj_tile, 0)

    point(b == 0, None, plan, 3)
    logits = [lt[o * 8 : o * 8 + 8, :] for o in range(KERNEL)]
    top = logits[0]
    for o in range(1, KERNEL):
        top = jnp.maximum(top, logits[o])
    exps = [jnp.exp(v - top) for v in logits]
    total = exps[0]
    for o in range(1, KERNEL):
        total = total + exps[o]
    inv = 1.0 / total
    for o in range(KERNEL):
        tap = exps[o] * inv
        taps_ref[0, o * 8 : o * 8 + 8, :] = tap
        lt[o * 8 : o * 8 + 8, :] = tap * vt[o]

    def conv_tile(i, carry):
        r0 = pl.multiple_of(i * 128, 128)
        rows = pl.ds(r0, 128)
        texp[...] = expand_taps(lt[:, rows], e_ref)
        for j in range(nch // 2):
            acc = None
            for o in range(KERNEL):
                part = cs[j, pl.ds(8 + r0 + o - REACH, 128), :] * texp[:, o * half + j * 128 : o * half + (j + 1) * 128]
                acc = part if acc is None else acc + part
            conv_ref[0, rows, pl.ds(j * 128, 128)] = acc.astype(BF16)
        return carry

    point(b == 1, None, plan, 4)
    lax.fori_loop(0, t // 128, conv_tile, 0)
    if plan is not None:
        for i in range(5, plan.last + 1):
            point(b == pl.num_programs(0) - 1, None, plan, i)


def whole(*shape):
    return pl.BlockSpec(shape, lambda *_: (0,) * len(shape), pipeline_mode=pl.Buffered(1))


def per_block(*shape):
    return pl.BlockSpec((1,) + shape, lambda b, *_: (b,) + (0,) * len(shape))


def params(n, cid=None):
    more = {} if cid is None else {"collective_id": cid, "has_side_effects": True}
    return pltpu.CompilerParams(dimension_semantics=("arbitrary",) * n, vmem_limit_bytes=VMEM_CAP, **more)


def point(when, first, plan, s):
    if plan is None:
        return

    @pl.when(when)
    def _():
        if s == 0:
            first()
        plan.step(s)


def stage_a(n, s, x, cot, segr, wp, sm, wpt, more):
    mb, t, d = x.shape
    half = d // 2
    sds = jax.ShapeDtypeStruct
    out = [
        ((t, d), BF16), ((t, d), BF16), ((t, half), BF16), ((t, half), BF16), ((t, half), BF16), ((t, half), BF16),
        ((t, d), BF16), ((t, half), F32), ((t, half), BF16), ((72, t), F32), ((t, half), BF16),
    ]
    return pl.pallas_call(
        partial(kernel_a, n, len(more)),
        out_shape=[sds((mb,) + sh, dt) for sh, dt in out] + [sds((24, d), F32), sds((72, half), BF16)] + gathered(n, more),
        grid_spec=pltpu.PrefetchScalarGridSpec(
            num_scalar_prefetch=1,
            grid=(mb,),
            in_specs=[
                per_block(t, d), per_block(t, d),
                pl.BlockSpec((pl.Squeezed(), 1, t), lambda b, *_: (b, 0, 0)),
                whole(*wp.shape), whole(*sm.shape), whole(*wpt.shape),
            ]
            + [ANY] * len(more),
            out_specs=[per_block(*sh) for sh, _ in out] + [whole(24, d), whole(72, half)] + [ANY] * len(more),
            scratch_shapes=[
                pltpu.VMEM((t + 128, 128), F32),
                pltpu.VMEM((d // 128, t + 16, 128), F32),
                pltpu.VMEM((t + 16, 128), F32),
                pltpu.VMEM((KERNEL, 8, t), F32),
                pltpu.VMEM((half // 128, t + 16, 128), F32),
                pltpu.VMEM((72, t), F32),
                pltpu.VMEM((144, KERNEL * half), BF16),
                pltpu.VMEM((128, KERNEL * half), F32),
            ]
            + (Gathers.sems(n, len(more)) if more else []),
        ),
        compiler_params=params(1, 2 if more else None),
        name="mix_fwd",
    )(s, x, cot, segr, wp, sm, wpt, *more)


QT = 256


def seg_codes(segb, first):
    lane = lanes(segb.shape) - first
    hot = segb == lane.astype(F32)
    inside = (lane >= 0) & (lane < 24)
    return jnp.where(hot & inside, 1.0, 0.0), jnp.where(inside & ~hot, -1e30, 0.0)


def steps_done():
    across = pl.num_programs(1)
    return pl.program_id(0) * across + pl.program_id(1), pl.num_programs(0) * across - 1


def stage_points(n, plan, now, early):
    if plan is None:
        return
    step, last = steps_done()
    if early:
        for s, at in enumerate(now):
            point(step == at, lambda: greet(n), plan, s)
    else:
        for s in range(len(now), plan.last + 1):
            point(step == last, None, plan, s)


def kernel_b(n, count, *refs):
    segt_ref, q_ref, k_ref, v_ref = refs[:4]
    srcs, (ctx_ref, lse_ref) = refs[4 : 4 + count], refs[4 + count : 6 + count]
    dsts, sems = refs[6 + count : 6 + 2 * count], refs[6 + 2 * count :]
    plan = Gathers(n, srcs, dsts, *sems) if count else None
    times = (0, 1, 2, 3, 5)
    stage_points(n, plan, times, True)
    t = q_ref.shape[1]
    tail = t - SEG_MOST
    low_half = lanes((1, 128)) < 64

    def finish(rows, outs, tops):
        both = jnp.where(low_half, outs[0], outs[1])
        sums = jnp.where(low_half, outs[1], outs[0])
        ctx_ref[0, rows, :] = (both / pltpu.roll(sums, 64, 1)).astype(BF16)
        lse_ref[0, rows, :] = jnp.where(low_half, tops[1], tops[0]) + jnp.log(sums)

    def one(q, k, v):
        scores = mm(q, k, NT)
        top = jnp.max(scores, -1, keepdims=True)
        return mm(jnp.exp(scores - top).astype(BF16), v), top

    k = k_ref[0, 0:SEG_MOST, :]
    v = v_ref[0, 0:SEG_MOST, :]
    one_b = jnp.ones((), BF16)
    vs = (jnp.where(low_half, v, one_b), jnp.where(low_half, one_b, v))

    def tile(i, carry):
        rows = pl.ds(pl.multiple_of(i * QT, QT), QT)
        q = q_ref[0, rows, :] * 0.125
        zero = jnp.zeros((), BF16)
        outs = [one(jnp.where(low_half, q, zero), k, vs[0]), one(jnp.where(low_half, zero, q), k, vs[1])]
        finish(rows, [o[0] for o in outs], [o[1] for o in outs])
        return carry

    lax.fori_loop(0, SEG_MOST // QT, tile, 0)
    rows = pl.ds(SEG_MOST, tail)
    q = q_ref[0, rows, :] * 0.125
    kt = k_ref[0, rows, :]
    vt = v_ref[0, rows, :]
    segb = jnp.broadcast_to(segt_ref[...], (128, tail)).T
    outs = []
    for h in range(2):
        hot, pen = seg_codes(segb, 64 - 64 * h)
        mine = low_half if h == 0 else ~low_half
        outs.append(
            one(
                jnp.where(mine, q, pen.astype(BF16)),
                jnp.where(mine, kt, hot.astype(BF16)),
                jnp.where(mine, vt, one_b),
            )
        )
    finish(rows, [o[0] for o in outs], [o[1] for o in outs])
    stage_points(n, plan, times, False)


def pair(t):
    return pl.BlockSpec((1, t, 128), lambda b, j: (b, 0, j))


def seg_tail(tail):
    return pl.BlockSpec((pl.Squeezed(), 1, tail), lambda b, *_: (b, 0, 0))


def stage_b(n, segt, q, k, v, more):
    mb, t, half = q.shape
    sds = jax.ShapeDtypeStruct
    return pl.pallas_call(
        partial(kernel_b, n, len(more)),
        out_shape=[sds((mb, t, half), BF16), sds((mb, t, half), F32)] + gathered(n, more),
        grid=(mb, half // 128),
        in_specs=[seg_tail(t - SEG_MOST), pair(t), pair(t), pair(t)] + [ANY] * len(more),
        out_specs=[pair(t), pair(t)] + [ANY] * len(more),
        scratch_shapes=Gathers.sems(n, len(more)) if more else [],
        compiler_params=params(2, 3 if more else None),
        name="att_fwd",
    )(segt, q, k, v, *more)


ROWS = 384


def norm_fwd(values):
    centre = values - jnp.mean(values, -1, keepdims=True)
    inv_std = lax.rsqrt(jnp.mean(centre * centre, -1, keepdims=True) + NORM_EPS)
    return centre * inv_std, inv_std


def norm_back(grad, normed, inv_std):
    one = jnp.mean(grad, -1, keepdims=True)
    two = jnp.mean(grad * normed, -1, keepdims=True)
    return inv_std * (grad - one - normed * two)


def gelu_both(x):
    z = jnp.abs(x) * 0.7071067811865476
    r = 1.0 / (1.0 + 0.3275911 * z)
    e = jnp.exp(-0.5 * (x * x))
    poly = r * (0.254829592 + r * (-0.284496736 + r * (1.421413741 + r * (-1.453152027 + r * 1.061405429))))
    tail = 0.5 * (poly * e)
    cdf = jnp.where(x < 0, tail, 1.0 - tail)
    return x * cdf, cdf + x * (e * 0.3989422804014327)


def col_sum(v):
    return jnp.sum(v, 0, keepdims=True)


def kernel_c(
    ctx_ref, conv_ref, x_ref, cot_ref, wo_ref, wi_ref, wdn_ref, ln_ref,
    out_ref, dres_ref, dctx_ref, dconv_ref, gf_ref, gs_ref,
    joined, act, slope, dinner, go_ref, gi_ref, gd_ref,
):
    first = (pl.program_id(0) == 0) & (pl.program_id(1) == 0)
    last = (pl.program_id(0) == pl.num_programs(0) - 1) & (pl.program_id(1) == pl.num_programs(1) - 1)
    d = x_ref.shape[-1]
    half = d // 2
    hid = wi_ref.shape[1]

    @pl.when(first)
    def _():
        go_ref[...] = jnp.zeros_like(go_ref)
        gi_ref[...] = jnp.zeros_like(gi_ref)
        gd_ref[...] = jnp.zeros_like(gd_ref)
        gs_ref[...] = jnp.zeros_like(gs_ref)

    joined[:, 0:half] = ctx_ref[0]
    joined[:, half:] = conv_ref[0]
    gain1, shift1, gain2, shift2 = (ln_ref[16 + i : 17 + i, :] for i in range(4))
    normed1, inv1 = norm_fwd(mm(joined[...], wo_ref[...]) + x_ref[0].astype(F32))
    hidden = normed1 * gain1 + shift1
    hidden_low = hidden.astype(BF16)
    outers = []
    for g in range(2):
        cols = pl.ds(g * hid, hid)
        inner = mm(hidden_low[:, g * half : (g + 1) * half], wi_ref[g * half : (g + 1) * half, :])
        value, deriv = gelu_both(inner)
        act[:, cols] = value.astype(BF16)
        slope[:, cols] = deriv
        outers.append(mm(act[:, cols], wdn_ref[g * hid : (g + 1) * hid, :]))
    normed2, inv2 = norm_fwd(jnp.concatenate(outers, 1) + hidden)
    out_ref[0] = (normed2 * gain2 + shift2).astype(BF16)
    cot = cot_ref[0].astype(F32)
    gs_ref[2:3, :] += col_sum(cot * normed2)
    gs_ref[3:4, :] += col_sum(cot)
    d_sum = norm_back(cot * gain2, normed2, inv2)
    d_outer = d_sum.astype(BF16)
    d_hid = []
    for g in range(2):
        cols = pl.ds(g * hid, hid)
        mine = d_outer[:, g * half : (g + 1) * half]
        d_act = mm(mine, wdn_ref[g * hid : (g + 1) * hid, :], NT)
        gd_ref[:, cols] += mm(mine, act[:, cols], TN)
        dinner[:, cols] = (d_act * slope[:, cols]).astype(BF16)
        d_hid.append(mm(dinner[:, cols], wi_ref[g * half : (g + 1) * half, :], NT))
        gi_ref[g * half : (g + 1) * half, :] += mm(hidden_low[:, g * half : (g + 1) * half], dinner[:, cols], TN)
    d_hidden = jnp.concatenate(d_hid, 1) + d_sum
    gs_ref[0:1, :] += col_sum(d_hidden * normed1)
    gs_ref[1:2, :] += col_sum(d_hidden)
    d_res = norm_back(d_hidden * gain1, normed1, inv1)
    dres_ref[0] = d_res
    d_attn = d_res.astype(BF16)
    d_joined = mm(d_attn, wo_ref[...], NT)
    dctx_ref[0] = d_joined[:, 0:half].astype(BF16)
    dconv_ref[0] = d_joined[:, half:]
    go_ref[...] += mm(joined[...], d_attn, TN)

    @pl.when(last)
    def _():
        n, _, _ = gf_ref.shape
        rows = d // n
        tall = 2 * hid // n

        def emit(p, c):
            at = pl.ds(pl.multiple_of(p * rows, 8), rows)
            gi = gi_ref[at, :]
            go = go_ref[at, :]
            parts = [gi[:, j * half : (j + 1) * half] for j in range(hid // half)] + [go[:, 0:half], go[:, half:]]
            gf_ref[p, tall : tall + rows * len(parts), :] = jnp.concatenate(parts, 0).astype(BF16)
            return c

        lax.fori_loop(0, n, emit, 0)

        step = 4
        wide = step * tall

        def emit_down(i, c):
            block = gd_ref[:, pl.ds(pl.multiple_of(i * wide, 128), wide)].T.astype(BF16)
            for j in range(step):
                gf_ref[i * step + j, 0:tall, :] = block[j * tall : (j + 1) * tall, :]
            return c

        lax.fori_loop(0, n // step, emit_down, 0)


def stage_c(n, ctx, conv, x, cot, wo, wi, wdn, ln):
    mb, t, d = x.shape
    half = d // 2
    hid = wi.shape[1]
    packed = (d * d + d * hid + 2 * hid * half) // (n * half)
    sds = jax.ShapeDtypeStruct

    def tile(cols):
        return pl.BlockSpec((1, ROWS, cols), lambda b, i: (b, i, 0))

    return pl.pallas_call(
        kernel_c,
        out_shape=[
            sds((mb, t, d), BF16), sds((mb, t, d), F32), sds((mb, t, half), BF16), sds((mb, t, half), F32),
            sds((n, packed, half), BF16), sds((8, d), F32),
        ],
        grid=(mb, t // ROWS),
        in_specs=[
            tile(half), tile(half), tile(d), tile(d),
            whole(*wo.shape), whole(*wi.shape), whole(*wdn.shape), whole(*ln.shape),
        ],
        out_specs=[
            tile(d), tile(d), tile(half), tile(half),
            whole(n, packed, half), whole(8, d),
        ],
        scratch_shapes=[
            pltpu.VMEM((ROWS, d), BF16),
            pltpu.VMEM((ROWS, 2 * hid), BF16),
            pltpu.VMEM((ROWS, 2 * hid), F32),
            pltpu.VMEM((ROWS, 2 * hid), BF16),
            pltpu.VMEM((d, d), F32),
            pltpu.VMEM((d, hid), F32),
            pltpu.VMEM((half, 2 * hid), F32),
        ],
        compiler_params=params(2),
        name="ffn",
    )(ctx, conv, x, cot, wo, wi, wdn, ln)


KT = 256


def kernel_d(n, cuts, *refs):
    count = 1 if cuts else 0
    segt_ref, q_ref, k_ref, v_ref, ctx_ref, lse_ref, do_ref = refs[:7]
    srcs, refs = refs[7 : 7 + count], refs[7 + count :]
    dq_ref, dk_ref, dv_ref = refs[:3]
    outs, refs = refs[3 : 3 + count], refs[3 + count :]
    qa, da, dqt, *rest = refs
    plan = Scatters(n, cuts, srcs, outs, rest) if count else None
    times = (0, 1, 3, 4, 5)
    stage_points(n, plan, times, True)
    t = q_ref.shape[1]
    tail = t - SEG_MOST
    lane = lanes((1, 128))
    low_half = lane < 64
    one_b = jnp.ones((), BF16)
    zero_b = jnp.zeros((), BF16)

    r = lax.broadcasted_iota(jnp.int32, (256, 128), 0) % 128
    c = lax.broadcasted_iota(jnp.int32, (256, 128), 1)
    swap = jnp.where((r < 64) != (c < 64), 1.0, 0.0).astype(BF16)
    prod = do_ref[0].astype(F32) * ctx_ref[0].astype(F32)
    hi, lo = split2(prod)
    dsum = mm(jnp.concatenate([hi, lo], 1), swap)
    q8 = q_ref[0] * 0.125
    do = do_ref[0]
    for stat, src, dst in ((lse_ref[0], q8, qa), (dsum, do, da)):
        pieces = split3(-stat)
        code = jnp.where(
            (lane & 63) == 0, pieces[0], jnp.where((lane & 63) == 1, pieces[1], jnp.where((lane & 63) == 2, pieces[2], zero_b))
        )
        dst[0] = jnp.where(low_half, src, code)
        dst[1] = jnp.where(low_half, code, src)

    def run(key_rows, q_rows, h, codes):
        mark = (lane & 63) < 3
        mine = low_half if h == 0 else ~low_half
        k = k_ref[0, key_rows, :]
        v = v_ref[0, key_rows, :]
        ka = jnp.where(mine, k, jnp.where(mark, one_b, zero_b))
        va = jnp.where(mine, v, jnp.where(mark, one_b, zero_b))
        qh = qa[h, q_rows, :]
        if codes is not None:
            hot, pen = codes
            qh = qh + pen
            ka = ka + hot
        p = jnp.exp(mm(ka, qh, NT))
        dp = mm(va, da[h, q_rows, :], NT)
        ds = (p * dp).astype(BF16)
        dv = mm(p.astype(BF16), do_ref[0, q_rows, :])
        dk = mm(ds, q_ref[0, q_rows, :] * 0.125)
        return ds, dk, dv, k

    main = pl.ds(0, SEG_MOST)

    def tile(i, carry):
        rows = pl.ds(pl.multiple_of(i * KT, KT), KT)
        halves = []
        for h in range(2):
            ds, dk, dv, k = run(rows, main, h, None)
            part = mm(k[:, 64 * h : 64 * h + 64], ds, TN)
            dqt[64 * h : 64 * h + 64, :] = jnp.where(i == 0, part, dqt[64 * h : 64 * h + 64, :] + part)
            halves.append((dk, dv))
        dk_ref[0, rows, :] = jnp.where(low_half, halves[0][0], halves[1][0]).astype(BF16)
        dv_ref[0, rows, :] = jnp.where(low_half, halves[0][1], halves[1][1]).astype(BF16)
        return carry

    dqt[...] = jnp.zeros_like(dqt)
    lax.fori_loop(0, SEG_MOST // KT, tile, 0)
    dq_ref[0, main, :] = dqt[...].T * 0.125

    rows = pl.ds(SEG_MOST, tail)
    segb = jnp.broadcast_to(segt_ref[...], (128, tail)).T
    halves = []
    for h in range(2):
        hot, pen = seg_codes(segb, 64 - 64 * h + 8)
        ds, dk, dv, k = run(rows, rows, h, (hot.astype(BF16), pen.astype(BF16)))
        halves.append((dk, dv, mm(ds, k, TN)))
    for ref, i in ((dk_ref, 0), (dv_ref, 1)):
        ref[0, rows, :] = jnp.where(low_half, halves[0][i], halves[1][i]).astype(BF16)
    dq_ref[0, rows, :] = jnp.where(low_half, halves[0][2], halves[1][2]) * 0.125
    stage_points(n, plan, times, False)


def stage_d(n, segt, q, k, v, ctx, lse, dctx, more):
    mb, t, half = q.shape
    cuts = Scatters.cuts(more, 2)
    sds = jax.ShapeDtypeStruct
    return pl.pallas_call(
        partial(kernel_d, n, cuts),
        out_shape=[sds((mb, t, half), F32), sds((mb, t, half), BF16), sds((mb, t, half), BF16)]
        + [sds(w.shape[1:], F32) for w in more],
        grid=(mb, half // 128),
        in_specs=[seg_tail(t - SEG_MOST)] + [pair(t)] * 6 + [ANY] * len(more),
        out_specs=[pair(t)] * 3 + [whole(*w.shape[1:]) for w in more],
        scratch_shapes=[
            pltpu.VMEM((2, t, 128), BF16), pltpu.VMEM((2, t, 128), BF16), pltpu.VMEM((128, SEG_MOST), F32),
        ]
        + (Scatters.scratch(n, cuts, more) if more else []),
        compiler_params=params(2, 4 if more else None),
        name="att_bwd",
    )(segt, q, k, v, ctx, lse, dctx, *more)


def kernel_e(
    s_ref, seg_ref, x_ref, out_ref_in, dres_ref, dconv_ref, dq_ref, dk_ref, dv_ref,
    q_ref, c_ref, depth_ref, span_ref, mixed_ref, taps_ref, wp_ref, wd_ref, wpt_ref, wk_ref, gs_ref,
    gx_ref, out_ref, gm_ref,
    pad, xs, segb, vt, dcs, dts, e_ref, er_ref, texp, dlt, rt, dm, dl, gacc, gp_ref, gpt_ref, gk_ref, small,
):
    t, d = x_ref.shape[1:]
    half = d // 2
    nch = d // 128
    b = pl.program_id(0)
    s = s_ref[b]

    @pl.when(b == 0)
    def _():
        fill_expander(e_ref)
        row = lax.broadcasted_iota(jnp.int32, er_ref.shape, 0)
        col = lax.broadcasted_iota(jnp.int32, er_ref.shape, 1)
        head = ((row % 768) % half) // 64
        er_ref[...] = jnp.where(col == (row // 768) * 8 + head, 1.0, 0.0).astype(BF16)
        for ref in (xs, dts, dcs):
            n = ref.shape[0]
            ref[:, 0:8, :] = jnp.zeros((n, 8, 128), F32)
            ref[:, t + 8 : t + 16, :] = jnp.zeros((n, 8, 128), F32)
        gp_ref[...] = jnp.zeros_like(gp_ref)
        gpt_ref[...] = jnp.zeros_like(gpt_ref)
        gk_ref[...] = jnp.zeros_like(gk_ref)
        gacc[...] = jnp.zeros_like(gacc)

    fill_segments(seg_ref, segb, vt)
    cw = xs
    for j in range(nch // 2):
        cols = pl.ds(j * 128, 128)
        cw[j, 8 : t + 8, :] = c_ref[0, :, cols].astype(F32)
        dcs[j, 8 : t + 8, :] = dconv_ref[0, :, cols]

    def dtap_tile(i, carry):
        r0 = pl.multiple_of(i * 128, 128)
        rows = pl.ds(r0, 128)
        acc = None
        for o in range(KERNEL):
            his, los = [], []
            for j in range(nch // 2):
                prod = cw[j, pl.ds(8 + r0 + o - REACH, 128), :] * dcs[j, pl.ds(8 + r0, 128), :]
                hi, lo = split2(prod)
                his.append(hi)
                los.append(lo)
            part = mm(jnp.concatenate(his + los, 1), er_ref[o * 768 : (o + 1) * 768, :])
            acc = part if acc is None else acc + part
        dlt[:, rows] = acc.T[0:72, :]
        return carry

    lax.fori_loop(0, t // 128, dtap_tile, 0)

    taps = [taps_ref[0, o * 8 : o * 8 + 8, :] for o in range(KERNEL)]
    dtaps = [dlt[o * 8 : o * 8 + 8, :] * vt[o] for o in range(KERNEL)]
    mean = taps[0] * dtaps[0]
    for o in range(1, KERNEL):
        mean = mean + taps[o] * dtaps[o]
    for o in range(KERNEL):
        dl[o * 8 : o * 8 + 8, :] = taps[o] * (dtaps[o] - mean)
        tv = taps[o] * vt[o]
        move = (o - REACH) % t
        rt[o * 8 : o * 8 + 8, :] = pltpu.roll(tv, move, 1) if move else tv

    def point_tile(i, carry):
        r0 = pl.multiple_of(i * 384, 128)
        rows = pl.ds(r0, 384)
        dlog = dl[:, rows].astype(BF16)
        d_mixed = mm(dlog, wk_ref[...], TN)
        gk_ref[...] += mm(dlog, mixed_ref[0, rows, :])
        d_span = (d_mixed * q_ref[0, rows, :].astype(F32)).astype(BF16)
        dm[rows, 0:half] = (dq_ref[0, rows, :] + d_mixed * span_ref[0, rows, :]).astype(BF16)
        dm[rows, half : 2 * half] = dk_ref[0, rows, :]
        dm[rows, 2 * half : 3 * half] = dv_ref[0, rows, :]
        gpt_ref[...] += mm(depth_ref[0, rows, :], d_span, TN)
        d_depth = mm(d_span, wpt_ref[...], NT)
        for j in range(nch):
            dts[j, pl.ds(8 + r0, 384), :] = d_depth[:, j * 128 : (j + 1) * 128]
        return carry

    lax.fori_loop(0, t // 384, point_tile, 0)

    def dc_tile(i, carry):
        r0 = pl.multiple_of(i * 128, 128)
        rows = pl.ds(r0, 128)
        texp[...] = expand_taps(rt[:, rows], e_ref)
        for j in range(nch // 2):
            acc = None
            for o in range(KERNEL):
                part = dcs[j, pl.ds(8 + r0 - o + REACH, 128), :] * texp[:, o * half + j * 128 : o * half + (j + 1) * 128]
                acc = part if acc is None else acc + part
            dm[rows, pl.ds(3 * half + j * 128, 128)] = acc.astype(BF16)
        return carry

    lax.fori_loop(0, t // 128, dc_tile, 0)

    for j in range(nch):
        xs[j, 8 : t + 8, :] = x_ref[0, :, pl.ds(j * 128, 128)].astype(F32)

    def proj_tile(i, carry):
        r0 = pl.multiple_of(i * 384, 128)
        rows = pl.ds(r0, 384)
        gp_ref[...] += mm(x_ref[0, rows, :], dm[rows, :], TN)
        gx = mm(dm[rows, :], wp_ref[...], NT) + dres_ref[0, rows, :]
        for j in range(nch):
            pad[j, pl.ds(r0, 384), :] = gx[:, j * 128 : (j + 1) * 128]
        return carry

    lax.fori_loop(0, t // 384, proj_tile, 0)

    def depth_tile(r0, masked):
        masks = mask_rows(segb, r0, 128) if masked else None
        for j in range(nch):
            acc = pad[j, pl.ds(r0, 128), :]
            own = dts[j, pl.ds(8 + r0, 128), :]
            for o in range(KERNEL):
                w = wd_ref[KERNEL - 1 - o : KERNEL - o, pl.ds(j * 128, 128)]
                near = dts[j, pl.ds(8 + r0 + o - REACH, 128), :]
                xw = xs[j, pl.ds(8 + r0 + o - REACH, 128), :]
                if masked:
                    near = near * masks[o]
                    xw = xw * masks[o]
                acc = acc + near * w
                term = (own * xw).reshape(16, 8, 128)
                gacc[o, :, pl.ds(j * 128, 128)] += jnp.sum(term, 0)
            pad[j, pl.ds(r0, 128), :] = acc

    masked_tiles(t, depth_tile)

    for j in range(nch):
        cols = pl.ds(j * 128, 128)
        pad[j, pl.ds(t, 128), :] = pad[j, 0:128, :]
        back = t - s
        first = pl.ds(back, 128)
        gx_ref[0, :, cols] = xs[j, 8 : t + 8, :]
        xs[j, 0:128, :] = pad[j, first, :]
        gx_ref[0, 0:128, cols] = xs[j, 0:128, :]
        gx_ref[0, 128:, cols] = pad[j, pl.ds(128 - s, t - 128), :]
        pad[j, 0:t, :] = out_ref_in[0, :, cols].astype(F32)
        pad[j, pl.ds(t, 128), :] = pad[j, 0:128, :]
        out_ref[0, 0:128, cols] = pad[j, first, :].astype(BF16)
        out_ref[0, 128:, cols] = pad[j, pl.ds(128 - s, t - 128), :].astype(BF16)

    @pl.when(b == pl.num_programs(0) - 1)
    def _():
        n = gm_ref.shape[0]
        rows = d // n
        small[...] = jnp.zeros_like(small)
        for o in range(KERNEL):
            small[o : o + 1, :] = jnp.sum(gacc[o], 0, keepdims=True)
        small[16:24, :] = gs_ref[...]
        row = lax.broadcasted_iota(jnp.int32, (128, 72), 0)
        col = lax.broadcasted_iota(jnp.int32, (128, 72), 1)
        order = jnp.where((row < HEADS * KERNEL) & (row % KERNEL * 8 + row // KERNEL == col), 1.0, 0.0).astype(BF16)
        gk = mm(order, gk_ref[...].astype(BF16)).astype(BF16)
        row = lax.broadcasted_iota(jnp.int32, (half, d), 0)
        col = lax.broadcasted_iota(jnp.int32, (half, d), 1)
        piece = col % PIECE
        put = jnp.where((piece < PIECE // 2) & (col // PIECE * (PIECE // 2) + piece == row), 1.0, 0.0).astype(BF16)
        gk = mm(gk, put)
        for j in range(nch):
            cols = pl.ds(j * 128, 128)
            pad[0, cols, :] = small[:, cols].T
            pad[1, cols, :] = gk[:, j * 128 : (j + 1) * 128].T

        def emit(p, c):
            at = pl.ds(pl.multiple_of(p * rows, 8), rows)
            gp = gp_ref[at, :]
            parts = [gp[:, j * half : (j + 1) * half] for j in range(gp.shape[1] // half)] + [gpt_ref[at, :]]
            parts.append(jnp.concatenate([pad[0, at, :], pad[1, at, :], jnp.zeros((rows, half - 256), F32)], 1))
            gm_ref[p] = jnp.concatenate(parts, 0).astype(BF16)
            return c

        lax.fori_loop(0, n, emit, 0)


def stage_e(n, s, segr, x, out_r, dres, dconv, dq, dk, dv, q, c, depth, span, mixed, taps, wp, wd, wpt, wk, gs):
    mb, t, d = x.shape
    half = d // 2
    packed = (d * 2 * d + d * half) // (n * half) + d // n
    sds = jax.ShapeDtypeStruct

    def slow(*shape):
        return pl.BlockSpec((1,) + shape, lambda b, *_: (b,) + (0,) * len(shape), pipeline_mode=pl.Buffered(1))

    return pl.pallas_call(
        kernel_e,
        out_shape=[
            sds((mb, t, d), F32), sds((mb, t, d), BF16), sds((n, packed, half), BF16),
        ],
        grid_spec=pltpu.PrefetchScalarGridSpec(
            num_scalar_prefetch=1,
            grid=(mb,),
            in_specs=[pl.BlockSpec((pl.Squeezed(), 1, t), lambda b, *_: (b, 0, 0))]
            + [slow(t, d), slow(t, d), slow(t, d), slow(t, half), slow(t, half), slow(t, half), slow(t, half)]
            + [slow(t, half), slow(t, half), slow(t, d), slow(t, half), slow(t, half), slow(72, t)]
            + [whole(*w.shape) for w in (wp, wd, wpt, wk, gs)],
            out_specs=[slow(t, d), slow(t, d), whole(n, packed, half)],
            scratch_shapes=[
                pltpu.VMEM((d // 128, t + 128, 128), F32),
                pltpu.VMEM((d // 128, t + 16, 128), F32),
                pltpu.VMEM((t + 16, 128), F32),
                pltpu.VMEM((KERNEL, 8, t), F32),
                pltpu.VMEM((half // 128, t + 16, 128), F32),
                pltpu.VMEM((d // 128, t + 16, 128), F32),
                pltpu.VMEM((144, KERNEL * half), BF16),
                pltpu.VMEM((KERNEL * 768, 128), BF16),
                pltpu.VMEM((128, KERNEL * half), F32),
                pltpu.VMEM((72, t), F32),
                pltpu.VMEM((72, t), F32),
                pltpu.VMEM((t, 2 * d), BF16),
                pltpu.VMEM((72, t), F32),
                pltpu.VMEM((KERNEL, 8, d), F32),
                pltpu.VMEM(wp.shape, F32),
                pltpu.VMEM(wpt.shape, F32),
                pltpu.VMEM((72, half), F32),
                pltpu.VMEM((128, d), F32),
            ],
        ),
        compiler_params=params(1),
        name="mix_bwd",
    )(s, segr, x, out_r, dres, dconv, dq, dk, dv, q, c, depth, span, mixed, taps, wp, wd, wpt, wk, gs)


def rolled_segments(segments):
    mb, t = segments.shape
    span = t - SEG_MOST + 1
    hit = segments[:, :span] == segments[:, SEG_MOST - 1 :]
    s = jnp.sum(jnp.where(hit, jnp.arange(span, dtype=jnp.int32)[None, :], 0), 1).astype(jnp.int32)
    twice = jnp.concatenate([segments, segments[:, : t - SEG_MOST]], 1).astype(F32)
    rows = [lax.dynamic_slice(twice[b], (s[b],), (t,)) for b in range(mb)]
    return s, jnp.stack(rows)[:, None, :]


def pack_small(w_depth, w_kernel, g1, b1, g2, b2):
    rows = w_depth.shape[0]
    units = rows // PIECE
    heads = w_kernel.reshape(units, PIECE // 2, HEADS, KERNEL).transpose(0, 1, 3, 2)
    heads = jnp.pad(heads, ((0, 0), (0, PIECE // 2), (0, 0), (0, 8 - HEADS))).reshape(rows, 8 * KERNEL)
    norms = jnp.stack([g1, b1, g2, b2], 1)
    gap = jnp.zeros((rows, 16 - KERNEL), BF16)
    return jnp.concatenate(
        [w_depth, gap, norms, jnp.zeros((rows, 128 - 20), BF16), heads, jnp.zeros((rows, 128 - 8 * KERNEL), BF16)], 1
    )


def finish_kernel(f_ref, m_ref, gp_ref, gdep_ref, gpt_ref, gk_ref, go_ref, gi_ref, gd_ref, gs_ref):
    half = f_ref.shape[1]
    rows = gp_ref.shape[0]
    tall = gd_ref.shape[0]
    gd_ref[...] = f_ref[0:tall, :]
    for j in range(gi_ref.shape[1] // half):
        gi_ref[:, j * half : (j + 1) * half] = f_ref[tall + j * rows : tall + (j + 1) * rows, :]
    tall = tall + rows * (gi_ref.shape[1] // half)
    for j in range(2):
        go_ref[:, j * half : (j + 1) * half] = f_ref[tall + j * rows : tall + (j + 1) * rows, :]
    wide = gp_ref.shape[1] // half
    for j in range(wide):
        gp_ref[:, j * half : (j + 1) * half] = m_ref[j * rows : (j + 1) * rows, :]
    gpt_ref[...] = m_ref[wide * rows : (wide + 1) * rows, :]
    small = m_ref[(wide + 1) * rows : (wide + 2) * rows, 0:256]
    gdep_ref[...] = small[:, 0:KERNEL]
    gk_ref[...] = small[0 : rows // 2, 128 : 128 + HEADS * KERNEL]
    gs_ref[...] = small[:, 16:24]


def finish(n, d, hid, f, m):
    half = d // 2
    sds = jax.ShapeDtypeStruct
    rows = d // n
    return pl.pallas_call(
        finish_kernel,
        out_shape=[
            sds((rows, 2 * d), F32), sds((rows, KERNEL), F32), sds((rows, half), F32), sds((half // n, HEADS * KERNEL), F32),
            sds((rows, d), F32), sds((rows, hid), F32), sds((2 * hid // n, half), F32), sds((rows, 8), F32),
        ],
        name="finish",
    )(f, m)


def side_by_side(block, parts):
    units, _, cols = block.shape
    return block.reshape(units, parts, PIECE, cols).transpose(0, 2, 1, 3).reshape(units * PIECE, parts * cols)


def native_sums(gf, gm, d, hid):
    gf, gm = gf.astype(F32), gm.astype(F32)
    half = d // 2
    tall = 2 * hid * PIECE // d
    wide = hid // half * PIECE
    many_p = 2 * d // half
    g_down = gf[:, :tall].reshape(-1, half)
    g_in = side_by_side(gf[:, tall : tall + wide], hid // half)
    g_out = side_by_side(gf[:, tall + wide :], 2)
    g_proj = side_by_side(gm[:, : many_p * PIECE], many_p)
    g_point = gm[:, many_p * PIECE : (many_p + 1) * PIECE].reshape(-1, half)
    small = gm[:, (many_p + 1) * PIECE :]
    g_kernel = small[:, : PIECE // 2, 128 : 128 + HEADS * KERNEL].reshape(half, -1)
    small = small[:, :, 0:24].reshape(d, -1)
    grads = [g_proj, small[:, :KERNEL], g_point, g_kernel, g_out, g_in, g_down, small[:, 16:]]
    return [lax.psum_scatter(g, "tok", scatter_dimension=0, tiled=True) for g in grads]


def rows_of(w):
    return w.reshape(-1, w.shape[2])


def shards(n, tokens, segments, cotangent, w_proj, w_depth, w_point, w_kernel, w_out, g1, b1, w_in, w_down, g2, b2):
    d = tokens.shape[-1]
    hid = w_in.shape[1]
    units = d // PIECE
    own = n == units
    if own:
        small = pack_small(w_depth, w_kernel, g1, b1, g2, b2)
        wp, sm, wpt = (rows_of(w) for w in gather_all(n, [w_proj, small, w_point]))
        more_a, more_b = [w_in, w_out], [w_down]
    else:
        given = [w_proj, w_in, w_down, w_point, w_out, w_depth, w_kernel, g1, b1, g2, b2]
        wp, wi, wdn, wpt, wo, *rest = [lax.all_gather(w, "tok", axis=0, tiled=True) for w in given]
        sm = pack_small(*rest)
        more_a = more_b = []
    s, segr = rolled_segments(segments[:, 0])
    segt = segr[:, :, SEG_MOST:]
    xr, cotr, q, k, v, c, depth, span, mixed, taps, conv, wd_rows, wk_rows, *got_a = stage_a(
        n, s, tokens, cotangent, segr, wp, sm, wpt, more_a
    )
    ctx, lse, *got_b = stage_b(n, segt, q, k, v, more_b)
    if own:
        wi, wo, wdn = (rows_of(w) for w in got_a + got_b)
    out_r, dres, dctx, dconv, gf, g_small = stage_c(units, ctx, conv, xr, cotr, wo, wi, wdn, wd_rows)
    dq, dk, dv, *sums = stage_d(n, segt, q, k, v, ctx, lse, dctx, [gf] if own else [])
    gx, out, gm = stage_e(
        units, s, segr, xr, out_r, dres, dconv, dq, dk, dv, q, c, depth, span, mixed, taps, wp, wd_rows, wpt, wk_rows,
        g_small,
    )
    if own:
        sums = finish(n, d, hid, sums[0], scatter_all(n, 1, [gm], 4)[0])
    else:
        sums = native_sums(gf, gm, d, hid)
    g_proj, g_depth, g_point, g_kernel, g_out, g_in, g_down, g_vec = sums
    return (
        out, gx, g_proj, g_depth, g_point, g_kernel, g_out, g_vec[:, 0], g_vec[:, 1], g_in, g_down,
        g_vec[:, 2], g_vec[:, 3],
    )


def solution(mesh):
    rows, vec, act = P("tok", None), P("tok"), P(None, "tok", None)
    in_specs = (act, act, act, rows, rows, rows, rows, rows, vec, vec, rows, rows, vec, vec)
    out_specs = (act, act, rows, rows, rows, rows, rows, vec, vec, rows, rows, vec, vec)
    run = partial(shards, mesh.shape["tok"])
    return jax.shard_map(run, mesh=mesh, in_specs=in_specs, out_specs=out_specs, check_vma=False)
```

```python
import math
from functools import partial

import jax
import jax.numpy as jnp
from jax import lax
from jax.experimental import pallas as pl
from jax.experimental.pallas import tpu as pltpu
from jax.sharding import PartitionSpec as P

HEADS = 6
KERNEL = 9
REACH = 4
SEG_MOST = 1024
NORM_EPS = 1e-12
F32 = jnp.float32
BF16 = jnp.bfloat16
NT = (((1,), (1,)), ((), ()))
NN = (((1,), (0,)), ((), ()))
TN = (((0,), (0,)), ((), ()))
VMEM_CAP = 62 * 1024 * 1024
MESH = pl.DeviceIdType.MESH
PIECE = 24


def mm(a, b, dims=NN):
    return lax.dot_general(a, b, dims, preferred_element_type=F32)


def lanes(shape):
    return lax.broadcasted_iota(jnp.int32, shape, 1)


def split2(v):
    hi = v.astype(BF16)
    return hi, (v - hi.astype(F32)).astype(BF16)


def split3(v):
    hi = v.astype(BF16)
    rest = v - hi.astype(F32)
    mid = rest.astype(BF16)
    return hi, mid, (rest - mid.astype(F32)).astype(BF16)


def partner(me, bit):
    return me + (1 - 2 * lax.rem(lax.div(me, bit), 2)) * bit


def bit_of(me, bit):
    return lax.rem(lax.div(me, bit), 2)


def bit_orders(n):
    one = [1 << b for b in range(n.bit_length() - 1)]
    two = one[:1] + one[2:3] + one[1:2] + one[3:] if len(one) > 2 else one
    return one, two


def greet(n):
    me = lax.axis_index("tok")
    barrier = pltpu.get_barrier_semaphore()
    bits = bit_orders(n)[0]
    for bit in bits:
        pl.semaphore_signal(barrier, inc=1, device_id=(partner(me, bit),), device_id_type=MESH)
    pl.semaphore_wait(barrier, len(bits))


class Gather:
    def __init__(self, src, dst, take, part, order, send, recv, own):
        self.src, self.all, self.part, self.order = src.at[take], dst, part, order[::-1]
        self.send, self.recv, self.own = send, recv, own
        self.me = lax.axis_index("tok")

    def sizes(self):
        one = math.prod(self.src.shape) * jnp.dtype(self.all.dtype).itemsize
        return [one << i for i in range(len(self.order))]

    def held(self, s):
        free = self.order[:s]
        bits = [1 << b for b in reversed(range(len(self.order)))]
        return self.all.at[tuple(ALL if bit in free else bit_of(self.me, bit) for bit in bits) + self.part]

    def wait(self, sem, s):
        ref = self.held(s)
        pltpu.make_async_copy(ref, ref, sem.at[s]).wait()

    def step(self, s):
        if s == 0:
            pltpu.make_async_copy(self.src, self.held(0), self.own).start()
        elif s == 1:
            pltpu.make_async_copy(self.src, self.held(0), self.own).wait()
        if s > 0:
            self.wait(self.recv, s - 1)
        if s < len(self.order):
            pltpu.make_async_remote_copy(
                src_ref=self.held(s) if s else self.src,
                dst_ref=self.held(s),
                send_sem=self.send.at[s],
                recv_sem=self.recv.at[s],
                device_id=(partner(self.me, self.order[s]),),
                device_id_type=MESH,
            ).start()
        else:
            for i in range(s):
                self.wait(self.send, i)


def halves(order, s):
    left = sorted(set(order) - set(order[:s]), reverse=True)
    at = left.index(order[s])
    return 1 << at, 1 << (len(left) - 1 - at)


class Scatter:
    def __init__(self, n, src, first, out, mine, got, order, send, recv, own):
        self.n, self.src, self.mine, self.got, self.order, self.out = n, src, mine, got, order, out
        self.rows = pl.ds(first, mine.shape[1])
        self.send, self.recv, self.own = send, recv, own
        self.me = lax.axis_index("tok")

    def sizes(self):
        one = math.prod(self.mine.shape[1:]) * 2
        return [one * (self.n >> (i + 1)) for i in range(len(self.order))]

    def side(self, s, keep):
        hi, lo = halves(self.order, s)
        bit = bit_of(self.me, self.order[s])
        which = bit if keep else 1 - bit
        if s == 0:
            view = self.src.reshape((hi, 2, lo) + self.src.shape[1:])
            return view.at[:, which, :, self.rows]
        held = self.got[s - 1]
        return held.reshape((hi, 2, lo) + held.shape[1:]).at[:, which]

    def there(self, ref, s):
        hi, lo = halves(self.order, s)
        return ref.reshape((hi, lo) + ref.shape[1:])

    def send_copy(self, s):
        return pltpu.make_async_remote_copy(
            src_ref=self.side(s, False),
            dst_ref=self.there(self.got[s], s),
            send_sem=self.send.at[s],
            recv_sem=self.recv.at[s],
            device_id=(partner(self.me, self.order[s]),),
            device_id_type=MESH,
        )

    def own_copy(self):
        return pltpu.make_async_copy(self.side(0, True), self.there(self.mine, 0), self.own)

    def add(self, s):
        self.send_copy(s).wait_recv()
        got = self.got[s]
        if s == 0:
            self.own_copy().wait()

            def first(k, c):
                got[k] = (got[k].astype(F32) + self.mine[k].astype(F32)).astype(BF16)
                return c

            lax.fori_loop(0, got.shape[0], first, 0)
            return
        hi, lo = halves(self.order, s)
        held = self.got[s - 1]
        bit = bit_of(self.me, self.order[s])

        def one(k, c):
            for i in range(lo):
                to, at = k * lo + i, (k * 2 + bit) * lo + i
                got[to] = (got[to].astype(F32) + held[at].astype(F32)).astype(BF16)
            return c

        if s < len(self.order) - 1:
            lax.fori_loop(0, hi, one, 0)
        else:
            self.out[self.rows, :] = got[0].astype(F32) + held[bit].astype(F32)

    def step(self, s):
        if s > 0:
            self.add(s - 1)
        if s < len(self.order):
            self.send_copy(s).start()
        if s == 0:
            self.own_copy().start()
        if s == len(self.order):
            for i in range(s):
                self.send_copy(i).wait_send()


ANY = pl.BlockSpec(memory_space=pl.ANY)


def remote(cid):
    return pltpu.CompilerParams(collective_id=cid, has_side_effects=True, vmem_limit_bytes=VMEM_CAP)


RATES = {1: 1 / 350e3, 2: 2 / 90e3, 4: 2 / 90e3, 8: 2 / 90e3, 16: 4 / 90e3}
STAGE = 2.5


def schedule(parts, last, spots):
    link = [{1: 0, 2: 1, 4: 2}.get(bit, 3) for bit in range(1 << last)]
    free, ready, at = [0.0] * 4, [0.0] * len(parts), [0] * len(parts)
    plan = []
    for now in spots:
        due = []
        for p, (bits, sizes) in enumerate(parts):
            if at[p] <= last and ready[p] <= now:
                due.append((p, at[p]))
                if at[p] < last:
                    bit = bits[at[p]]
                    begin = max(now, free[link[bit]])
                    free[link[bit]] = begin + sizes[at[p]] * RATES.get(bit, 4 / 90e3)
                    ready[p] = free[link[bit]] + STAGE
                at[p] += 1
        plan.append(due)
    plan.append([(p, i) for i in range(last + 1) for p in range(len(parts)) if at[p] <= i])
    return plan


class Timed:
    def __init__(self, n, parts, spots=None):
        self.parts = parts
        self.last = n.bit_length() - 1
        self.ticks = self.last + 1
        self.plan = [[(p, t) for p in range(len(parts))] for t in range(self.ticks)]
        if spots is not None:
            self.plan = schedule([(p.order, p.sizes()) for p in parts], self.last, spots)
            self.ticks = len(self.plan)

    def tick(self, t):
        for p, i in self.plan[t]:
            self.parts[p].step(i)


ALL = slice(None)


def pieces(wide, count, rows=False):
    size = wide // count
    cuts = [pl.ds(i * size, size) for i in range(count)]
    return [(c, ALL) if rows else (ALL, c) for c in cuts]


def gathers(n, srcs, dsts, layout, sems, spots=None):
    send, recv, own = sems
    orders = bit_orders(n)
    return Timed(
        n,
        [
            Gather(srcs[a], dsts[a], parts[0], parts[-1], orders[i % 2], send.at[i], recv.at[i], own.at[i])
            for i, (a, *parts) in enumerate(layout)
        ],
        spots,
    )


def gather_sems(n, layout):
    stages, count = n.bit_length() - 1, len(layout)
    dma = pltpu.SemaphoreType.DMA
    return [dma((count, stages)), dma((count, stages)), dma((count,))]


def gathered(n, shards):
    return [jax.ShapeDtypeStruct((2,) * (n.bit_length() - 1) + w.shape, w.dtype) for w in shards]


def split_rows(rows, parts):
    tiles = rows // 16
    cuts = [tiles * i // parts * 16 for i in range(parts + 1)]
    return [(a, b - a) for a, b in zip(cuts, cuts[1:]) if b > a]


def scatters(n, cuts, srcs, outs, refs, spots=None):
    total, stages = len(cuts), n.bit_length() - 1
    accs, gots, (send, recv, own) = refs[:total], refs[total:-3], refs[-3:]
    gots = [gots[stages * j : stages * (j + 1)] for j in range(total)]
    orders = bit_orders(n)
    return Timed(
        n,
        [
            Scatter(n, srcs[i], a, outs[i], accs[j], gots[j], orders[j % 2], send.at[j], recv.at[j], own.at[j])
            for j, (i, a, r) in enumerate(cuts)
        ],
        spots,
    )


def scatter_cuts(packed, parts):
    return [(i, a, r) for i, w in enumerate(packed) for a, r in split_rows(w.shape[1], parts)]


def scatter_scratch(n, cuts, packed):
    total, stages = len(cuts), n.bit_length() - 1
    dma = pltpu.SemaphoreType.DMA
    bufs = [(r, packed[i].shape[2]) for i, a, r in cuts]
    return (
        [pltpu.VMEM((n // 2,) + b, BF16) for b in bufs]
        + [pltpu.VMEM((n >> (s + 1),) + b, BF16) for b in bufs for s in range(stages)]
        + [dma((total, stages)), dma((total, stages)), dma((total,))]
    )


def scatter_all(n, cid, packed, parts):
    cuts = scatter_cuts(packed, parts)
    count = len(packed)

    def kernel(*refs):
        greet(n)
        plan = scatters(n, cuts, refs[:count], refs[count : 2 * count], refs[2 * count :])
        for t in range(plan.ticks):
            plan.tick(t)

    return pl.pallas_call(
        kernel,
        out_shape=[jax.ShapeDtypeStruct(w.shape[1:], F32) for w in packed],
        in_specs=[ANY] * count,
        out_specs=[pl.BlockSpec(memory_space=pltpu.VMEM)] * count,
        scratch_shapes=scatter_scratch(n, cuts, packed),
        compiler_params=remote(cid),
        name="scatter",
    )(*packed)


def expand_taps(tap_rows, e_ref):
    hi, lo = split2(tap_rows)
    both = jnp.concatenate([hi, lo], 0)
    return mm(both, e_ref[...], TN)


def fill_expander(e_ref):
    half = e_ref.shape[1] // KERNEL
    shape = (72, 128)
    row = lax.broadcasted_iota(jnp.int32, shape, 0)
    upper = jnp.where(lanes(shape) >= 64, 1, 0)
    for o in range(KERNEL):
        for j in range(half // 128):
            one = jnp.where(row == upper + (o * 8 + 2 * j), 1.0, 0.0).astype(BF16)
            cols = pl.ds(o * half + j * 128, 128)
            e_ref[0:72, cols] = one
            e_ref[72:144, cols] = one


def mask_rows(segb_ref, r0, rows):
    own = segb_ref[pl.ds(8 + r0, rows), :]
    return [
        jnp.where(segb_ref[pl.ds(8 + r0 + o - REACH, rows), :] == own, 1.0, 0.0)
        for o in range(KERNEL)
    ]


def fill_segments(seg_ref, segb_ref, vt_ref):
    t = seg_ref.shape[-1]
    row = seg_ref[...]
    if segb_ref is not None:
        wide = jnp.broadcast_to(row, (128, t))
        segb_ref[0:8, :] = jnp.full((8, 128), -1.0, F32)
        segb_ref[t + 8 : t + 16, :] = jnp.full((8, 128), -1.0, F32)
        segb_ref[8 : t + 8, :] = wide.T
    if vt_ref is None:
        return
    tall = jnp.broadcast_to(row, (8, t))
    pos = lanes((8, t))
    for o in range(KERNEL):
        d = o - REACH
        moved = pltpu.roll(tall, (-d) % t, 1) if d else tall
        inside = (pos + d >= 0) & (pos + d < t)
        vt_ref[o] = jnp.where(inside & (moved == tall), 1.0, 0.0)


def masked_tiles(t, body, between=None):
    full = SEG_MOST // 128

    def inner(i, c):
        body(pl.multiple_of(i * 128, 128), False)
        return c

    lax.fori_loop(1, full - 1, inner, 0)
    if between is not None:
        between()

    def edge(i, c):
        idx = jnp.where(i == 0, 0, i + full - 2)
        body(pl.multiple_of(idx * 128, 128), True)
        return c

    lax.fori_loop(0, t // 128 - full + 2, edge, 0)


def piece_rows(d):
    small = PIECE // 2
    row = lax.broadcasted_iota(jnp.int32, (d, d // 2), 0)
    col = lanes((1, d // 2))
    return jnp.where(row == col + col // small * small, 1.0, 0.0).astype(BF16)


def unpack_small(sm_ref, wd_ref, wk_ref):
    d = sm_ref.shape[0]
    parts = [sm_ref[j * 128 : (j + 1) * 128, :].T for j in range(d // 128)]
    tall = jnp.concatenate(parts, 1)
    wd_ref[...] = tall[0:24, :]
    wk_ref[...] = mm(tall[32:104, :].astype(BF16), piece_rows(d), NN).astype(BF16)


def front_layout(d, half):
    cols = pieces(2 * d, 4)
    rest = [(1, (ALL, pl.ds(0, 128))), (1, (ALL, pl.ds(128, half - 128)))]
    return [(0, cols[0]), (0, cols[1]), (2, (ALL, ALL)), (0, cols[2]), (0, cols[3])] + rest


def kernel_front(n, layout, *refs):
    s_ref, x_ref, cot_ref = refs[:3]
    if layout:
        sm_src, wp_src, wpt_src = refs[3:6]
        xr_ref, cotr_ref, wd_ref, wk_ref, wp_far, wpt_far = refs[6:12]
        raw, sm, *sems = refs[12:]
        plan = gathers(n, (wp_src, wpt_src, sm_src), (wp_far, wpt_far, sm), layout, sems)
    else:
        sm_src = refs[3]
        xr_ref, cotr_ref, wd_ref, wk_ref = refs[4:8]
        raw, sm = refs[8:]
        plan = None
    t, d = x_ref.shape[1:]
    nch = d // 128
    b = pl.program_id(0)
    s = s_ref[b]
    end = pl.num_programs(0) - 1
    point(b == 0, lambda: greet(n), plan, 0)
    for src, dst in ((cot_ref, cotr_ref), (x_ref, xr_ref)):
        for j in range(nch):
            col = pl.ds(j * 128, 128)
            raw[0:t, :] = src[0, :, col].astype(F32)
            raw[t : t + 128, :] = src[0, 0:128, col].astype(F32)
            dst[0, :, col] = raw[pl.ds(s, t), :].astype(BF16)

    point(b == 0, None, plan, 1)

    @pl.when(b == end)
    def _():
        if plan is not None:
            for i in range(2, plan.ticks):
                plan.tick(i)
            unpack_small(sm.reshape(d, 128), wd_ref, wk_ref)
        else:
            unpack_small(sm_src, wd_ref, wk_ref)


def stage_front(n, s, x, cot, small, wp, wpt, own):
    mb, t, d = x.shape
    half = d // 2
    sds = jax.ShapeDtypeStruct
    layout = front_layout(d, half) if own else []
    more = [wp, wpt] if own else []
    out = [((mb, t, d), BF16)] * 2
    return pl.pallas_call(
        partial(kernel_front, n, layout),
        out_shape=[sds(*o) for o in out] + [sds((24, d), F32), sds((72, half), BF16)] + gathered(n, more),
        grid_spec=pltpu.PrefetchScalarGridSpec(
            num_scalar_prefetch=1,
            grid=(mb,),
            in_specs=[per_block(t, d), per_block(t, d), ANY if own else whole(*small.shape)] + [ANY] * len(more),
            out_specs=[per_block(t, d)] * 2 + [whole(24, d), whole(72, half)] + [ANY] * len(more),
            scratch_shapes=[
                pltpu.VMEM((t + 128, 128), F32),
                pltpu.VMEM((2,) * (n.bit_length() - 1) + (PIECE, 128) if own else (8, 128), F32),
            ]
            + (gather_sems(n, layout) if own else []),
        ),
        compiler_params=params(1, 0 if own else None),
        name="front",
    )(s, x, cot, small, *more)


A_SPOTS = [block + at for block in (0.0, 16.5) for at in (0.0, 3.0, 6.0, 7.4, 8.6, 11.0, 12.3, 13.6)]


def kernel_a(n, layout, count, *refs):
    seg_ref, xr_ref, wp_ref, wd_ref, wpt_ref, wk_ref = refs[:6]
    srcs, refs = refs[6 : 6 + count], refs[6 + count :]
    q_ref, k_ref, v_ref, c_ref, depth_ref, span_ref, mixed_ref, taps_ref, conv_ref = refs[:9]
    dsts, refs = refs[9 : 9 + count], refs[9 + count :]
    xs, segb, vt, cs, lt, e_ref, texp, *sems = refs
    plan = gathers(n, srcs, dsts, layout, sems, A_SPOTS) if count else None
    t, d = xr_ref.shape[1:]
    half = d // 2
    nch = d // 128
    b = pl.program_id(0)
    end = pl.num_programs(0) - 1
    if plan is not None:
        @pl.when(b == 0)
        def _():
            greet(n)

    def spot(i, loop, every):
        for at in range(3):
            for block in range(2):
                point((b == block) & (i == at * every), None, plan, 8 * block + 2 + 3 * loop + at)

    def early(at):
        for block in range(2):
            point(b == block, None, plan, 8 * block + at)

    early(0)

    @pl.when(b == 0)
    def _():
        fill_expander(e_ref)
        cs[:, 0:8, :] = jnp.zeros((nch // 2, 8, 128), F32)
        cs[:, t + 8 : t + 16, :] = jnp.zeros((nch // 2, 8, 128), F32)
        xs[:, 0:8, :] = jnp.zeros((nch, 8, 128), F32)
        xs[:, t + 8 : t + 16, :] = jnp.zeros((nch, 8, 128), F32)

    fill_segments(seg_ref, segb, vt)
    for j in range(nch):
        xs[j, 8 : t + 8, :] = xr_ref[0, :, pl.ds(j * 128, 128)].astype(F32)

    def depth_tile(r0, masked):
        masks = mask_rows(segb, r0, 128) if masked else None
        for j in range(nch):
            acc = None
            for o in range(KERNEL):
                part = xs[j, pl.ds(8 + r0 + o - REACH, 128), :]
                w = wd_ref[o : o + 1, pl.ds(j * 128, 128)]
                part = part * (masks[o] * w) if masked else part * w
                acc = part if acc is None else acc + part
            depth_ref[0, pl.ds(r0, 128), pl.ds(j * 128, 128)] = acc.astype(BF16)

    masked_tiles(t, depth_tile, lambda: early(1))

    def proj_tile(i, carry):
        spot(i, 0, 1)
        r0 = pl.multiple_of(i * 384, 128)
        rows = pl.ds(r0, 384)
        merged = mm(xr_ref[0, rows, :], wp_ref[...]).astype(BF16)
        q = merged[:, 0:half]
        q_ref[0, rows, :] = q
        k_ref[0, rows, :] = merged[:, half : 2 * half]
        v_ref[0, rows, :] = merged[:, 2 * half : 3 * half]
        c = merged[:, 3 * half :]
        c_ref[0, rows, :] = c
        for j in range(nch // 2):
            cs[j, pl.ds(8 + r0, 384), :] = c[:, j * 128 : (j + 1) * 128].astype(F32)
        span = mm(depth_ref[0, rows, :], wpt_ref[...])
        span_ref[0, rows, :] = span
        mixed = (span * q.astype(F32)).astype(BF16)
        mixed_ref[0, rows, :] = mixed
        lt[:, rows] = mm(wk_ref[...], mixed, NT)
        return carry

    lax.fori_loop(0, t // 384, proj_tile, 0)

    logits = [lt[o * 8 : o * 8 + 8, :] for o in range(KERNEL)]
    top = logits[0]
    for o in range(1, KERNEL):
        top = jnp.maximum(top, logits[o])
    exps = [jnp.exp(v - top) for v in logits]
    total = exps[0]
    for o in range(1, KERNEL):
        total = total + exps[o]
    inv = 1.0 / total
    for o in range(KERNEL):
        tap = exps[o] * inv
        taps_ref[0, o * 8 : o * 8 + 8, :] = tap
        lt[o * 8 : o * 8 + 8, :] = tap * vt[o]

    def conv_tile(i, carry):
        spot(i, 1, 3)
        r0 = pl.multiple_of(i * 128, 128)
        rows = pl.ds(r0, 128)
        texp[...] = expand_taps(lt[:, rows], e_ref)
        for j in range(nch // 2):
            acc = None
            for o in range(KERNEL):
                part = cs[j, pl.ds(8 + r0 + o - REACH, 128), :] * texp[:, o * half + j * 128 : o * half + (j + 1) * 128]
                acc = part if acc is None else acc + part
            conv_ref[0, rows, pl.ds(j * 128, 128)] = acc.astype(BF16)
        return carry

    lax.fori_loop(0, t // 128, conv_tile, 0)
    point(b == end, None, plan, len(A_SPOTS))


def whole(*shape):
    return pl.BlockSpec(shape, lambda *_: (0,) * len(shape), pipeline_mode=pl.Buffered(1))


def per_block(*shape):
    return pl.BlockSpec((1,) + shape, lambda b, *_: (b,) + (0,) * len(shape))


def params(n, cid=None):
    more = {} if cid is None else {"collective_id": cid, "has_side_effects": True}
    return pltpu.CompilerParams(dimension_semantics=("arbitrary",) * n, vmem_limit_bytes=VMEM_CAP, **more)


def point(when, first, plan, s):
    if plan is None or not plan.plan[s]:
        return

    @pl.when(when)
    def _():
        if first is not None:
            first()
        plan.tick(s)


def stage_a(n, segr, xr, wp, wd, wpt, wk, more):
    mb, t, d = xr.shape
    half = d // 2
    sds = jax.ShapeDtypeStruct
    out = [
        ((t, half), BF16), ((t, half), BF16), ((t, half), BF16), ((t, half), BF16), ((t, d), BF16),
        ((t, half), F32), ((t, half), BF16), ((72, t), F32), ((t, half), BF16),
    ]
    layout, far = [], []
    if more:
        hid = more[1].shape[1] // 2
        layout = [(0, p) for p in pieces(d, 2)] + [(1, p) for p in pieces(hid, 2)]
        layout = [layout[i] for i in (2, 3, 0, 1)]
        far = [more[0], jax.ShapeDtypeStruct((more[1].shape[0], hid), BF16)]
    return pl.pallas_call(
        partial(kernel_a, n, layout, len(more)),
        out_shape=[sds((mb,) + sh, dt) for sh, dt in out] + gathered(n, far),
        grid=(mb,),
        in_specs=[
            pl.BlockSpec((pl.Squeezed(), 1, t), lambda b: (b, 0, 0)),
            per_block(t, d), whole(*wp.shape), whole(*wd.shape), whole(*wpt.shape), whole(*wk.shape),
        ]
        + [ANY] * len(more),
        out_specs=[per_block(*sh) for sh, _ in out] + [ANY] * len(more),
        scratch_shapes=[
            pltpu.VMEM((d // 128, t + 16, 128), F32),
            pltpu.VMEM((t + 16, 128), F32),
            pltpu.VMEM((KERNEL, 8, t), F32),
            pltpu.VMEM((half // 128, t + 16, 128), F32),
            pltpu.VMEM((72, t), F32),
            pltpu.VMEM((144, KERNEL * half), BF16),
            pltpu.VMEM((128, KERNEL * half), F32),
        ]
        + (gather_sems(n, layout) if more else []),
        compiler_params=params(1, 2 if more else None),
        name="mix_fwd",
    )(segr, xr, wp, wd, wpt, wk, *more)


QT = 256


def seg_codes(segb, first):
    lane = lanes(segb.shape) - first
    hot = segb == lane.astype(F32)
    inside = (lane >= 0) & (lane < 24)
    return jnp.where(hot & inside, 1.0, 0.0), jnp.where(inside & ~hot, -1e30, 0.0)


def tile_points(n, plan, spots, i, tiles):
    if plan is None:
        return
    step = pl.program_id(0) * pl.num_programs(1) + pl.program_id(1)
    for t in range(len(spots)):
        point((step == t // tiles) & (i == t % tiles), (lambda: greet(n)) if t == 0 else None, plan, t)


def end_points(plan):
    if plan is None:
        return
    last = (pl.program_id(0) == pl.num_programs(0) - 1) & (pl.program_id(1) == pl.num_programs(1) - 1)
    point(last, None, plan, plan.ticks - 1)


B_SPOTS = [1.46 * i for i in range(24)]


def kernel_b(n, layout, count, *refs):
    segt_ref, q_ref, k_ref, v_ref = refs[:4]
    srcs, (ctx_ref, lse_ref) = refs[4 : 4 + count], refs[4 + count : 6 + count]
    dsts, sems = refs[6 + count : 6 + 2 * count], refs[6 + 2 * count :]
    plan = gathers(n, srcs, dsts, layout, sems, B_SPOTS) if count else None
    t = q_ref.shape[1]
    tail = t - SEG_MOST
    low_half = lanes((1, 128)) < 64

    def finish(rows, outs, tops):
        both = jnp.where(low_half, outs[0], outs[1])
        sums = jnp.where(low_half, outs[1], outs[0])
        ctx_ref[0, rows, :] = (both / pltpu.roll(sums, 64, 1)).astype(BF16)
        lse_ref[0, rows, :] = jnp.where(low_half, tops[1], tops[0]) + jnp.log(sums)

    def one(q, k, v):
        scores = mm(q, k, NT)
        top = jnp.max(scores, -1, keepdims=True)
        return mm(jnp.exp(scores - top).astype(BF16), v), top

    k = k_ref[0, 0:SEG_MOST, :]
    v = v_ref[0, 0:SEG_MOST, :]
    one_b = jnp.ones((), BF16)
    vs = (jnp.where(low_half, v, one_b), jnp.where(low_half, one_b, v))

    def tile(i, carry):
        tile_points(n, plan, B_SPOTS, i, SEG_MOST // QT)
        rows = pl.ds(pl.multiple_of(i * QT, QT), QT)
        q = q_ref[0, rows, :] * 0.125
        zero = jnp.zeros((), BF16)
        outs = [one(jnp.where(low_half, q, zero), k, vs[0]), one(jnp.where(low_half, zero, q), k, vs[1])]
        finish(rows, [o[0] for o in outs], [o[1] for o in outs])
        return carry

    lax.fori_loop(0, SEG_MOST // QT, tile, 0)
    rows = pl.ds(SEG_MOST, tail)
    q = q_ref[0, rows, :] * 0.125
    kt = k_ref[0, rows, :]
    vt = v_ref[0, rows, :]
    segb = jnp.broadcast_to(segt_ref[...], (128, tail)).T
    outs = []
    for h in range(2):
        hot, pen = seg_codes(segb, 64 - 64 * h)
        mine = low_half if h == 0 else ~low_half
        outs.append(
            one(
                jnp.where(mine, q, pen.astype(BF16)),
                jnp.where(mine, kt, hot.astype(BF16)),
                jnp.where(mine, vt, one_b),
            )
        )
    finish(rows, [o[0] for o in outs], [o[1] for o in outs])
    end_points(plan)


def pair(t):
    return pl.BlockSpec((1, t, 128), lambda b, j: (b, 0, j))


def seg_tail(tail):
    return pl.BlockSpec((pl.Squeezed(), 1, tail), lambda b, *_: (b, 0, SEG_MOST // tail))


def stage_b(n, segt, q, k, v, more):
    mb, t, half = q.shape
    sds = jax.ShapeDtypeStruct
    layout, far = [], []
    if more:
        hid = more[0].shape[1] // 2
        cols = pieces(hid, 2)
        wide = [(0, (ALL, pl.ds(hid + i * (hid // 2), hid // 2)), p) for i, p in enumerate(cols)]
        tall = [(1, p) for p in pieces(more[1].shape[0], 4, True)]
        layout = tall[:2] + wide + tall[2:]
        far = [jax.ShapeDtypeStruct((more[0].shape[0], hid), BF16), more[1]]
    return pl.pallas_call(
        partial(kernel_b, n, layout, len(more)),
        out_shape=[sds((mb, t, half), BF16), sds((mb, t, half), F32)] + gathered(n, far),
        grid=(mb, half // 128),
        in_specs=[seg_tail(t - SEG_MOST), pair(t), pair(t), pair(t)] + [ANY] * len(more),
        out_specs=[pair(t), pair(t)] + [ANY] * len(more),
        scratch_shapes=gather_sems(n, layout) if more else [],
        compiler_params=params(2, 3 if more else None),
        name="att_fwd",
    )(segt, q, k, v, *more)


ROWS = 384


def norm_fwd(values):
    centre = values - jnp.mean(values, -1, keepdims=True)
    inv_std = lax.rsqrt(jnp.mean(centre * centre, -1, keepdims=True) + NORM_EPS)
    return centre * inv_std, inv_std


def norm_back(grad, normed, inv_std):
    one = jnp.mean(grad, -1, keepdims=True)
    two = jnp.mean(grad * normed, -1, keepdims=True)
    return inv_std * (grad - one - normed * two)


def gelu_both(x):
    cdf = 0.5 + 0.5 * lax.erf(x * 0.7071067811865476)
    bell = jnp.exp(x * (x * -0.5))
    return x * cdf, cdf + x * (bell * 0.3989422804014327)


def col_sum(v):
    return jnp.sum(v, 0, keepdims=True)


def kernel_c(
    ctx_ref, conv_ref, x_ref, cot_ref, wo_ref, wia_ref, wib_ref, wdn_ref, ln_ref,
    out_ref, dres_ref, dctx_ref, dconv_ref, gf_ref, gs_ref,
    joined, act, slope, dinner, go_ref, gi_ref, gd_ref, wi_ref,
):
    first = (pl.program_id(0) == 0) & (pl.program_id(1) == 0)
    last = (pl.program_id(0) == pl.num_programs(0) - 1) & (pl.program_id(1) == pl.num_programs(1) - 1)
    d = x_ref.shape[-1]
    half = d // 2
    hid = wi_ref.shape[1]

    @pl.when(first)
    def _():
        wi_ref[:, 0 : hid // 2] = wia_ref[...]
        wi_ref[:, hid // 2 :] = wib_ref[...]
        go_ref[...] = jnp.zeros_like(go_ref)
        gi_ref[...] = jnp.zeros_like(gi_ref)
        gd_ref[...] = jnp.zeros_like(gd_ref)
        gs_ref[...] = jnp.zeros_like(gs_ref)

    joined[:, 0:half] = ctx_ref[0]
    joined[:, half:] = conv_ref[0]
    gain1, shift1, gain2, shift2 = (ln_ref[16 + i : 17 + i, :] for i in range(4))
    normed1, inv1 = norm_fwd(mm(joined[...], wo_ref[...]) + x_ref[0].astype(F32))
    hidden = normed1 * gain1 + shift1
    hidden_low = hidden.astype(BF16)
    outers = []
    for g in range(2):
        cols = pl.ds(g * hid, hid)
        inner = mm(hidden_low[:, g * half : (g + 1) * half], wi_ref[g * half : (g + 1) * half, :])
        value, deriv = gelu_both(inner)
        act[:, cols] = value.astype(BF16)
        slope[:, cols] = deriv
        outers.append(mm(act[:, cols], wdn_ref[g * hid : (g + 1) * hid, :]))
    normed2, inv2 = norm_fwd(jnp.concatenate(outers, 1) + hidden)
    out_ref[0] = (normed2 * gain2 + shift2).astype(BF16)
    cot = cot_ref[0].astype(F32)
    gs_ref[2:3, :] += col_sum(cot * normed2)
    gs_ref[3:4, :] += col_sum(cot)
    d_sum = norm_back(cot * gain2, normed2, inv2)
    d_outer = d_sum.astype(BF16)
    d_hid = []
    for g in range(2):
        cols = pl.ds(g * hid, hid)
        mine = d_outer[:, g * half : (g + 1) * half]
        d_act = mm(mine, wdn_ref[g * hid : (g + 1) * hid, :], NT)
        gd_ref[:, cols] += mm(mine, act[:, cols], TN)
        dinner[:, cols] = (d_act * slope[:, cols]).astype(BF16)
        d_hid.append(mm(dinner[:, cols], wi_ref[g * half : (g + 1) * half, :], NT))
        gi_ref[g * half : (g + 1) * half, :] += mm(hidden_low[:, g * half : (g + 1) * half], dinner[:, cols], TN)
    d_hidden = jnp.concatenate(d_hid, 1) + d_sum
    gs_ref[0:1, :] += col_sum(d_hidden * normed1)
    gs_ref[1:2, :] += col_sum(d_hidden)
    d_res = norm_back(d_hidden * gain1, normed1, inv1)
    dres_ref[0] = d_res
    d_attn = d_res.astype(BF16)
    d_joined = mm(d_attn, wo_ref[...], NT)
    dctx_ref[0] = d_joined[:, 0:half].astype(BF16)
    dconv_ref[0] = d_joined[:, half:]
    go_ref[...] += mm(joined[...], d_attn, TN)

    @pl.when(last)
    def _():
        n, _, _ = gf_ref.shape
        rows = d // n
        tall = 2 * hid // n

        def emit(p, c):
            at = pl.ds(pl.multiple_of(p * rows, 8), rows)
            gi = gi_ref[at, :]
            go = go_ref[at, :]
            parts = [gi[:, j * half : (j + 1) * half] for j in range(hid // half)] + [go[:, 0:half], go[:, half:]]
            gf_ref[p, tall : tall + rows * len(parts), :] = jnp.concatenate(parts, 0).astype(BF16)
            return c

        lax.fori_loop(0, n, emit, 0)

        step = 4
        wide = step * tall

        def emit_down(i, c):
            block = gd_ref[:, pl.ds(pl.multiple_of(i * wide, 128), wide)].T.astype(BF16)
            for j in range(step):
                gf_ref[i * step + j, 0:tall, :] = block[j * tall : (j + 1) * tall, :]
            return c

        lax.fori_loop(0, n // step, emit_down, 0)


def stage_c(n, ctx, conv, x, cot, wo, wi_a, wi_b, wdn, ln):
    mb, t, d = x.shape
    half = d // 2
    hid = 2 * wi_a.shape[1]
    packed = (d * d + d * hid + 2 * hid * half) // (n * half)
    sds = jax.ShapeDtypeStruct

    def tile(cols):
        return pl.BlockSpec((1, ROWS, cols), lambda b, i: (b, i, 0))

    return pl.pallas_call(
        kernel_c,
        out_shape=[
            sds((mb, t, d), BF16), sds((mb, t, d), F32), sds((mb, t, half), BF16), sds((mb, t, half), F32),
            sds((n, packed, half), BF16), sds((8, d), F32),
        ],
        grid=(mb, t // ROWS),
        in_specs=[
            tile(half), tile(half), tile(d), tile(d),
            whole(*wo.shape), whole(*wi_a.shape), whole(*wi_b.shape), whole(*wdn.shape), whole(*ln.shape),
        ],
        out_specs=[
            tile(d), tile(d), tile(half), tile(half),
            whole(n, packed, half), whole(8, d),
        ],
        scratch_shapes=[
            pltpu.VMEM((ROWS, d), BF16),
            pltpu.VMEM((ROWS, 2 * hid), BF16),
            pltpu.VMEM((ROWS, 2 * hid), F32),
            pltpu.VMEM((ROWS, 2 * hid), BF16),
            pltpu.VMEM((d, d), F32),
            pltpu.VMEM((d, hid), F32),
            pltpu.VMEM((half, 2 * hid), F32),
            pltpu.VMEM((d, hid), BF16),
        ],
        compiler_params=params(2),
        name="ffn",
    )(ctx, conv, x, cot, wo, wi_a, wi_b, wdn, ln)


KT = 256
D_SPOTS = [1.98 * i for i in range(24)]


def kernel_d(n, cuts, *refs):
    count = 1 if cuts else 0
    segt_ref, q_ref, k_ref, v_ref, ctx_ref, lse_ref, do_ref = refs[:7]
    srcs, refs = refs[7 : 7 + count], refs[7 + count :]
    dq_ref, dk_ref, dv_ref = refs[:3]
    outs, refs = refs[3 : 3 + count], refs[3 + count :]
    qa, da, dqt, *rest = refs
    plan = scatters(n, cuts, srcs, outs, rest, D_SPOTS) if count else None
    t = q_ref.shape[1]
    tail = t - SEG_MOST
    lane = lanes((1, 128))
    low_half = lane < 64
    one_b = jnp.ones((), BF16)
    zero_b = jnp.zeros((), BF16)

    r = lax.broadcasted_iota(jnp.int32, (256, 128), 0) % 128
    c = lax.broadcasted_iota(jnp.int32, (256, 128), 1)
    swap = jnp.where((r < 64) != (c < 64), 1.0, 0.0).astype(BF16)
    prod = do_ref[0].astype(F32) * ctx_ref[0].astype(F32)
    hi, lo = split2(prod)
    dsum = mm(jnp.concatenate([hi, lo], 1), swap)
    q8 = q_ref[0] * 0.125
    do = do_ref[0]
    for stat, src, dst in ((lse_ref[0], q8, qa), (dsum, do, da)):
        pieces = split3(-stat)
        code = jnp.where(
            (lane & 63) == 0, pieces[0], jnp.where((lane & 63) == 1, pieces[1], jnp.where((lane & 63) == 2, pieces[2], zero_b))
        )
        dst[0] = jnp.where(low_half, src, code)
        dst[1] = jnp.where(low_half, code, src)

    def run(key_rows, q_rows, h, codes):
        mark = (lane & 63) < 3
        mine = low_half if h == 0 else ~low_half
        k = k_ref[0, key_rows, :]
        v = v_ref[0, key_rows, :]
        ka = jnp.where(mine, k, jnp.where(mark, one_b, zero_b))
        va = jnp.where(mine, v, jnp.where(mark, one_b, zero_b))
        qh = qa[h, q_rows, :]
        if codes is not None:
            hot, pen = codes
            qh = qh + pen
            ka = ka + hot
        p = jnp.exp(mm(ka, qh, NT))
        dp = mm(va, da[h, q_rows, :], NT)
        ds = (p * dp).astype(BF16)
        dv = mm(p.astype(BF16), do_ref[0, q_rows, :])
        dk = mm(ds, q_ref[0, q_rows, :] * 0.125)
        return ds, dk, dv, k

    main = pl.ds(0, SEG_MOST)

    def tile(i, carry):
        tile_points(n, plan, D_SPOTS, i, SEG_MOST // KT)
        rows = pl.ds(pl.multiple_of(i * KT, KT), KT)
        halves = []
        for h in range(2):
            ds, dk, dv, k = run(rows, main, h, None)
            part = mm(k[:, 64 * h : 64 * h + 64], ds, TN)
            dqt[64 * h : 64 * h + 64, :] = jnp.where(i == 0, part, dqt[64 * h : 64 * h + 64, :] + part)
            halves.append((dk, dv))
        dk_ref[0, rows, :] = jnp.where(low_half, halves[0][0], halves[1][0]).astype(BF16)
        dv_ref[0, rows, :] = jnp.where(low_half, halves[0][1], halves[1][1]).astype(BF16)
        return carry

    dqt[...] = jnp.zeros_like(dqt)
    lax.fori_loop(0, SEG_MOST // KT, tile, 0)
    dq_ref[0, main, :] = dqt[...].T * 0.125

    rows = pl.ds(SEG_MOST, tail)
    segb = jnp.broadcast_to(segt_ref[...], (128, tail)).T
    halves = []
    for h in range(2):
        hot, pen = seg_codes(segb, 64 - 64 * h + 8)
        ds, dk, dv, k = run(rows, rows, h, (hot.astype(BF16), pen.astype(BF16)))
        halves.append((dk, dv, mm(ds, k, TN)))
    for ref, i in ((dk_ref, 0), (dv_ref, 1)):
        ref[0, rows, :] = jnp.where(low_half, halves[0][i], halves[1][i]).astype(BF16)
    dq_ref[0, rows, :] = jnp.where(low_half, halves[0][2], halves[1][2]) * 0.125
    end_points(plan)


def stage_d(n, segt, q, k, v, ctx, lse, dctx, more):
    mb, t, half = q.shape
    cuts = scatter_cuts(more, 4)
    sds = jax.ShapeDtypeStruct
    return pl.pallas_call(
        partial(kernel_d, n, cuts),
        out_shape=[sds((mb, t, half), F32), sds((mb, t, half), BF16), sds((mb, t, half), BF16)]
        + [sds(w.shape[1:], F32) for w in more],
        grid=(mb, half // 128),
        in_specs=[seg_tail(t - SEG_MOST)] + [pair(t)] * 6 + [ANY] * len(more),
        out_specs=[pair(t)] * 3 + [whole(*w.shape[1:]) for w in more],
        scratch_shapes=[
            pltpu.VMEM((2, t, 128), BF16), pltpu.VMEM((2, t, 128), BF16), pltpu.VMEM((128, SEG_MOST), F32),
        ]
        + (scatter_scratch(n, cuts, more) if more else []),
        compiler_params=params(2, 4 if more else None),
        name="att_bwd",
    )(segt, q, k, v, ctx, lse, dctx, *more)


def kernel_e(
    s_ref, seg_ref, c_far, dconv_far, taps_far, mixed_far, q_far, dq_far, span_far, dk_far, dv_far, depth_far,
    x_far, dres_far, outr_far, wp_ref, wd_ref, wpt_ref, wk_ref, gs_ref,
    gx_far, out_far, gm_ref,
    pad, xs, segb, vt, dcs, dts, e_ref, er_ref, texp, dlt, rt, dm, dl, gacc, gp_ref, gpt_ref, gk_ref, small,
    c_ref, dconv_ref, taps_ref, mixed_ref, q_ref, dq_ref, span_ref, dk_ref, dv_ref, depth_ref,
    x_ref, dres_ref, out_ref_in, gx_ref, out_ref, in_sem, out_sem,
):
    t, d = x_ref.shape[1:]
    far = (
        c_far, dconv_far, taps_far, mixed_far, q_far, dq_far, span_far, dk_far, dv_far, depth_far,
        x_far, dres_far, outr_far,
    )
    near = (
        c_ref, dconv_ref, taps_ref, mixed_ref, q_ref, dq_ref, span_ref, dk_ref, dv_ref, depth_ref,
        x_ref, dres_ref, out_ref_in,
    )

    def fetch(i, block):
        return pltpu.make_async_copy(far[i].at[pl.ds(block, 1)], near[i], in_sem.at[i])

    def arrived(*which):
        for i in which:
            fetch(i, b).wait()

    def done_with(*which):
        @pl.when(b + 1 < pl.num_programs(0))
        def _():
            for i in which:
                fetch(i, b + 1).start()

    def put_back(j, block):
        cols = pl.ds(j * 128, 128)
        return [
            pltpu.make_async_copy(src.at[:, :, cols], dst.at[pl.ds(block, 1), :, cols], out_sem.at[k, j])
            for k, (src, dst) in enumerate(((gx_ref, gx_far), (out_ref, out_far)))
        ]

    half = d // 2
    nch = d // 128
    b = pl.program_id(0)
    s = s_ref[b]

    @pl.when(b == 0)
    def _():
        for i in range(len(far)):
            fetch(i, 0).start()
        fill_expander(e_ref)
        col = lanes((128, 128))
        upper = jnp.where(lax.broadcasted_iota(jnp.int32, (128, 128), 0) >= 64, 1, 0)
        for o in range(KERNEL):
            for j in range(half // 128):
                one = jnp.where(col == upper + (o * 8 + 2 * j), 1.0, 0.0).astype(BF16)
                er_ref[pl.ds(o * half + j * 128, 128), :] = one
        for ref in (xs, dts, dcs):
            n = ref.shape[0]
            ref[:, 0:8, :] = jnp.zeros((n, 8, 128), F32)
            ref[:, t + 8 : t + 16, :] = jnp.zeros((n, 8, 128), F32)
        gp_ref[...] = jnp.zeros_like(gp_ref)
        gpt_ref[...] = jnp.zeros_like(gpt_ref)
        gk_ref[...] = jnp.zeros_like(gk_ref)
        gacc[...] = jnp.zeros_like(gacc)

    fill_segments(seg_ref, segb, vt)
    arrived(0, 1)
    cw = xs
    for j in range(nch // 2):
        cols = pl.ds(j * 128, 128)
        cw[j, 8 : t + 8, :] = c_ref[0, :, cols].astype(F32)
        dcs[j, 8 : t + 8, :] = dconv_ref[0, :, cols]
    done_with(0, 1)

    def dtap_tile(i, carry):
        r0 = pl.multiple_of(i * 128, 128)
        rows = pl.ds(r0, 128)
        acc = None
        for o in range(KERNEL):
            prods = [
                (cw[j, pl.ds(8 + r0 + o - REACH, 128), :] * dcs[j, pl.ds(8 + r0, 128), :]).astype(BF16)
                for j in range(nch // 2)
            ]
            part = mm(jnp.concatenate(prods, 1), er_ref[o * half : (o + 1) * half, :])
            acc = part if acc is None else acc + part
        dlt[:, rows] = acc.T[0:72, :]
        return carry

    lax.fori_loop(0, t // 128, dtap_tile, 0)

    arrived(2)
    taps = [taps_ref[0, o * 8 : o * 8 + 8, :] for o in range(KERNEL)]
    dtaps = [dlt[o * 8 : o * 8 + 8, :] * vt[o] for o in range(KERNEL)]
    mean = taps[0] * dtaps[0]
    for o in range(1, KERNEL):
        mean = mean + taps[o] * dtaps[o]
    for o in range(KERNEL):
        dl[o * 8 : o * 8 + 8, :] = taps[o] * (dtaps[o] - mean)
        tv = taps[o] * vt[o]
        move = (o - REACH) % t
        rt[o * 8 : o * 8 + 8, :] = pltpu.roll(tv, move, 1) if move else tv

    done_with(2)
    arrived(*range(3, 10))

    def point_tile(i, carry):
        r0 = pl.multiple_of(i * 384, 128)
        rows = pl.ds(r0, 384)
        dlog = dl[:, rows].astype(BF16)
        d_mixed = mm(dlog, wk_ref[...], TN)
        gk_ref[...] += mm(dlog, mixed_ref[0, rows, :])
        d_span = (d_mixed * q_ref[0, rows, :].astype(F32)).astype(BF16)
        dm[rows, 0:half] = (dq_ref[0, rows, :] + d_mixed * span_ref[0, rows, :]).astype(BF16)
        dm[rows, half : 2 * half] = dk_ref[0, rows, :]
        dm[rows, 2 * half : 3 * half] = dv_ref[0, rows, :]
        gpt_ref[...] += mm(depth_ref[0, rows, :], d_span, TN)
        d_depth = mm(d_span, wpt_ref[...], NT)
        for j in range(nch):
            dts[j, pl.ds(8 + r0, 384), :] = d_depth[:, j * 128 : (j + 1) * 128]
        return carry

    lax.fori_loop(0, t // 384, point_tile, 0)
    done_with(*range(3, 10))

    def dc_tile(i, carry):
        r0 = pl.multiple_of(i * 128, 128)
        rows = pl.ds(r0, 128)
        texp[...] = expand_taps(rt[:, rows], e_ref)
        for j in range(nch // 2):
            acc = None
            for o in range(KERNEL):
                part = dcs[j, pl.ds(8 + r0 - o + REACH, 128), :] * texp[:, o * half + j * 128 : o * half + (j + 1) * 128]
                acc = part if acc is None else acc + part
            dm[rows, pl.ds(3 * half + j * 128, 128)] = acc.astype(BF16)
        return carry

    lax.fori_loop(0, t // 128, dc_tile, 0)

    arrived(10, 11)
    for j in range(nch):
        xs[j, 8 : t + 8, :] = x_ref[0, :, pl.ds(j * 128, 128)].astype(F32)

    def proj_tile(i, carry):
        r0 = pl.multiple_of(i * 384, 128)
        rows = pl.ds(r0, 384)
        gp_ref[...] += mm(x_ref[0, rows, :], dm[rows, :], TN)
        gx = mm(dm[rows, :], wp_ref[...], NT) + dres_ref[0, rows, :]
        for j in range(nch):
            pad[j, pl.ds(r0, 384), :] = gx[:, j * 128 : (j + 1) * 128]
        return carry

    lax.fori_loop(0, t // 384, proj_tile, 0)

    done_with(10, 11)

    def depth_tile(r0, masked):
        masks = mask_rows(segb, r0, 128) if masked else None
        for j in range(nch):
            acc = pad[j, pl.ds(r0, 128), :]
            own = dts[j, pl.ds(8 + r0, 128), :]
            for o in range(KERNEL):
                w = wd_ref[KERNEL - 1 - o : KERNEL - o, pl.ds(j * 128, 128)]
                near = dts[j, pl.ds(8 + r0 + o - REACH, 128), :]
                xw = xs[j, pl.ds(8 + r0 + o - REACH, 128), :]
                if masked:
                    near = near * masks[o]
                    xw = xw * masks[o]
                acc = acc + near * w
                term = (own * xw).reshape(16, 8, 128)
                gacc[o, :, pl.ds(j * 128, 128)] += jnp.sum(term, 0)
            pad[j, pl.ds(r0, 128), :] = acc

    masked_tiles(t, depth_tile)

    arrived(12)

    @pl.when(b > 0)
    def _():
        for j in range(nch):
            for copy in put_back(j, b - 1):
                copy.wait()

    for j in range(nch):
        cols = pl.ds(j * 128, 128)
        pad[j, pl.ds(t, 128), :] = pad[j, 0:128, :]
        back = t - s
        first = pl.ds(back, 128)
        gx_ref[0, :, cols] = xs[j, 8 : t + 8, :]
        xs[j, 0:128, :] = pad[j, first, :]
        gx_ref[0, 0:128, cols] = xs[j, 0:128, :]
        gx_ref[0, 128:, cols] = pad[j, pl.ds(128 - s, t - 128), :]
        pad[j, 0:t, :] = out_ref_in[0, :, cols].astype(F32)
        pad[j, pl.ds(t, 128), :] = pad[j, 0:128, :]
        out_ref[0, 0:128, cols] = pad[j, first, :].astype(BF16)
        out_ref[0, 128:, cols] = pad[j, pl.ds(128 - s, t - 128), :].astype(BF16)
        for copy in put_back(j, b):
            copy.start()
    done_with(12)

    @pl.when(b == pl.num_programs(0) - 1)
    def _():
        n = gm_ref.shape[0]
        rows = d // n
        small[...] = jnp.zeros_like(small)
        for o in range(KERNEL):
            small[o : o + 1, :] = jnp.sum(gacc[o], 0, keepdims=True)
        small[16:24, :] = gs_ref[...]
        row = lax.broadcasted_iota(jnp.int32, (128, 72), 0)
        col = lax.broadcasted_iota(jnp.int32, (128, 72), 1)
        order = jnp.where((row < HEADS * KERNEL) & (row % KERNEL * 8 + row // KERNEL == col), 1.0, 0.0).astype(BF16)
        gk = mm(order, gk_ref[...].astype(BF16)).astype(BF16)
        gk = mm(gk, piece_rows(d), NT)
        for j in range(nch):
            cols = pl.ds(j * 128, 128)
            pad[0, cols, :] = small[:, cols].T
            pad[1, cols, :] = gk[:, j * 128 : (j + 1) * 128].T

        def emit(p, c):
            at = pl.ds(pl.multiple_of(p * rows, 8), rows)
            gp = gp_ref[at, :]
            parts = [gp[:, j * half : (j + 1) * half] for j in range(gp.shape[1] // half)] + [gpt_ref[at, :]]
            parts.append(jnp.concatenate([pad[0, at, :], pad[1, at, :], jnp.zeros((rows, half - 256), F32)], 1))
            gm_ref[p] = jnp.concatenate(parts, 0).astype(BF16)
            return c

        lax.fori_loop(0, n, emit, 0)
        for j in range(nch):
            for copy in put_back(j, b):
                copy.wait()


def stage_e(n, s, segr, x, out_r, dres, dconv, dq, dk, dv, q, c, depth, span, mixed, taps, wp, wd, wpt, wk, gs):
    mb, t, d = x.shape
    half = d // 2
    packed = (d * 2 * d + d * half) // (n * half) + d // n
    sds = jax.ShapeDtypeStruct

    blocks = (c, dconv, taps, mixed, q, dq, span, dk, dv, depth, x, dres, out_r)
    return pl.pallas_call(
        kernel_e,
        out_shape=[
            sds((mb, t, d), F32), sds((mb, t, d), BF16), sds((n, packed, half), BF16),
        ],
        grid_spec=pltpu.PrefetchScalarGridSpec(
            num_scalar_prefetch=1,
            grid=(mb,),
            in_specs=[pl.BlockSpec((pl.Squeezed(), 1, t), lambda b, *_: (b, 0, 0))]
            + [ANY] * len(blocks)
            + [whole(*w.shape) for w in (wp, wd, wpt, wk, gs)],
            out_specs=[ANY, ANY, whole(n, packed, half)],
            scratch_shapes=[
                pltpu.VMEM((d // 128, t + 128, 128), F32),
                pltpu.VMEM((d // 128, t + 16, 128), F32),
                pltpu.VMEM((t + 16, 128), F32),
                pltpu.VMEM((KERNEL, 8, t), F32),
                pltpu.VMEM((half // 128, t + 16, 128), F32),
                pltpu.VMEM((d // 128, t + 16, 128), F32),
                pltpu.VMEM((144, KERNEL * half), BF16),
                pltpu.VMEM((KERNEL * half, 128), BF16),
                pltpu.VMEM((128, KERNEL * half), F32),
                pltpu.VMEM((72, t), F32),
                pltpu.VMEM((72, t), F32),
                pltpu.VMEM((t, 2 * d), BF16),
                pltpu.VMEM((72, t), F32),
                pltpu.VMEM((KERNEL, 8, d), F32),
                pltpu.VMEM(wp.shape, F32),
                pltpu.VMEM(wpt.shape, F32),
                pltpu.VMEM((72, half), F32),
                pltpu.VMEM((128, d), F32),
            ]
            + [pltpu.VMEM((1,) + v.shape[1:], v.dtype) for v in blocks]
            + [
                pltpu.VMEM((1, t, d), F32),
                pltpu.VMEM((1, t, d), BF16),
                pltpu.SemaphoreType.DMA((len(blocks),)),
                pltpu.SemaphoreType.DMA((2, d // 128)),
            ],
        ),
        compiler_params=params(1),
        name="mix_bwd",
    )(s, segr, *blocks, wp, wd, wpt, wk, gs)


def prep_kernel(seg_ref, wd_ref, wk_ref, norm_ref, s_ref, segr_ref, small_ref, flip):
    mb, t = seg_ref.shape
    span = t - SEG_MOST + 1
    pos = lanes((1, t))
    for b in range(mb):
        row = seg_ref[b : b + 1, :].astype(F32)
        later = pltpu.roll(jnp.broadcast_to(row, (8, t)), t - (SEG_MOST - 1), 1)
        hit = (later[0:1, :] == row) & (pos < span)
        s = jnp.sum(jnp.where(hit, pos.astype(F32), 0.0)).astype(jnp.int32)
        s_ref[b] = s
        segr_ref[b] = pltpu.roll(jnp.broadcast_to(row, (8, t)), t - s, 1)[0:1, :]
    flip[...] = jnp.zeros_like(flip)
    rows = wd_ref.shape[0]
    flip[0:4, 0:rows] = norm_ref[...].astype(F32)
    small_ref[...] = jnp.zeros_like(small_ref)
    small_ref[:, 0:KERNEL] = wd_ref[...].astype(F32)
    small_ref[:, 16:20] = flip[...].T[0:rows, 0:4]
    row = lax.broadcasted_iota(jnp.int32, (HEADS * KERNEL, 8 * KERNEL), 0)
    col = lanes((HEADS * KERNEL, 8 * KERNEL))
    order = jnp.where(row % KERNEL * 8 + row // KERNEL == col, 1.0, 0.0).astype(BF16)
    heads = mm(wk_ref[...], order)
    small = PIECE // 2
    for p in range(rows // PIECE):
        small_ref[p * PIECE : p * PIECE + small, 32 : 32 + 8 * KERNEL] = heads[p * small : (p + 1) * small, :]


def prep(segments, w_depth, w_kernel, norms):
    mb, t = segments.shape
    rows = w_depth.shape[0]
    sds = jax.ShapeDtypeStruct
    vmem = pl.BlockSpec(memory_space=pltpu.VMEM)
    return pl.pallas_call(
        prep_kernel,
        out_shape=[sds((mb,), jnp.int32), sds((mb, 1, t), F32), sds((rows, 128), F32)],
        in_specs=[vmem] * 4,
        out_specs=[pl.BlockSpec(memory_space=pltpu.SMEM), vmem, vmem],
        scratch_shapes=[pltpu.VMEM((128, -(-rows // 128) * 128), F32)],
        name="prep",
    )(segments, w_depth, w_kernel, norms)


def finish_kernel(f_ref, m_ref, gp_ref, gdep_ref, gpt_ref, gk_ref, go_ref, gi_ref, gd_ref, gs_ref):
    half = f_ref.shape[1]
    rows = gp_ref.shape[0]
    tall = gd_ref.shape[0]
    gd_ref[...] = f_ref[0:tall, :]
    for j in range(gi_ref.shape[1] // half):
        gi_ref[:, j * half : (j + 1) * half] = f_ref[tall + j * rows : tall + (j + 1) * rows, :]
    tall = tall + rows * (gi_ref.shape[1] // half)
    for j in range(2):
        go_ref[:, j * half : (j + 1) * half] = f_ref[tall + j * rows : tall + (j + 1) * rows, :]
    wide = gp_ref.shape[1] // half
    for j in range(wide):
        gp_ref[:, j * half : (j + 1) * half] = m_ref[j * rows : (j + 1) * rows, :]
    gpt_ref[...] = m_ref[wide * rows : (wide + 1) * rows, :]
    small = m_ref[(wide + 1) * rows : (wide + 2) * rows, 0:256]
    gdep_ref[...] = small[:, 0:KERNEL]
    gk_ref[...] = small[0 : rows // 2, 128 : 128 + HEADS * KERNEL]
    gs_ref[...] = small[:, 16:24]


def finish(n, d, hid, f, m):
    half = d // 2
    sds = jax.ShapeDtypeStruct
    rows = d // n
    return pl.pallas_call(
        finish_kernel,
        out_shape=[
            sds((rows, 2 * d), F32), sds((rows, KERNEL), F32), sds((rows, half), F32), sds((half // n, HEADS * KERNEL), F32),
            sds((rows, d), F32), sds((rows, hid), F32), sds((2 * hid // n, half), F32), sds((rows, 8), F32),
        ],
        name="finish",
    )(f, m)


def side_by_side(block, parts):
    units, _, cols = block.shape
    return block.reshape(units, parts, PIECE, cols).transpose(0, 2, 1, 3).reshape(units * PIECE, parts * cols)


def native_sums(gf, gm, d, hid):
    gf, gm = gf.astype(F32), gm.astype(F32)
    half = d // 2
    tall = 2 * hid * PIECE // d
    wide = hid // half * PIECE
    many_p = 2 * d // half
    g_down = gf[:, :tall].reshape(-1, half)
    g_in = side_by_side(gf[:, tall : tall + wide], hid // half)
    g_out = side_by_side(gf[:, tall + wide :], 2)
    g_proj = side_by_side(gm[:, : many_p * PIECE], many_p)
    g_point = gm[:, many_p * PIECE : (many_p + 1) * PIECE].reshape(-1, half)
    small = gm[:, (many_p + 1) * PIECE :]
    g_kernel = small[:, : PIECE // 2, 128 : 128 + HEADS * KERNEL].reshape(half, -1)
    small = small[:, :, 0:24].reshape(d, -1)
    grads = [g_proj, small[:, :KERNEL], g_point, g_kernel, g_out, g_in, g_down, small[:, 16:]]
    return [lax.psum_scatter(g, "tok", scatter_dimension=0, tiled=True) for g in grads]


def rows_of(w):
    return w.reshape(-1, w.shape[-1])


def shards(n, tokens, segments, cotangent, w_proj, w_depth, w_point, w_kernel, w_out, g1, b1, w_in, w_down, g2, b2):
    d = tokens.shape[-1]
    hid = w_in.shape[1]
    units = d // PIECE
    own = n == units
    norms = [g1, b1, g2, b2]
    if own:
        more_a, more_b = [w_out, w_in], [w_in, w_down]
    else:
        given = [w_proj, w_in, w_down, w_point, w_out, w_depth, w_kernel] + norms
        wp, wi, wdn, wpt, wo, w_depth, w_kernel, *norms = [lax.all_gather(w, "tok", axis=0, tiled=True) for w in given]
        more_a = more_b = []
    s, segr, small = prep(segments[:, 0], w_depth, w_kernel, jnp.stack(norms))
    xr, cotr, wd_rows, wk_rows, *got = stage_front(n, s, tokens, cotangent, small, w_proj, w_point, own)
    if own:
        wp, wpt = (rows_of(w) for w in got)
    q, k, v, c, depth, span, mixed, taps, conv, *got_a = stage_a(n, segr, xr, wp, wd_rows, wpt, wk_rows, more_a)
    ctx, lse, *got_b = stage_b(n, segr, q, k, v, more_b)
    if own:
        wo, wi_a, wi_b, wdn = (rows_of(w) for w in got_a + got_b)
    else:
        wi_a, wi_b = jnp.split(wi, 2, 1)
    out_r, dres, dctx, dconv, gf, g_small = stage_c(units, ctx, conv, xr, cotr, wo, wi_a, wi_b, wdn, wd_rows)
    dq, dk, dv, *sums = stage_d(n, segr, q, k, v, ctx, lse, dctx, [gf] if own else [])
    gx, out, gm = stage_e(
        units, s, segr, xr, out_r, dres, dconv, dq, dk, dv, q, c, depth, span, mixed, taps, wp, wd_rows, wpt, wk_rows,
        g_small,
    )
    if own:
        sums = finish(n, d, hid, sums[0], scatter_all(n, 1, [gm], 6)[0])
    else:
        sums = native_sums(gf, gm, d, hid)
    g_proj, g_depth, g_point, g_kernel, g_out, g_in, g_down, g_vec = sums
    return (
        out, gx, g_proj, g_depth, g_point, g_kernel, g_out, g_vec[:, 0], g_vec[:, 1], g_in, g_down,
        g_vec[:, 2], g_vec[:, 3],
    )


def solution(mesh):
    rows, vec, act = P("tok", None), P("tok"), P(None, "tok", None)
    in_specs = (act, act, act, rows, rows, rows, rows, rows, vec, vec, rows, rows, vec, vec)
    out_specs = (act, act, rows, rows, rows, rows, rows, vec, vec, rows, rows, vec, vec)
    run = partial(shards, mesh.shape["tok"])
    return jax.shard_map(run, mesh=mesh, in_specs=in_specs, out_specs=out_specs, check_vma=False)
```

```python
import math
from functools import partial

import jax
import jax.numpy as jnp
from jax import lax
from jax.experimental import pallas as pl
from jax.experimental.pallas import tpu as pltpu
from jax.sharding import PartitionSpec as P

HEADS = 6
KERNEL = 9
REACH = 4
SEG_MOST = 1024
NORM_EPS = 1e-12
F32 = jnp.float32
BF16 = jnp.bfloat16
NT = (((1,), (1,)), ((), ()))
NN = (((1,), (0,)), ((), ()))
TN = (((0,), (0,)), ((), ()))
VMEM_CAP = 62 * 1024 * 1024
MESH = pl.DeviceIdType.MESH
PIECE = 24


def mm(a, b, dims=NN):
    return lax.dot_general(a, b, dims, preferred_element_type=F32)


def lanes(shape):
    return lax.broadcasted_iota(jnp.int32, shape, 1)


def split2(v):
    hi = v.astype(BF16)
    return hi, (v - hi.astype(F32)).astype(BF16)


def split3(v):
    hi = v.astype(BF16)
    rest = v - hi.astype(F32)
    mid = rest.astype(BF16)
    return hi, mid, (rest - mid.astype(F32)).astype(BF16)


def partner(me, bit):
    return me + (1 - 2 * lax.rem(lax.div(me, bit), 2)) * bit


def bit_of(me, bit):
    return lax.rem(lax.div(me, bit), 2)


def bit_orders(n):
    one = [1 << b for b in range(n.bit_length() - 1)]
    two = one[:1] + one[2:3] + one[1:2] + one[3:] if len(one) > 2 else one
    return one, two


def greet(n):
    me = lax.axis_index("tok")
    barrier = pltpu.get_barrier_semaphore()
    bits = bit_orders(n)[0]
    for bit in bits:
        pl.semaphore_signal(barrier, inc=1, device_id=(partner(me, bit),), device_id_type=MESH)
    pl.semaphore_wait(barrier, len(bits))


class Gather:
    def __init__(self, src, dst, take, part, order, send, recv, own):
        self.src, self.all, self.part, self.order = src.at[take], dst, part, order[::-1]
        self.send, self.recv, self.own = send, recv, own
        self.me = lax.axis_index("tok")

    def sizes(self):
        one = math.prod(self.src.shape) * jnp.dtype(self.all.dtype).itemsize
        return [one << i for i in range(len(self.order))]

    def held(self, s):
        free = self.order[:s]
        bits = [1 << b for b in reversed(range(len(self.order)))]
        return self.all.at[tuple(ALL if bit in free else bit_of(self.me, bit) for bit in bits) + self.part]

    def wait(self, sem, s):
        ref = self.held(s)
        pltpu.make_async_copy(ref, ref, sem.at[s]).wait()

    def step(self, s):
        if s == 0:
            pltpu.make_async_copy(self.src, self.held(0), self.own).start()
        elif s == 1:
            pltpu.make_async_copy(self.src, self.held(0), self.own).wait()
        if s > 0:
            self.wait(self.recv, s - 1)
        if s < len(self.order):
            pltpu.make_async_remote_copy(
                src_ref=self.held(s) if s else self.src,
                dst_ref=self.held(s),
                send_sem=self.send.at[s],
                recv_sem=self.recv.at[s],
                device_id=(partner(self.me, self.order[s]),),
                device_id_type=MESH,
            ).start()
        else:
            for i in range(s):
                self.wait(self.send, i)


def halves(order, s):
    left = sorted(set(order) - set(order[:s]), reverse=True)
    at = left.index(order[s])
    return 1 << at, 1 << (len(left) - 1 - at)


class Scatter:
    def __init__(self, n, src, first, out, mine, got, order, send, recv, own):
        self.n, self.src, self.mine, self.got, self.order, self.out = n, src, mine, got, order, out
        self.rows = pl.ds(first, mine.shape[1])
        self.send, self.recv, self.own = send, recv, own
        self.me = lax.axis_index("tok")

    def sizes(self):
        one = math.prod(self.mine.shape[1:]) * 2
        return [one * (self.n >> (i + 1)) for i in range(len(self.order))]

    def side(self, s, keep):
        hi, lo = halves(self.order, s)
        bit = bit_of(self.me, self.order[s])
        which = bit if keep else 1 - bit
        if s == 0:
            view = self.src.reshape((hi, 2, lo) + self.src.shape[1:])
            return view.at[:, which, :, self.rows]
        held = self.got[s - 1]
        return held.reshape((hi, 2, lo) + held.shape[1:]).at[:, which]

    def there(self, ref, s):
        hi, lo = halves(self.order, s)
        return ref.reshape((hi, lo) + ref.shape[1:])

    def send_copy(self, s):
        return pltpu.make_async_remote_copy(
            src_ref=self.side(s, False),
            dst_ref=self.there(self.got[s], s),
            send_sem=self.send.at[s],
            recv_sem=self.recv.at[s],
            device_id=(partner(self.me, self.order[s]),),
            device_id_type=MESH,
        )

    def own_copy(self):
        return pltpu.make_async_copy(self.side(0, True), self.there(self.mine, 0), self.own)

    def add(self, s):
        self.send_copy(s).wait_recv()
        got = self.got[s]
        if s == 0:
            self.own_copy().wait()

            def first(k, c):
                got[k] = (got[k].astype(F32) + self.mine[k].astype(F32)).astype(BF16)
                return c

            lax.fori_loop(0, got.shape[0], first, 0)
            return
        hi, lo = halves(self.order, s)
        held = self.got[s - 1]
        bit = bit_of(self.me, self.order[s])

        def one(k, c):
            for i in range(lo):
                to, at = k * lo + i, (k * 2 + bit) * lo + i
                got[to] = (got[to].astype(F32) + held[at].astype(F32)).astype(BF16)
            return c

        if s < len(self.order) - 1:
            lax.fori_loop(0, hi, one, 0)
        else:
            self.out[self.rows, :] = got[0].astype(F32) + held[bit].astype(F32)

    def step(self, s):
        if s > 0:
            self.add(s - 1)
        if s < len(self.order):
            self.send_copy(s).start()
        if s == 0:
            self.own_copy().start()
        if s == len(self.order):
            for i in range(s):
                self.send_copy(i).wait_send()


ANY = pl.BlockSpec(memory_space=pl.ANY)


def remote(cid):
    return pltpu.CompilerParams(collective_id=cid, has_side_effects=True, vmem_limit_bytes=VMEM_CAP)


GATHER_PACE = (2.5, 90e3)
SCATTER_PACE = (2.2, 95e3)


def schedule(parts, last, spots, pace):
    stage, rate = pace
    cost = {1: 1 / (4 * rate), 2: 2 / rate, 4: 2 / rate, 8: 2 / rate}
    link = [{1: 0, 2: 1, 4: 2}.get(bit, 3) for bit in range(1 << last)]
    free, ready, at = [0.0] * 4, [0.0] * len(parts), [0] * len(parts)
    plan = []
    for now in spots:
        due = []
        for p, (bits, sizes) in enumerate(parts):
            if at[p] <= last and ready[p] <= now:
                due.append((p, at[p]))
                if at[p] < last:
                    bit = bits[at[p]]
                    begin = max(now, free[link[bit]])
                    free[link[bit]] = begin + sizes[at[p]] * cost.get(bit, 4 / rate)
                    ready[p] = free[link[bit]] + stage
                at[p] += 1
        plan.append(due)
    plan.append([(p, i) for i in range(last + 1) for p in range(len(parts)) if at[p] <= i])
    return plan


class Timed:
    def __init__(self, n, parts, spots, pace):
        self.parts = parts
        self.last = n.bit_length() - 1
        self.ticks = self.last + 1
        self.plan = [[(p, t) for p in range(len(parts))] for t in range(self.ticks)]
        if spots is not None:
            self.plan = schedule([(p.order, p.sizes()) for p in parts], self.last, spots, pace)
            self.ticks = len(self.plan)

    def tick(self, t):
        for p, i in self.plan[t]:
            self.parts[p].step(i)


ALL = slice(None)


def pieces(wide, count, rows=False):
    size = wide // count
    cuts = [pl.ds(i * size, size) for i in range(count)]
    return [(c, ALL) if rows else (ALL, c) for c in cuts]


def gathers(n, srcs, dsts, layout, sems, spots=None):
    send, recv, own = sems
    orders = bit_orders(n)
    return Timed(
        n,
        [
            Gather(srcs[a], dsts[a], parts[0], parts[-1], orders[i % 2], send.at[i], recv.at[i], own.at[i])
            for i, (a, *parts) in enumerate(layout)
        ],
        spots,
        GATHER_PACE,
    )


def gather_sems(n, layout):
    stages, count = n.bit_length() - 1, len(layout)
    dma = pltpu.SemaphoreType.DMA
    return [dma((count, stages)), dma((count, stages)), dma((count,))]


def gathered(n, shards):
    return [jax.ShapeDtypeStruct((2,) * (n.bit_length() - 1) + w.shape, w.dtype) for w in shards]


def split_rows(rows, parts):
    tiles = rows // 16
    cuts = [tiles * i // parts * 16 for i in range(parts + 1)]
    return [(a, b - a) for a, b in zip(cuts, cuts[1:]) if b > a]


def scatters(n, cuts, srcs, outs, refs, spots=None):
    total, stages = len(cuts), n.bit_length() - 1
    accs, gots, (send, recv, own) = refs[:total], refs[total:-3], refs[-3:]
    gots = [gots[stages * j : stages * (j + 1)] for j in range(total)]
    orders = bit_orders(n)
    return Timed(
        n,
        [
            Scatter(n, srcs[i], a, outs[i], accs[j], gots[j], orders[j % 2], send.at[j], recv.at[j], own.at[j])
            for j, (i, a, r) in enumerate(cuts)
        ],
        spots,
        SCATTER_PACE,
    )


def scatter_cuts(packed, parts):
    return [(i, a, r) for i, w in enumerate(packed) for a, r in split_rows(w.shape[1], parts)]


def scatter_scratch(n, cuts, packed):
    total, stages = len(cuts), n.bit_length() - 1
    dma = pltpu.SemaphoreType.DMA
    bufs = [(r, packed[i].shape[2]) for i, a, r in cuts]
    return (
        [pltpu.VMEM((n // 2,) + b, BF16) for b in bufs]
        + [pltpu.VMEM((n >> (s + 1),) + b, BF16) for b in bufs for s in range(stages)]
        + [dma((total, stages)), dma((total, stages)), dma((total,))]
    )


def scatter_all(n, cid, packed, parts):
    cuts = scatter_cuts(packed, parts)
    count = len(packed)

    def kernel(*refs):
        greet(n)
        plan = scatters(n, cuts, refs[:count], refs[count : 2 * count], refs[2 * count :])
        for t in range(plan.ticks):
            plan.tick(t)

    return pl.pallas_call(
        kernel,
        out_shape=[jax.ShapeDtypeStruct(w.shape[1:], F32) for w in packed],
        in_specs=[ANY] * count,
        out_specs=[pl.BlockSpec(memory_space=pltpu.VMEM)] * count,
        scratch_shapes=scatter_scratch(n, cuts, packed),
        compiler_params=remote(cid),
        name="scatter",
    )(*packed)


def expand_taps(tap_rows, e_ref):
    hi, lo = split2(tap_rows)
    both = jnp.concatenate([hi, lo], 0)
    return mm(both, e_ref[...], TN)


def fill_expander(e_ref):
    half = e_ref.shape[1] // KERNEL
    shape = (72, 128)
    row = lax.broadcasted_iota(jnp.int32, shape, 0)
    upper = jnp.where(lanes(shape) >= 64, 1, 0)
    for o in range(KERNEL):
        for j in range(half // 128):
            one = jnp.where(row == upper + (o * 8 + 2 * j), 1.0, 0.0).astype(BF16)
            cols = pl.ds(o * half + j * 128, 128)
            e_ref[0:72, cols] = one
            e_ref[72:144, cols] = one


def mask_rows(segb_ref, r0, rows):
    own = segb_ref[pl.ds(8 + r0, rows), :]
    return [
        jnp.where(segb_ref[pl.ds(8 + r0 + o - REACH, rows), :] == own, 1.0, 0.0)
        for o in range(KERNEL)
    ]


def fill_segments(seg_ref, segb_ref, vt_ref):
    t = seg_ref.shape[-1]
    row = seg_ref[...]
    if segb_ref is not None:
        wide = jnp.broadcast_to(row, (128, t))
        segb_ref[0:8, :] = jnp.full((8, 128), -1.0, F32)
        segb_ref[t + 8 : t + 16, :] = jnp.full((8, 128), -1.0, F32)
        segb_ref[8 : t + 8, :] = wide.T
    if vt_ref is None:
        return
    tall = jnp.broadcast_to(row, (8, t))
    pos = lanes((8, t))
    for o in range(KERNEL):
        d = o - REACH
        moved = pltpu.roll(tall, (-d) % t, 1) if d else tall
        inside = (pos + d >= 0) & (pos + d < t)
        vt_ref[o] = jnp.where(inside & (moved == tall), 1.0, 0.0)


def masked_tiles(t, body, between=None):
    full = SEG_MOST // 128

    def inner(i, c):
        body(pl.multiple_of(i * 128, 128), False)
        return c

    lax.fori_loop(1, full - 1, inner, 0)
    if between is not None:
        between()

    def edge(i, c):
        idx = jnp.where(i == 0, 0, i + full - 2)
        body(pl.multiple_of(idx * 128, 128), True)
        return c

    lax.fori_loop(0, t // 128 - full + 2, edge, 0)


def piece_rows(d):
    small = PIECE // 2
    row = lax.broadcasted_iota(jnp.int32, (d, d // 2), 0)
    col = lanes((1, d // 2))
    return jnp.where(row == col + col // small * small, 1.0, 0.0).astype(BF16)


def unpack_small(sm_ref, wd_ref, wk_ref):
    d = sm_ref.shape[0]
    parts = [sm_ref[j * 128 : (j + 1) * 128, :].T for j in range(d // 128)]
    tall = jnp.concatenate(parts, 1)
    wd_ref[...] = tall[0:24, :]
    wk_ref[...] = mm(tall[32:104, :].astype(BF16), piece_rows(d), NN).astype(BF16)


def front_layout(d, half):
    cols = pieces(2 * d, 4)
    rest = [(1, (ALL, pl.ds(0, 128))), (1, (ALL, pl.ds(128, half - 128)))]
    return [(0, cols[0]), (0, cols[1]), (2, (ALL, ALL)), (0, cols[2]), (0, cols[3])] + rest


def kernel_front(n, layout, *refs):
    s_ref, x_ref, cot_ref = refs[:3]
    if layout:
        sm_src, wp_src, wpt_src = refs[3:6]
        xr_ref, cotr_ref, wd_ref, wk_ref, wp_far, wpt_far = refs[6:12]
        raw, sm, *sems = refs[12:]
        plan = gathers(n, (wp_src, wpt_src, sm_src), (wp_far, wpt_far, sm), layout, sems)
    else:
        sm_src = refs[3]
        xr_ref, cotr_ref, wd_ref, wk_ref = refs[4:8]
        raw, sm = refs[8:]
        plan = None
    t, d = x_ref.shape[1:]
    nch = d // 128
    b = pl.program_id(0)
    s = s_ref[b]
    end = pl.num_programs(0) - 1
    point(b == 0, lambda: greet(n), plan, 0)
    for src, dst in ((cot_ref, cotr_ref), (x_ref, xr_ref)):
        for j in range(nch):
            col = pl.ds(j * 128, 128)
            raw[0:t, :] = src[0, :, col].astype(F32)
            raw[t : t + 128, :] = src[0, 0:128, col].astype(F32)
            dst[0, :, col] = raw[pl.ds(s, t), :].astype(BF16)

    point(b == 0, None, plan, 1)

    @pl.when(b == end)
    def _():
        if plan is not None:
            for i in range(2, plan.ticks):
                plan.tick(i)
            unpack_small(sm.reshape(d, 128), wd_ref, wk_ref)
        else:
            unpack_small(sm_src, wd_ref, wk_ref)


def stage_front(n, s, x, cot, small, wp, wpt, own):
    mb, t, d = x.shape
    half = d // 2
    sds = jax.ShapeDtypeStruct
    layout = front_layout(d, half) if own else []
    more = [wp, wpt] if own else []
    out = [((mb, t, d), BF16)] * 2
    return pl.pallas_call(
        partial(kernel_front, n, layout),
        out_shape=[sds(*o) for o in out] + [sds((24, d), F32), sds((72, half), BF16)] + gathered(n, more),
        grid_spec=pltpu.PrefetchScalarGridSpec(
            num_scalar_prefetch=1,
            grid=(mb,),
            in_specs=[per_block(t, d), per_block(t, d), ANY if own else whole(*small.shape)] + [ANY] * len(more),
            out_specs=[per_block(t, d)] * 2 + [whole(24, d), whole(72, half)] + [ANY] * len(more),
            scratch_shapes=[
                pltpu.VMEM((t + 128, 128), F32),
                pltpu.VMEM((2,) * (n.bit_length() - 1) + (PIECE, 128) if own else (8, 128), F32),
            ]
            + (gather_sems(n, layout) if own else []),
        ),
        compiler_params=params(1, 0 if own else None),
        name="front",
    )(s, x, cot, small, *more)


A_SPOTS = [block + at for block in (0.0, 16.5) for at in (0.0, 3.0, 6.0, 7.4, 8.6, 11.0, 12.3, 13.6)]


def kernel_a(n, layout, count, *refs):
    seg_ref, xr_ref, wp_ref, wd_ref, wpt_ref, wk_ref = refs[:6]
    srcs, refs = refs[6 : 6 + count], refs[6 + count :]
    q_ref, k_ref, v_ref, c_ref, depth_ref, span_ref, mixed_ref, taps_ref, conv_ref = refs[:9]
    dsts, refs = refs[9 : 9 + count], refs[9 + count :]
    xs, segb, vt, cs, lt, e_ref, texp, *sems = refs
    plan = gathers(n, srcs, dsts, layout, sems, A_SPOTS) if count else None
    t, d = xr_ref.shape[1:]
    half = d // 2
    nch = d // 128
    b = pl.program_id(0)
    end = pl.num_programs(0) - 1
    if plan is not None:
        @pl.when(b == 0)
        def _():
            greet(n)

    def spot(i, loop, every):
        for at in range(3):
            for block in range(2):
                point((b == block) & (i == at * every), None, plan, 8 * block + 2 + 3 * loop + at)

    def early(at):
        for block in range(2):
            point(b == block, None, plan, 8 * block + at)

    early(0)

    @pl.when(b == 0)
    def _():
        fill_expander(e_ref)
        cs[:, 0:8, :] = jnp.zeros((nch // 2, 8, 128), F32)
        cs[:, t + 8 : t + 16, :] = jnp.zeros((nch // 2, 8, 128), F32)
        xs[:, 0:8, :] = jnp.zeros((nch, 8, 128), F32)
        xs[:, t + 8 : t + 16, :] = jnp.zeros((nch, 8, 128), F32)

    fill_segments(seg_ref, segb, vt)
    for j in range(nch):
        xs[j, 8 : t + 8, :] = xr_ref[0, :, pl.ds(j * 128, 128)].astype(F32)

    def depth_tile(r0, masked):
        masks = mask_rows(segb, r0, 128) if masked else None
        for j in range(nch):
            acc = None
            for o in range(KERNEL):
                part = xs[j, pl.ds(8 + r0 + o - REACH, 128), :]
                w = wd_ref[o : o + 1, pl.ds(j * 128, 128)]
                part = part * (masks[o] * w) if masked else part * w
                acc = part if acc is None else acc + part
            depth_ref[0, pl.ds(r0, 128), pl.ds(j * 128, 128)] = acc.astype(BF16)

    masked_tiles(t, depth_tile, lambda: early(1))

    def proj_tile(i, carry):
        spot(i, 0, 1)
        r0 = pl.multiple_of(i * 384, 128)
        rows = pl.ds(r0, 384)
        merged = mm(xr_ref[0, rows, :], wp_ref[...]).astype(BF16)
        q = merged[:, 0:half]
        q_ref[0, rows, :] = q
        k_ref[0, rows, :] = merged[:, half : 2 * half]
        v_ref[0, rows, :] = merged[:, 2 * half : 3 * half]
        c = merged[:, 3 * half :]
        c_ref[0, rows, :] = c
        for j in range(nch // 2):
            cs[j, pl.ds(8 + r0, 384), :] = c[:, j * 128 : (j + 1) * 128].astype(F32)
        span = mm(depth_ref[0, rows, :], wpt_ref[...])
        span_ref[0, rows, :] = span
        mixed = (span * q.astype(F32)).astype(BF16)
        mixed_ref[0, rows, :] = mixed
        lt[:, rows] = mm(wk_ref[...], mixed, NT)
        return carry

    lax.fori_loop(0, t // 384, proj_tile, 0)

    logits = [lt[o * 8 : o * 8 + 8, :] for o in range(KERNEL)]
    top = logits[0]
    for o in range(1, KERNEL):
        top = jnp.maximum(top, logits[o])
    exps = [jnp.exp(v - top) for v in logits]
    total = exps[0]
    for o in range(1, KERNEL):
        total = total + exps[o]
    inv = 1.0 / total
    for o in range(KERNEL):
        tap = exps[o] * inv
        taps_ref[0, o * 8 : o * 8 + 8, :] = tap
        lt[o * 8 : o * 8 + 8, :] = tap * vt[o]

    def conv_tile(i, carry):
        spot(i, 1, 3)
        r0 = pl.multiple_of(i * 128, 128)
        rows = pl.ds(r0, 128)
        texp[...] = expand_taps(lt[:, rows], e_ref)
        for j in range(nch // 2):
            acc = None
            for o in range(KERNEL):
                part = cs[j, pl.ds(8 + r0 + o - REACH, 128), :] * texp[:, o * half + j * 128 : o * half + (j + 1) * 128]
                acc = part if acc is None else acc + part
            conv_ref[0, rows, pl.ds(j * 128, 128)] = acc.astype(BF16)
        return carry

    lax.fori_loop(0, t // 128, conv_tile, 0)
    point(b == end, None, plan, len(A_SPOTS))


def whole(*shape):
    return pl.BlockSpec(shape, lambda *_: (0,) * len(shape), pipeline_mode=pl.Buffered(1))


def per_block(*shape):
    return pl.BlockSpec((1,) + shape, lambda b, *_: (b,) + (0,) * len(shape))


def params(n, cid=None):
    more = {} if cid is None else {"collective_id": cid, "has_side_effects": True}
    return pltpu.CompilerParams(dimension_semantics=("arbitrary",) * n, vmem_limit_bytes=VMEM_CAP, **more)


def point(when, first, plan, s):
    if plan is None or not plan.plan[s]:
        return

    @pl.when(when)
    def _():
        if first is not None:
            first()
        plan.tick(s)


def stage_a(n, segr, xr, wp, wd, wpt, wk, more):
    mb, t, d = xr.shape
    half = d // 2
    sds = jax.ShapeDtypeStruct
    out = [
        ((t, half), BF16), ((t, half), BF16), ((t, half), BF16), ((t, half), BF16), ((t, d), BF16),
        ((t, half), F32), ((t, half), BF16), ((72, t), F32), ((t, half), BF16),
    ]
    layout, far = [], []
    if more:
        hid = more[1].shape[1] // 2
        layout = [(0, p) for p in pieces(d, 2)] + [(1, p) for p in pieces(hid, 2)]
        layout = [layout[i] for i in (2, 3, 0, 1)]
        far = [more[0], jax.ShapeDtypeStruct((more[1].shape[0], hid), BF16)]
    return pl.pallas_call(
        partial(kernel_a, n, layout, len(more)),
        out_shape=[sds((mb,) + sh, dt) for sh, dt in out] + gathered(n, far),
        grid=(mb,),
        in_specs=[
            pl.BlockSpec((pl.Squeezed(), 1, t), lambda b: (b, 0, 0)),
            per_block(t, d), whole(*wp.shape), whole(*wd.shape), whole(*wpt.shape), whole(*wk.shape),
        ]
        + [ANY] * len(more),
        out_specs=[per_block(*sh) for sh, _ in out] + [ANY] * len(more),
        scratch_shapes=[
            pltpu.VMEM((d // 128, t + 16, 128), F32),
            pltpu.VMEM((t + 16, 128), F32),
            pltpu.VMEM((KERNEL, 8, t), F32),
            pltpu.VMEM((half // 128, t + 16, 128), F32),
            pltpu.VMEM((72, t), F32),
            pltpu.VMEM((144, KERNEL * half), BF16),
            pltpu.VMEM((128, KERNEL * half), F32),
        ]
        + (gather_sems(n, layout) if more else []),
        compiler_params=params(1, 2 if more else None),
        name="mix_fwd",
    )(segr, xr, wp, wd, wpt, wk, *more)


QT = 1024


def seg_codes(segb, first):
    lane = lanes(segb.shape) - first
    hot = segb == lane.astype(F32)
    inside = (lane >= 0) & (lane < 24)
    return jnp.where(hot & inside, 1.0, 0.0), jnp.where(inside & ~hot, -1e30, 0.0)


def tile_points(n, plan, spots, i, tiles, h=0, heads=2):
    if plan is None:
        return
    step = pl.program_id(0) * pl.num_programs(1) + pl.program_id(1)
    for t in range(h, len(spots), heads):
        at = t // heads
        point((step == at // tiles) & (i == at % tiles), (lambda: greet(n)) if t == 0 else None, plan, t)


def end_points(plan):
    if plan is None:
        return
    last = (pl.program_id(0) == pl.num_programs(0) - 1) & (pl.program_id(1) == pl.num_programs(1) - 1)
    point(last, None, plan, plan.ticks - 1)


B_SPOTS = [5.0 * i for i in range(6)]


def kernel_b(n, layout, count, *refs):
    segt_ref, q_ref, k_ref, v_ref = refs[:4]
    srcs, (ctx_ref, lse_ref) = refs[4 : 4 + count], refs[4 + count : 6 + count]
    dsts, sems = refs[6 + count : 6 + 2 * count], refs[6 + 2 * count :]
    plan = gathers(n, srcs, dsts, layout, sems, B_SPOTS) if count else None
    t = q_ref.shape[1]
    tail = t - SEG_MOST
    low_half = lanes((1, 128)) < 64

    def finish(rows, outs, tops):
        both = jnp.where(low_half, outs[0], outs[1])
        sums = jnp.where(low_half, outs[1], outs[0])
        ctx_ref[0, rows, :] = (both / pltpu.roll(sums, 64, 1)).astype(BF16)
        lse_ref[0, rows, :] = jnp.where(low_half, tops[1], tops[0]) + jnp.log(sums)

    def one(q, k, v):
        scores = mm(q, k, NT)
        top = jnp.max(scores, -1, keepdims=True)
        return mm(jnp.exp(scores - top).astype(BF16), v), top

    k = k_ref[0, 0:SEG_MOST, :]
    v = v_ref[0, 0:SEG_MOST, :]
    one_b = jnp.ones((), BF16)
    vs = (jnp.where(low_half, v, one_b), jnp.where(low_half, one_b, v))

    def tile(i, carry):
        rows = pl.ds(pl.multiple_of(i * QT, QT), QT)
        q = q_ref[0, rows, :] * 0.125
        zero = jnp.zeros((), BF16)
        tile_points(n, plan, B_SPOTS, i, SEG_MOST // QT, heads=1)
        outs = [one(jnp.where(low_half, q, zero), k, vs[0])]
        outs.append(one(jnp.where(low_half, zero, q), k, vs[1]))
        finish(rows, [o[0] for o in outs], [o[1] for o in outs])
        return carry

    lax.fori_loop(0, SEG_MOST // QT, tile, 0)
    rows = pl.ds(SEG_MOST, tail)
    q = q_ref[0, rows, :] * 0.125
    kt = k_ref[0, rows, :]
    vt = v_ref[0, rows, :]
    segb = jnp.broadcast_to(segt_ref[...], (128, tail)).T
    outs = []
    for h in range(2):
        hot, pen = seg_codes(segb, 64 - 64 * h)
        mine = low_half if h == 0 else ~low_half
        outs.append(
            one(
                jnp.where(mine, q, pen.astype(BF16)),
                jnp.where(mine, kt, hot.astype(BF16)),
                jnp.where(mine, vt, one_b),
            )
        )
    finish(rows, [o[0] for o in outs], [o[1] for o in outs])
    end_points(plan)


def pair(t):
    return pl.BlockSpec((1, t, 128), lambda b, j: (b, 0, j))


def seg_tail(tail):
    return pl.BlockSpec((pl.Squeezed(), 1, tail), lambda b, *_: (b, 0, SEG_MOST // tail))


def stage_b(n, segt, q, k, v, more):
    mb, t, half = q.shape
    sds = jax.ShapeDtypeStruct
    layout, far = [], []
    if more:
        hid = more[0].shape[1] // 2
        cols = pieces(hid, 2)
        wide = [(0, (ALL, pl.ds(hid + i * (hid // 2), hid // 2)), p) for i, p in enumerate(cols)]
        tall = [(1, p) for p in pieces(more[1].shape[0], 4, True)]
        layout = tall[:2] + wide + tall[2:]
        far = [jax.ShapeDtypeStruct((more[0].shape[0], hid), BF16), more[1]]
    return pl.pallas_call(
        partial(kernel_b, n, layout, len(more)),
        out_shape=[sds((mb, t, half), BF16), sds((mb, t, half), F32)] + gathered(n, far),
        grid=(mb, half // 128),
        in_specs=[seg_tail(t - SEG_MOST), pair(t), pair(t), pair(t)] + [ANY] * len(more),
        out_specs=[pair(t), pair(t)] + [ANY] * len(more),
        scratch_shapes=gather_sems(n, layout) if more else [],
        compiler_params=params(2, 3 if more else None),
        name="att_fwd",
    )(segt, q, k, v, *more)


ROWS = 384


def norm_fwd(values):
    centre = values - jnp.mean(values, -1, keepdims=True)
    inv_std = lax.rsqrt(jnp.mean(centre * centre, -1, keepdims=True) + NORM_EPS)
    return centre * inv_std, inv_std


def norm_back(grad, normed, inv_std):
    one = jnp.mean(grad, -1, keepdims=True)
    two = jnp.mean(grad * normed, -1, keepdims=True)
    return inv_std * (grad - one - normed * two)


def gelu_both(x):
    cdf = 0.5 + 0.5 * lax.erf(x * 0.7071067811865476)
    bell = jnp.exp(x * (x * -0.5))
    return x * cdf, cdf + x * (bell * 0.3989422804014327)


def col_sum(v):
    return jnp.sum(v, 0, keepdims=True)


def kernel_c(
    ctx_ref, conv_ref, x_ref, cot_ref, wo_ref, wia_ref, wib_ref, wdn_ref, ln_ref,
    out_ref, dres_ref, dctx_ref, dconv_ref, gf_ref, gs_ref,
    joined, act, slope, dinner, go_ref, gi_ref, gd_ref, wi_ref,
):
    first = (pl.program_id(0) == 0) & (pl.program_id(1) == 0)
    last = (pl.program_id(0) == pl.num_programs(0) - 1) & (pl.program_id(1) == pl.num_programs(1) - 1)
    d = x_ref.shape[-1]
    half = d // 2
    hid = wi_ref.shape[1]

    @pl.when(first)
    def _():
        wi_ref[:, 0 : hid // 2] = wia_ref[...]
        wi_ref[:, hid // 2 :] = wib_ref[...]
        go_ref[...] = jnp.zeros_like(go_ref)
        gi_ref[...] = jnp.zeros_like(gi_ref)
        gd_ref[...] = jnp.zeros_like(gd_ref)
        gs_ref[...] = jnp.zeros_like(gs_ref)

    joined[:, 0:half] = ctx_ref[0]
    joined[:, half:] = conv_ref[0]
    gain1, shift1, gain2, shift2 = (ln_ref[16 + i : 17 + i, :] for i in range(4))
    normed1, inv1 = norm_fwd(mm(joined[...], wo_ref[...]) + x_ref[0].astype(F32))
    hidden = normed1 * gain1 + shift1
    hidden_low = hidden.astype(BF16)
    outers = []
    for g in range(2):
        cols = pl.ds(g * hid, hid)
        inner = mm(hidden_low[:, g * half : (g + 1) * half], wi_ref[g * half : (g + 1) * half, :])
        value, deriv = gelu_both(inner)
        act[:, cols] = value.astype(BF16)
        slope[:, cols] = deriv
        outers.append(mm(act[:, cols], wdn_ref[g * hid : (g + 1) * hid, :]))
    normed2, inv2 = norm_fwd(jnp.concatenate(outers, 1) + hidden)
    out_ref[0] = (normed2 * gain2 + shift2).astype(BF16)
    cot = cot_ref[0].astype(F32)
    gs_ref[2:3, :] += col_sum(cot * normed2)
    gs_ref[3:4, :] += col_sum(cot)
    d_sum = norm_back(cot * gain2, normed2, inv2)
    d_outer = d_sum.astype(BF16)
    d_hid = []
    for g in range(2):
        cols = pl.ds(g * hid, hid)
        mine = d_outer[:, g * half : (g + 1) * half]
        d_act = mm(mine, wdn_ref[g * hid : (g + 1) * hid, :], NT)
        gd_ref[:, cols] += mm(mine, act[:, cols], TN)
        dinner[:, cols] = (d_act * slope[:, cols]).astype(BF16)
        d_hid.append(mm(dinner[:, cols], wi_ref[g * half : (g + 1) * half, :], NT))
        gi_ref[g * half : (g + 1) * half, :] += mm(hidden_low[:, g * half : (g + 1) * half], dinner[:, cols], TN)
    d_hidden = jnp.concatenate(d_hid, 1) + d_sum
    gs_ref[0:1, :] += col_sum(d_hidden * normed1)
    gs_ref[1:2, :] += col_sum(d_hidden)
    d_res = norm_back(d_hidden * gain1, normed1, inv1)
    dres_ref[0] = d_res
    d_attn = d_res.astype(BF16)
    d_joined = mm(d_attn, wo_ref[...], NT)
    dctx_ref[0] = d_joined[:, 0:half].astype(BF16)
    dconv_ref[0] = d_joined[:, half:]
    go_ref[...] += mm(joined[...], d_attn, TN)

    @pl.when(last)
    def _():
        n, _, _ = gf_ref.shape
        rows = d // n
        tall = 2 * hid // n

        def emit(p, c):
            at = pl.ds(pl.multiple_of(p * rows, 8), rows)
            gi = gi_ref[at, :]
            go = go_ref[at, :]
            parts = [gi[:, j * half : (j + 1) * half] for j in range(hid // half)] + [go[:, 0:half], go[:, half:]]
            gf_ref[p, tall : tall + rows * len(parts), :] = jnp.concatenate(parts, 0).astype(BF16)
            return c

        lax.fori_loop(0, n, emit, 0)

        step = 4
        wide = step * tall

        def emit_down(i, c):
            block = gd_ref[:, pl.ds(pl.multiple_of(i * wide, 128), wide)].T.astype(BF16)
            for j in range(step):
                gf_ref[i * step + j, 0:tall, :] = block[j * tall : (j + 1) * tall, :]
            return c

        lax.fori_loop(0, n // step, emit_down, 0)


def stage_c(n, ctx, conv, x, cot, wo, wi_a, wi_b, wdn, ln):
    mb, t, d = x.shape
    half = d // 2
    hid = 2 * wi_a.shape[1]
    packed = (d * d + d * hid + 2 * hid * half) // (n * half)
    sds = jax.ShapeDtypeStruct

    def tile(cols):
        return pl.BlockSpec((1, ROWS, cols), lambda b, i: (b, i, 0))

    return pl.pallas_call(
        kernel_c,
        out_shape=[
            sds((mb, t, d), BF16), sds((mb, t, d), F32), sds((mb, t, half), BF16), sds((mb, t, half), F32),
            sds((n, packed, half), BF16), sds((8, d), F32),
        ],
        grid=(mb, t // ROWS),
        in_specs=[
            tile(half), tile(half), tile(d), tile(d),
            whole(*wo.shape), whole(*wi_a.shape), whole(*wi_b.shape), whole(*wdn.shape), whole(*ln.shape),
        ],
        out_specs=[
            tile(d), tile(d), tile(half), tile(half),
            whole(n, packed, half), whole(8, d),
        ],
        scratch_shapes=[
            pltpu.VMEM((ROWS, d), BF16),
            pltpu.VMEM((ROWS, 2 * hid), BF16),
            pltpu.VMEM((ROWS, 2 * hid), F32),
            pltpu.VMEM((ROWS, 2 * hid), BF16),
            pltpu.VMEM((d, d), F32),
            pltpu.VMEM((d, hid), F32),
            pltpu.VMEM((half, 2 * hid), F32),
            pltpu.VMEM((d, hid), BF16),
        ],
        compiler_params=params(2),
        name="ffn",
    )(ctx, conv, x, cot, wo, wi_a, wi_b, wdn, ln)


KT = 512
D_SPOTS = [1.9 * i for i in range(24)]


def kernel_d(n, cuts, *refs):
    count = 1 if cuts else 0
    segt_ref, q_ref, k_ref, v_ref, ctx_ref, lse_ref, do_ref = refs[:7]
    srcs, refs = refs[7 : 7 + count], refs[7 + count :]
    dq_ref, dk_ref, dv_ref = refs[:3]
    outs, refs = refs[3 : 3 + count], refs[3 + count :]
    qa, da, dqt, *rest = refs
    plan = scatters(n, cuts, srcs, outs, rest, D_SPOTS) if count else None
    t = q_ref.shape[1]
    tail = t - SEG_MOST
    lane = lanes((1, 128))
    low_half = lane < 64
    one_b = jnp.ones((), BF16)
    zero_b = jnp.zeros((), BF16)

    r = lax.broadcasted_iota(jnp.int32, (256, 128), 0) % 128
    c = lax.broadcasted_iota(jnp.int32, (256, 128), 1)
    swap = jnp.where((r < 64) != (c < 64), 1.0, 0.0).astype(BF16)
    prod = do_ref[0].astype(F32) * ctx_ref[0].astype(F32)
    hi, lo = split2(prod)
    dsum = mm(jnp.concatenate([hi, lo], 1), swap)
    q8 = q_ref[0] * 0.125
    do = do_ref[0]
    for stat, src, dst in ((lse_ref[0], q8, qa), (dsum, do, da)):
        pieces = split3(-stat)
        code = jnp.where(
            (lane & 63) == 0, pieces[0], jnp.where((lane & 63) == 1, pieces[1], jnp.where((lane & 63) == 2, pieces[2], zero_b))
        )
        dst[0] = jnp.where(low_half, src, code)
        dst[1] = jnp.where(low_half, code, src)

    def run(key_rows, q_rows, h, codes):
        mark = (lane & 63) < 3
        mine = low_half if h == 0 else ~low_half
        k = k_ref[0, key_rows, :]
        v = v_ref[0, key_rows, :]
        ka = jnp.where(mine, k, jnp.where(mark, one_b, zero_b))
        va = jnp.where(mine, v, jnp.where(mark, one_b, zero_b))
        qh = qa[h, q_rows, :]
        if codes is not None:
            hot, pen = codes
            qh = qh + pen
            ka = ka + hot
        p = jnp.exp(mm(ka, qh, NT))
        dp = mm(va, da[h, q_rows, :], NT)
        ds = (p * dp).astype(BF16)
        dv = mm(p.astype(BF16), do_ref[0, q_rows, :])
        dk = mm(ds, q_ref[0, q_rows, :] * 0.125)
        return ds, dk, dv, k

    main = pl.ds(0, SEG_MOST)

    def tile(i, carry):
        rows = pl.ds(pl.multiple_of(i * KT, KT), KT)
        halves = []
        for h in range(2):
            tile_points(n, plan, D_SPOTS, i, SEG_MOST // KT, h)
            ds, dk, dv, k = run(rows, main, h, None)
            part = mm(k[:, 64 * h : 64 * h + 64], ds, TN)
            dqt[64 * h : 64 * h + 64, :] = jnp.where(i == 0, part, dqt[64 * h : 64 * h + 64, :] + part)
            halves.append((dk, dv))
        dk_ref[0, rows, :] = jnp.where(low_half, halves[0][0], halves[1][0]).astype(BF16)
        dv_ref[0, rows, :] = jnp.where(low_half, halves[0][1], halves[1][1]).astype(BF16)
        return carry

    dqt[...] = jnp.zeros_like(dqt)
    lax.fori_loop(0, SEG_MOST // KT, tile, 0)
    dq_ref[0, main, :] = dqt[...].T * 0.125

    rows = pl.ds(SEG_MOST, tail)
    segb = jnp.broadcast_to(segt_ref[...], (128, tail)).T
    halves = []
    for h in range(2):
        hot, pen = seg_codes(segb, 64 - 64 * h + 8)
        ds, dk, dv, k = run(rows, rows, h, (hot.astype(BF16), pen.astype(BF16)))
        halves.append((dk, dv, mm(ds, k, TN)))
    for ref, i in ((dk_ref, 0), (dv_ref, 1)):
        ref[0, rows, :] = jnp.where(low_half, halves[0][i], halves[1][i]).astype(BF16)
    dq_ref[0, rows, :] = jnp.where(low_half, halves[0][2], halves[1][2]) * 0.125
    end_points(plan)


def stage_d(n, segt, q, k, v, ctx, lse, dctx, more):
    mb, t, half = q.shape
    cuts = scatter_cuts(more, 4)
    sds = jax.ShapeDtypeStruct
    return pl.pallas_call(
        partial(kernel_d, n, cuts),
        out_shape=[sds((mb, t, half), F32), sds((mb, t, half), BF16), sds((mb, t, half), BF16)]
        + [sds(w.shape[1:], F32) for w in more],
        grid=(mb, half // 128),
        in_specs=[seg_tail(t - SEG_MOST)] + [pair(t)] * 6 + [ANY] * len(more),
        out_specs=[pair(t)] * 3 + [whole(*w.shape[1:]) for w in more],
        scratch_shapes=[
            pltpu.VMEM((2, t, 128), BF16), pltpu.VMEM((2, t, 128), BF16), pltpu.VMEM((128, SEG_MOST), F32),
        ]
        + (scatter_scratch(n, cuts, more) if more else []),
        compiler_params=params(2, 4 if more else None),
        name="att_bwd",
    )(segt, q, k, v, ctx, lse, dctx, *more)


def kernel_e(
    s_ref, seg_ref, c_far, dconv_far, taps_far, mixed_far, q_far, dq_far, span_far, dk_far, dv_far, depth_far,
    x_far, dres_far, outr_far, wp_ref, wd_ref, wpt_ref, wk_ref, gs_ref,
    gx_far, out_far, gm_ref,
    pad, xs, segb, vt, dcs, dts, e_ref, er_ref, texp, dlt, rt, dm, dl, gacc, gp_ref, gpt_ref, gk_ref, small,
    c_ref, dconv_ref, taps_ref, mixed_ref, q_ref, dq_ref, span_ref, dk_ref, dv_ref, depth_ref,
    x_ref, dres_ref, out_ref_in, gx_ref, out_ref, in_sem, out_sem,
):
    t, d = x_ref.shape[1:]
    far = (
        c_far, dconv_far, taps_far, mixed_far, q_far, dq_far, span_far, dk_far, dv_far, depth_far,
        x_far, dres_far, outr_far,
    )
    near = (
        c_ref, dconv_ref, taps_ref, mixed_ref, q_ref, dq_ref, span_ref, dk_ref, dv_ref, depth_ref,
        x_ref, dres_ref, out_ref_in,
    )

    def fetch(i, block):
        return pltpu.make_async_copy(far[i].at[pl.ds(block, 1)], near[i], in_sem.at[i])

    def arrived(*which):
        for i in which:
            fetch(i, b).wait()

    def done_with(*which):
        @pl.when(b + 1 < pl.num_programs(0))
        def _():
            for i in which:
                fetch(i, b + 1).start()

    def put_back(j, block):
        cols = pl.ds(j * 128, 128)
        return [
            pltpu.make_async_copy(src.at[:, :, cols], dst.at[pl.ds(block, 1), :, cols], out_sem.at[k, j])
            for k, (src, dst) in enumerate(((gx_ref, gx_far), (out_ref, out_far)))
        ]

    half = d // 2
    nch = d // 128
    b = pl.program_id(0)
    s = s_ref[b]

    @pl.when(b == 0)
    def _():
        for i in range(len(far)):
            fetch(i, 0).start()
        fill_expander(e_ref)
        col = lanes((128, 128))
        upper = jnp.where(lax.broadcasted_iota(jnp.int32, (128, 128), 0) >= 64, 1, 0)
        for o in range(KERNEL):
            for j in range(half // 128):
                one = jnp.where(col == upper + (o * 8 + 2 * j), 1.0, 0.0).astype(BF16)
                er_ref[pl.ds(o * half + j * 128, 128), :] = one
        for ref in (xs, dts, dcs):
            n = ref.shape[0]
            ref[:, 0:8, :] = jnp.zeros((n, 8, 128), F32)
            ref[:, t + 8 : t + 16, :] = jnp.zeros((n, 8, 128), F32)
        gp_ref[...] = jnp.zeros_like(gp_ref)
        gpt_ref[...] = jnp.zeros_like(gpt_ref)
        gk_ref[...] = jnp.zeros_like(gk_ref)
        gacc[...] = jnp.zeros_like(gacc)

    fill_segments(seg_ref, segb, vt)
    arrived(0, 1)
    cw = xs
    for j in range(nch // 2):
        cols = pl.ds(j * 128, 128)
        cw[j, 8 : t + 8, :] = c_ref[0, :, cols].astype(F32)
        dcs[j, 8 : t + 8, :] = dconv_ref[0, :, cols]
    done_with(0, 1)

    def dtap_tile(i, carry):
        r0 = pl.multiple_of(i * 128, 128)
        rows = pl.ds(r0, 128)
        acc = None
        for o in range(KERNEL):
            prods = [
                (cw[j, pl.ds(8 + r0 + o - REACH, 128), :] * dcs[j, pl.ds(8 + r0, 128), :]).astype(BF16)
                for j in range(nch // 2)
            ]
            part = mm(jnp.concatenate(prods, 1), er_ref[o * half : (o + 1) * half, :])
            acc = part if acc is None else acc + part
        dlt[:, rows] = acc.T[0:72, :]
        return carry

    lax.fori_loop(0, t // 128, dtap_tile, 0)

    arrived(2)
    taps = [taps_ref[0, o * 8 : o * 8 + 8, :] for o in range(KERNEL)]
    dtaps = [dlt[o * 8 : o * 8 + 8, :] * vt[o] for o in range(KERNEL)]
    mean = taps[0] * dtaps[0]
    for o in range(1, KERNEL):
        mean = mean + taps[o] * dtaps[o]
    for o in range(KERNEL):
        dl[o * 8 : o * 8 + 8, :] = taps[o] * (dtaps[o] - mean)
        tv = taps[o] * vt[o]
        move = (o - REACH) % t
        rt[o * 8 : o * 8 + 8, :] = pltpu.roll(tv, move, 1) if move else tv

    done_with(2)
    arrived(*range(3, 10))

    def point_tile(i, carry):
        r0 = pl.multiple_of(i * 384, 128)
        rows = pl.ds(r0, 384)
        dlog = dl[:, rows].astype(BF16)
        d_mixed = mm(dlog, wk_ref[...], TN)
        gk_ref[...] += mm(dlog, mixed_ref[0, rows, :])
        d_span = (d_mixed * q_ref[0, rows, :].astype(F32)).astype(BF16)
        dm[rows, 0:half] = (dq_ref[0, rows, :] + d_mixed * span_ref[0, rows, :]).astype(BF16)
        dm[rows, half : 2 * half] = dk_ref[0, rows, :]
        dm[rows, 2 * half : 3 * half] = dv_ref[0, rows, :]
        gpt_ref[...] += mm(depth_ref[0, rows, :], d_span, TN)
        d_depth = mm(d_span, wpt_ref[...], NT)
        for j in range(nch):
            dts[j, pl.ds(8 + r0, 384), :] = d_depth[:, j * 128 : (j + 1) * 128]
        return carry

    lax.fori_loop(0, t // 384, point_tile, 0)
    done_with(*range(3, 10))

    def dc_tile(i, carry):
        r0 = pl.multiple_of(i * 128, 128)
        rows = pl.ds(r0, 128)
        texp[...] = expand_taps(rt[:, rows], e_ref)
        for j in range(nch // 2):
            acc = None
            for o in range(KERNEL):
                part = dcs[j, pl.ds(8 + r0 - o + REACH, 128), :] * texp[:, o * half + j * 128 : o * half + (j + 1) * 128]
                acc = part if acc is None else acc + part
            dm[rows, pl.ds(3 * half + j * 128, 128)] = acc.astype(BF16)
        return carry

    lax.fori_loop(0, t // 128, dc_tile, 0)

    arrived(10, 11)
    for j in range(nch):
        xs[j, 8 : t + 8, :] = x_ref[0, :, pl.ds(j * 128, 128)].astype(F32)

    def proj_tile(i, carry):
        r0 = pl.multiple_of(i * 384, 128)
        rows = pl.ds(r0, 384)
        gp_ref[...] += mm(x_ref[0, rows, :], dm[rows, :], TN)
        gx = mm(dm[rows, :], wp_ref[...], NT) + dres_ref[0, rows, :]
        for j in range(nch):
            pad[j, pl.ds(r0, 384), :] = gx[:, j * 128 : (j + 1) * 128]
        return carry

    lax.fori_loop(0, t // 384, proj_tile, 0)

    done_with(10, 11)

    def depth_tile(r0, masked):
        masks = mask_rows(segb, r0, 128) if masked else None
        for j in range(nch):
            acc = pad[j, pl.ds(r0, 128), :]
            own = dts[j, pl.ds(8 + r0, 128), :]
            for o in range(KERNEL):
                w = wd_ref[KERNEL - 1 - o : KERNEL - o, pl.ds(j * 128, 128)]
                near = dts[j, pl.ds(8 + r0 + o - REACH, 128), :]
                xw = xs[j, pl.ds(8 + r0 + o - REACH, 128), :]
                if masked:
                    near = near * masks[o]
                    xw = xw * masks[o]
                acc = acc + near * w
                term = (own * xw).reshape(16, 8, 128)
                gacc[o, :, pl.ds(j * 128, 128)] += jnp.sum(term, 0)
            pad[j, pl.ds(r0, 128), :] = acc

    masked_tiles(t, depth_tile)

    arrived(12)

    @pl.when(b > 0)
    def _():
        for j in range(nch):
            for copy in put_back(j, b - 1):
                copy.wait()

    for j in range(nch):
        cols = pl.ds(j * 128, 128)
        pad[j, pl.ds(t, 128), :] = pad[j, 0:128, :]
        back = t - s
        first = pl.ds(back, 128)
        gx_ref[0, :, cols] = xs[j, 8 : t + 8, :]
        xs[j, 0:128, :] = pad[j, first, :]
        gx_ref[0, 0:128, cols] = xs[j, 0:128, :]
        gx_ref[0, 128:, cols] = pad[j, pl.ds(128 - s, t - 128), :]
        pad[j, 0:t, :] = out_ref_in[0, :, cols].astype(F32)
        pad[j, pl.ds(t, 128), :] = pad[j, 0:128, :]
        out_ref[0, 0:128, cols] = pad[j, first, :].astype(BF16)
        out_ref[0, 128:, cols] = pad[j, pl.ds(128 - s, t - 128), :].astype(BF16)
        for copy in put_back(j, b):
            copy.start()
    done_with(12)

    @pl.when(b == pl.num_programs(0) - 1)
    def _():
        n = gm_ref.shape[0]
        rows = d // n
        small[...] = jnp.zeros_like(small)
        for o in range(KERNEL):
            small[o : o + 1, :] = jnp.sum(gacc[o], 0, keepdims=True)
        small[16:24, :] = gs_ref[...]
        row = lax.broadcasted_iota(jnp.int32, (128, 72), 0)
        col = lax.broadcasted_iota(jnp.int32, (128, 72), 1)
        order = jnp.where((row < HEADS * KERNEL) & (row % KERNEL * 8 + row // KERNEL == col), 1.0, 0.0).astype(BF16)
        gk = mm(order, gk_ref[...].astype(BF16)).astype(BF16)
        gk = mm(gk, piece_rows(d), NT)
        for j in range(nch):
            cols = pl.ds(j * 128, 128)
            pad[0, cols, :] = small[:, cols].T
            pad[1, cols, :] = gk[:, j * 128 : (j + 1) * 128].T

        def emit(p, c):
            at = pl.ds(pl.multiple_of(p * rows, 8), rows)
            gp = gp_ref[at, :]
            parts = [gp[:, j * half : (j + 1) * half] for j in range(gp.shape[1] // half)] + [gpt_ref[at, :]]
            parts.append(jnp.concatenate([pad[0, at, :], pad[1, at, :], jnp.zeros((rows, half - 256), F32)], 1))
            gm_ref[p] = jnp.concatenate(parts, 0).astype(BF16)
            return c

        lax.fori_loop(0, n, emit, 0)
        for j in range(nch):
            for copy in put_back(j, b):
                copy.wait()


def stage_e(n, s, segr, x, out_r, dres, dconv, dq, dk, dv, q, c, depth, span, mixed, taps, wp, wd, wpt, wk, gs):
    mb, t, d = x.shape
    half = d // 2
    packed = (d * 2 * d + d * half) // (n * half) + d // n
    sds = jax.ShapeDtypeStruct

    blocks = (c, dconv, taps, mixed, q, dq, span, dk, dv, depth, x, dres, out_r)
    return pl.pallas_call(
        kernel_e,
        out_shape=[
            sds((mb, t, d), F32), sds((mb, t, d), BF16), sds((n, packed, half), BF16),
        ],
        grid_spec=pltpu.PrefetchScalarGridSpec(
            num_scalar_prefetch=1,
            grid=(mb,),
            in_specs=[pl.BlockSpec((pl.Squeezed(), 1, t), lambda b, *_: (b, 0, 0))]
            + [ANY] * len(blocks)
            + [whole(*w.shape) for w in (wp, wd, wpt, wk, gs)],
            out_specs=[ANY, ANY, whole(n, packed, half)],
            scratch_shapes=[
                pltpu.VMEM((d // 128, t + 128, 128), F32),
                pltpu.VMEM((d // 128, t + 16, 128), F32),
                pltpu.VMEM((t + 16, 128), F32),
                pltpu.VMEM((KERNEL, 8, t), F32),
                pltpu.VMEM((half // 128, t + 16, 128), F32),
                pltpu.VMEM((d // 128, t + 16, 128), F32),
                pltpu.VMEM((144, KERNEL * half), BF16),
                pltpu.VMEM((KERNEL * half, 128), BF16),
                pltpu.VMEM((128, KERNEL * half), F32),
                pltpu.VMEM((72, t), F32),
                pltpu.VMEM((72, t), F32),
                pltpu.VMEM((t, 2 * d), BF16),
                pltpu.VMEM((72, t), F32),
                pltpu.VMEM((KERNEL, 8, d), F32),
                pltpu.VMEM(wp.shape, F32),
                pltpu.VMEM(wpt.shape, F32),
                pltpu.VMEM((72, half), F32),
                pltpu.VMEM((128, d), F32),
            ]
            + [pltpu.VMEM((1,) + v.shape[1:], v.dtype) for v in blocks]
            + [
                pltpu.VMEM((1, t, d), F32),
                pltpu.VMEM((1, t, d), BF16),
                pltpu.SemaphoreType.DMA((len(blocks),)),
                pltpu.SemaphoreType.DMA((2, d // 128)),
            ],
        ),
        compiler_params=params(1),
        name="mix_bwd",
    )(s, segr, *blocks, wp, wd, wpt, wk, gs)


def prep_kernel(seg_ref, wd_ref, wk_ref, norm_ref, s_ref, segr_ref, small_ref, flip):
    mb, t = seg_ref.shape
    span = t - SEG_MOST + 1
    pos = lanes((1, t))
    for b in range(mb):
        row = seg_ref[b : b + 1, :].astype(F32)
        later = pltpu.roll(jnp.broadcast_to(row, (8, t)), t - (SEG_MOST - 1), 1)
        hit = (later[0:1, :] == row) & (pos < span)
        s = jnp.sum(jnp.where(hit, pos.astype(F32), 0.0)).astype(jnp.int32)
        s_ref[b] = s
        segr_ref[b] = pltpu.roll(jnp.broadcast_to(row, (8, t)), t - s, 1)[0:1, :]
    flip[...] = jnp.zeros_like(flip)
    rows = wd_ref.shape[1]
    flip[0:KERNEL, 0:rows] = wd_ref[...].astype(F32)
    flip[16:20, 0:rows] = norm_ref[...].astype(F32)
    row = lax.broadcasted_iota(jnp.int32, (8 * KERNEL, HEADS * KERNEL), 0)
    col = lanes((8 * KERNEL, HEADS * KERNEL))
    order = jnp.where(col % KERNEL * 8 + col // KERNEL == row, 1.0, 0.0).astype(BF16)
    heads = mm(order, wk_ref[...]).astype(BF16)
    flip[32 : 32 + 8 * KERNEL, 0:rows] = mm(heads, piece_rows(rows), NT)
    small_ref[...] = flip[...].T[0:rows, :]


def prep(segments, w_depth, w_kernel, norms):
    mb, t = segments.shape
    rows = w_depth.shape[0]
    sds = jax.ShapeDtypeStruct
    vmem = pl.BlockSpec(memory_space=pltpu.VMEM)
    return pl.pallas_call(
        prep_kernel,
        out_shape=[sds((mb,), jnp.int32), sds((mb, 1, t), F32), sds((rows, 128), F32)],
        in_specs=[vmem] * 4,
        out_specs=[pl.BlockSpec(memory_space=pltpu.SMEM), vmem, vmem],
        scratch_shapes=[pltpu.VMEM((128, -(-rows // 128) * 128), F32)],
        name="prep",
    )(segments, w_depth.T, w_kernel.T, norms)


def finish_kernel(f_ref, m_ref, gp_ref, gdep_ref, gpt_ref, gk_ref, go_ref, gi_ref, gd_ref, gs_ref, flip):
    half = f_ref.shape[1]
    rows = gp_ref.shape[0]
    tall = gd_ref.shape[0]
    gd_ref[...] = f_ref[0:tall, :]
    for j in range(gi_ref.shape[1] // half):
        gi_ref[:, j * half : (j + 1) * half] = f_ref[tall + j * rows : tall + (j + 1) * rows, :]
    tall = tall + rows * (gi_ref.shape[1] // half)
    for j in range(2):
        go_ref[:, j * half : (j + 1) * half] = f_ref[tall + j * rows : tall + (j + 1) * rows, :]
    wide = gp_ref.shape[1] // half
    for j in range(wide):
        gp_ref[:, j * half : (j + 1) * half] = m_ref[j * rows : (j + 1) * rows, :]
    gpt_ref[...] = m_ref[wide * rows : (wide + 1) * rows, :]
    flip[...] = jnp.zeros_like(flip)
    flip[0:rows, :] = m_ref[(wide + 1) * rows : (wide + 2) * rows, 0:256]
    first = flip[:, 0:128].T
    gdep_ref[...] = first[0:KERNEL, 0:rows]
    gs_ref[...] = first[16:24, 0:rows]
    gk_ref[...] = flip[:, 128:256].T[0 : HEADS * KERNEL, 0 : rows // 2]


def finish(n, d, hid, f, m):
    half = d // 2
    sds = jax.ShapeDtypeStruct
    rows = d // n
    return pl.pallas_call(
        finish_kernel,
        out_shape=[
            sds((rows, 2 * d), F32), sds((KERNEL, rows), F32), sds((rows, half), F32), sds((HEADS * KERNEL, half // n), F32),
            sds((rows, d), F32), sds((rows, hid), F32), sds((2 * hid // n, half), F32), sds((8, rows), F32),
        ],
        scratch_shapes=[pltpu.VMEM((128, 256), F32)],
        name="finish",
    )(f, m)


def side_by_side(block, parts):
    units, _, cols = block.shape
    return block.reshape(units, parts, PIECE, cols).transpose(0, 2, 1, 3).reshape(units * PIECE, parts * cols)


def native_sums(gf, gm, d, hid):
    gf, gm = gf.astype(F32), gm.astype(F32)
    half = d // 2
    tall = 2 * hid * PIECE // d
    wide = hid // half * PIECE
    many_p = 2 * d // half
    g_down = gf[:, :tall].reshape(-1, half)
    g_in = side_by_side(gf[:, tall : tall + wide], hid // half)
    g_out = side_by_side(gf[:, tall + wide :], 2)
    g_proj = side_by_side(gm[:, : many_p * PIECE], many_p)
    g_point = gm[:, many_p * PIECE : (many_p + 1) * PIECE].reshape(-1, half)
    small = gm[:, (many_p + 1) * PIECE :]
    g_kernel = small[:, : PIECE // 2, 128 : 128 + HEADS * KERNEL].reshape(half, -1)
    small = small[:, :, 0:24].reshape(d, -1)
    grads = [g_proj, small[:, :KERNEL], g_point, g_kernel, g_out, g_in, g_down, small[:, 16:]]
    return [lax.psum_scatter(g, "tok", scatter_dimension=0, tiled=True) for g in grads]


def rows_of(w):
    return w.reshape(-1, w.shape[-1])


def shards(n, tokens, segments, cotangent, w_proj, w_depth, w_point, w_kernel, w_out, g1, b1, w_in, w_down, g2, b2):
    d = tokens.shape[-1]
    hid = w_in.shape[1]
    units = d // PIECE
    own = n == units
    norms = [g1, b1, g2, b2]
    if own:
        more_a, more_b = [w_out, w_in], [w_in, w_down]
    else:
        given = [w_proj, w_in, w_down, w_point, w_out, w_depth, w_kernel] + norms
        wp, wi, wdn, wpt, wo, w_depth, w_kernel, *norms = [lax.all_gather(w, "tok", axis=0, tiled=True) for w in given]
        more_a = more_b = []
    s, segr, small = prep(segments[:, 0], w_depth, w_kernel, jnp.stack(norms))
    xr, cotr, wd_rows, wk_rows, *got = stage_front(n, s, tokens, cotangent, small, w_proj, w_point, own)
    if own:
        wp, wpt = (rows_of(w) for w in got)
    q, k, v, c, depth, span, mixed, taps, conv, *got_a = stage_a(n, segr, xr, wp, wd_rows, wpt, wk_rows, more_a)
    ctx, lse, *got_b = stage_b(n, segr, q, k, v, more_b)
    if own:
        wo, wi_a, wi_b, wdn = (rows_of(w) for w in got_a + got_b)
    else:
        wi_a, wi_b = jnp.split(wi, 2, 1)
    out_r, dres, dctx, dconv, gf, g_small = stage_c(units, ctx, conv, xr, cotr, wo, wi_a, wi_b, wdn, wd_rows)
    dq, dk, dv, *sums = stage_d(n, segr, q, k, v, ctx, lse, dctx, [gf] if own else [])
    gx, out, gm = stage_e(
        units, s, segr, xr, out_r, dres, dconv, dq, dk, dv, q, c, depth, span, mixed, taps, wp, wd_rows, wpt, wk_rows,
        g_small,
    )
    if own:
        sums = finish(n, d, hid, sums[0], scatter_all(n, 1, [gm], 6)[0])
        sums = [v.T if i in (1, 3, 7) else v for i, v in enumerate(sums)]
    else:
        sums = native_sums(gf, gm, d, hid)
    g_proj, g_depth, g_point, g_kernel, g_out, g_in, g_down, g_vec = sums
    return (
        out, gx, g_proj, g_depth, g_point, g_kernel, g_out, g_vec[:, 0], g_vec[:, 1], g_in, g_down,
        g_vec[:, 2], g_vec[:, 3],
    )


def solution(mesh):
    rows, vec, act = P("tok", None), P("tok"), P(None, "tok", None)
    in_specs = (act, act, act, rows, rows, rows, rows, rows, vec, vec, rows, rows, vec, vec)
    out_specs = (act, act, rows, rows, rows, rows, rows, vec, vec, rows, rows, vec, vec)
    run = partial(shards, mesh.shape["tok"])
    return jax.shard_map(run, mesh=mesh, in_specs=in_specs, out_specs=out_specs, check_vma=False)
```

```python
import math
from functools import partial

import jax
import jax.numpy as jnp
from jax import lax
from jax.experimental import pallas as pl
from jax.experimental.pallas import tpu as pltpu
from jax.sharding import PartitionSpec as P

HEADS = 6
KERNEL = 9
REACH = 4
SEG_MOST = 1024
NORM_EPS = 1e-12
F32 = jnp.float32
BF16 = jnp.bfloat16
NT = (((1,), (1,)), ((), ()))
NN = (((1,), (0,)), ((), ()))
TN = (((0,), (0,)), ((), ()))
VMEM_CAP = 62 * 1024 * 1024
MESH = pl.DeviceIdType.MESH
PIECE = 24


def mm(a, b, dims=NN):
    return lax.dot_general(a, b, dims, preferred_element_type=F32)


def lanes(shape):
    return lax.broadcasted_iota(jnp.int32, shape, 1)


def split2(v):
    hi = v.astype(BF16)
    return hi, (v - hi.astype(F32)).astype(BF16)


def split3(v):
    hi = v.astype(BF16)
    rest = v - hi.astype(F32)
    mid = rest.astype(BF16)
    return hi, mid, (rest - mid.astype(F32)).astype(BF16)


def partner(me, bit):
    return me + (1 - 2 * lax.rem(lax.div(me, bit), 2)) * bit


def bit_of(me, bit):
    return lax.rem(lax.div(me, bit), 2)


def bit_orders(n):
    one = [1 << b for b in range(n.bit_length() - 1)]
    two = one[:1] + one[2:3] + one[1:2] + one[3:] if len(one) > 2 else one
    return one, two


def greet(n):
    me = lax.axis_index("tok")
    barrier = pltpu.get_barrier_semaphore()
    bits = bit_orders(n)[0]
    for bit in bits:
        pl.semaphore_signal(barrier, inc=1, device_id=(partner(me, bit),), device_id_type=MESH)
    pl.semaphore_wait(barrier, len(bits))


class Gather:
    def __init__(self, src, dst, take, part, order, send, recv, own):
        self.src, self.all, self.part, self.order = src.at[take], dst, part, order[::-1]
        self.send, self.recv, self.own = send, recv, own
        self.me = lax.axis_index("tok")

    def sizes(self):
        one = math.prod(self.src.shape) * jnp.dtype(self.all.dtype).itemsize
        return [one << i for i in range(len(self.order))]

    def held(self, s):
        free = self.order[:s]
        bits = [1 << b for b in reversed(range(len(self.order)))]
        return self.all.at[tuple(ALL if bit in free else bit_of(self.me, bit) for bit in bits) + self.part]

    def wait(self, sem, s):
        ref = self.held(s)
        pltpu.make_async_copy(ref, ref, sem.at[s]).wait()

    def step(self, s):
        if s == 0:
            pltpu.make_async_copy(self.src, self.held(0), self.own).start()
        elif s == 1:
            pltpu.make_async_copy(self.src, self.held(0), self.own).wait()
        if s > 0:
            self.wait(self.recv, s - 1)
        if s < len(self.order):
            pltpu.make_async_remote_copy(
                src_ref=self.held(s) if s else self.src,
                dst_ref=self.held(s),
                send_sem=self.send.at[s],
                recv_sem=self.recv.at[s],
                device_id=(partner(self.me, self.order[s]),),
                device_id_type=MESH,
            ).start()
        else:
            for i in range(s):
                self.wait(self.send, i)


def halves(order, s):
    left = sorted(set(order) - set(order[:s]), reverse=True)
    at = left.index(order[s])
    return 1 << at, 1 << (len(left) - 1 - at)


class Scatter:
    def __init__(self, n, src, first, out, mine, got, order, send, recv, own):
        self.n, self.src, self.mine, self.got, self.order, self.out = n, src, mine, got, order, out
        self.rows = pl.ds(first, mine.shape[1])
        self.send, self.recv, self.own = send, recv, own
        self.me = lax.axis_index("tok")

    def sizes(self):
        one = math.prod(self.mine.shape[1:]) * 2
        return [one * (self.n >> (i + 1)) for i in range(len(self.order))]

    def side(self, s, keep):
        hi, lo = halves(self.order, s)
        bit = bit_of(self.me, self.order[s])
        which = bit if keep else 1 - bit
        if s == 0:
            view = self.src.reshape((hi, 2, lo) + self.src.shape[1:])
            return view.at[:, which, :, self.rows]
        held = self.got[s - 1]
        return held.reshape((hi, 2, lo) + held.shape[1:]).at[:, which]

    def there(self, ref, s):
        hi, lo = halves(self.order, s)
        return ref.reshape((hi, lo) + ref.shape[1:])

    def send_copy(self, s):
        return pltpu.make_async_remote_copy(
            src_ref=self.side(s, False),
            dst_ref=self.there(self.got[s], s),
            send_sem=self.send.at[s],
            recv_sem=self.recv.at[s],
            device_id=(partner(self.me, self.order[s]),),
            device_id_type=MESH,
        )

    def own_copy(self):
        return pltpu.make_async_copy(self.side(0, True), self.there(self.mine, 0), self.own)

    def add(self, s):
        self.send_copy(s).wait_recv()
        got = self.got[s]
        if s == 0:
            self.own_copy().wait()

            def first(k, c):
                got[k] = (got[k].astype(F32) + self.mine[k].astype(F32)).astype(BF16)
                return c

            lax.fori_loop(0, got.shape[0], first, 0)
            return
        hi, lo = halves(self.order, s)
        held = self.got[s - 1]
        bit = bit_of(self.me, self.order[s])

        def one(k, c):
            for i in range(lo):
                to, at = k * lo + i, (k * 2 + bit) * lo + i
                got[to] = (got[to].astype(F32) + held[at].astype(F32)).astype(BF16)
            return c

        if s < len(self.order) - 1:
            lax.fori_loop(0, hi, one, 0)
        else:
            self.out[self.rows, :] = got[0].astype(F32) + held[bit].astype(F32)

    def step(self, s):
        if s > 0:
            self.add(s - 1)
        if s < len(self.order):
            self.send_copy(s).start()
        if s == 0:
            self.own_copy().start()
        if s == len(self.order):
            for i in range(s):
                self.send_copy(i).wait_send()


ANY = pl.BlockSpec(memory_space=pl.ANY)


def remote(cid):
    return pltpu.CompilerParams(collective_id=cid, has_side_effects=True, vmem_limit_bytes=VMEM_CAP)


GATHER_PACE = (2.5, 90e3)
SCATTER_PACE = (2.2, 95e3)


def schedule(parts, last, spots, pace):
    stage, rate = pace
    cost = {1: 1 / (4 * rate), 2: 2 / rate, 4: 2 / rate, 8: 2 / rate}
    link = [{1: 0, 2: 1, 4: 2}.get(bit, 3) for bit in range(1 << last)]
    free, ready, at = [0.0] * 4, [0.0] * len(parts), [0] * len(parts)
    plan = []
    for now in spots:
        due = []
        for p, (bits, sizes) in enumerate(parts):
            if at[p] <= last and ready[p] <= now:
                due.append((p, at[p]))
                if at[p] < last:
                    bit = bits[at[p]]
                    begin = max(now, free[link[bit]])
                    free[link[bit]] = begin + sizes[at[p]] * cost.get(bit, 4 / rate)
                    ready[p] = free[link[bit]] + stage
                at[p] += 1
        plan.append(due)
    plan.append([(p, i) for i in range(last + 1) for p in range(len(parts)) if at[p] <= i])
    return plan


class Timed:
    def __init__(self, n, parts, spots, pace):
        self.parts = parts
        self.last = n.bit_length() - 1
        self.ticks = self.last + 1
        self.plan = [[(p, t) for p in range(len(parts))] for t in range(self.ticks)]
        if spots is not None:
            self.plan = schedule([(p.order, p.sizes()) for p in parts], self.last, spots, pace)
            self.ticks = len(self.plan)

    def tick(self, t):
        for p, i in self.plan[t]:
            self.parts[p].step(i)


ALL = slice(None)


def pieces(wide, count, rows=False):
    size = wide // count
    cuts = [pl.ds(i * size, size) for i in range(count)]
    return [(c, ALL) if rows else (ALL, c) for c in cuts]


def gathers(n, srcs, dsts, layout, sems, spots=None):
    send, recv, own = sems
    orders = bit_orders(n)
    return Timed(
        n,
        [
            Gather(srcs[a], dsts[a], parts[0], parts[-1], orders[i % 2], send.at[i], recv.at[i], own.at[i])
            for i, (a, *parts) in enumerate(layout)
        ],
        spots,
        GATHER_PACE,
    )


def gather_sems(n, layout):
    stages, count = n.bit_length() - 1, len(layout)
    dma = pltpu.SemaphoreType.DMA
    return [dma((count, stages)), dma((count, stages)), dma((count,))]


def gathered(n, shards):
    return [jax.ShapeDtypeStruct((2,) * (n.bit_length() - 1) + w.shape, w.dtype) for w in shards]


def split_rows(rows, parts):
    tiles = rows // 16
    cuts = [tiles * i // parts * 16 for i in range(parts + 1)]
    return [(a, b - a) for a, b in zip(cuts, cuts[1:]) if b > a]


def scatters(n, cuts, srcs, outs, refs, spots=None):
    total, stages = len(cuts), n.bit_length() - 1
    accs, gots, (send, recv, own) = refs[:total], refs[total:-3], refs[-3:]
    gots = [gots[stages * j : stages * (j + 1)] for j in range(total)]
    orders = bit_orders(n)
    return Timed(
        n,
        [
            Scatter(n, srcs[i], a, outs[i], accs[j], gots[j], orders[j % 2], send.at[j], recv.at[j], own.at[j])
            for j, (i, a, r) in enumerate(cuts)
        ],
        spots,
        SCATTER_PACE,
    )


def scatter_cuts(packed, parts):
    return [(i, a, r) for i, w in enumerate(packed) for a, r in split_rows(w.shape[1], parts)]


def scatter_scratch(n, cuts, packed):
    total, stages = len(cuts), n.bit_length() - 1
    dma = pltpu.SemaphoreType.DMA
    bufs = [(r, packed[i].shape[2]) for i, a, r in cuts]
    return (
        [pltpu.VMEM((n // 2,) + b, BF16) for b in bufs]
        + [pltpu.VMEM((n >> (s + 1),) + b, BF16) for b in bufs for s in range(stages)]
        + [dma((total, stages)), dma((total, stages)), dma((total,))]
    )


def scatter_all(n, cid, packed, parts):
    cuts = scatter_cuts(packed, parts)
    count = len(packed)

    def kernel(*refs):
        greet(n)
        plan = scatters(n, cuts, refs[:count], refs[count : 2 * count], refs[2 * count :])
        for t in range(plan.ticks):
            plan.tick(t)

    return pl.pallas_call(
        kernel,
        out_shape=[jax.ShapeDtypeStruct(w.shape[1:], F32) for w in packed],
        in_specs=[ANY] * count,
        out_specs=[pl.BlockSpec(memory_space=pltpu.VMEM)] * count,
        scratch_shapes=scatter_scratch(n, cuts, packed),
        compiler_params=remote(cid),
        name="scatter",
    )(*packed)


def expand_taps(tap_rows, e_ref):
    hi, lo = split2(tap_rows)
    both = jnp.concatenate([hi, lo], 0)
    return mm(both, e_ref[...], TN)


def fill_expander(e_ref):
    half = e_ref.shape[1] // KERNEL
    shape = (72, 128)
    row = lax.broadcasted_iota(jnp.int32, shape, 0)
    upper = jnp.where(lanes(shape) >= 64, 1, 0)
    for o in range(KERNEL):
        for j in range(half // 128):
            one = jnp.where(row == upper + (o * 8 + 2 * j), 1.0, 0.0).astype(BF16)
            cols = pl.ds(o * half + j * 128, 128)
            e_ref[0:72, cols] = one
            e_ref[72:144, cols] = one


def mask_rows(segb_ref, r0, rows):
    own = segb_ref[pl.ds(8 + r0, rows), :]
    return [
        jnp.where(segb_ref[pl.ds(8 + r0 + o - REACH, rows), :] == own, 1.0, 0.0)
        for o in range(KERNEL)
    ]


def fill_segments(seg_ref, segb_ref, vt_ref):
    t = seg_ref.shape[-1]
    row = seg_ref[...]
    if segb_ref is not None:
        wide = jnp.broadcast_to(row, (128, t))
        segb_ref[0:8, :] = jnp.full((8, 128), -1.0, F32)
        segb_ref[t + 8 : t + 16, :] = jnp.full((8, 128), -1.0, F32)
        segb_ref[8 : t + 8, :] = wide.T
    if vt_ref is None:
        return
    tall = jnp.broadcast_to(row, (8, t))
    pos = lanes((8, t))
    for o in range(KERNEL):
        d = o - REACH
        moved = pltpu.roll(tall, (-d) % t, 1) if d else tall
        inside = (pos + d >= 0) & (pos + d < t)
        vt_ref[o] = jnp.where(inside & (moved == tall), 1.0, 0.0)


def masked_tiles(t, body, between=None):
    full = SEG_MOST // 128

    def inner(i, c):
        body(pl.multiple_of(i * 128, 128), False)
        return c

    lax.fori_loop(1, full - 1, inner, 0)
    if between is not None:
        between()

    def edge(i, c):
        idx = jnp.where(i == 0, 0, i + full - 2)
        body(pl.multiple_of(idx * 128, 128), True)
        return c

    lax.fori_loop(0, t // 128 - full + 2, edge, 0)


def piece_rows(d):
    small = PIECE // 2
    row = lax.broadcasted_iota(jnp.int32, (d, d // 2), 0)
    col = lanes((1, d // 2))
    return jnp.where(row == col + col // small * small, 1.0, 0.0).astype(BF16)


def unpack_small(sm_ref, wd_ref, wk_ref):
    d = sm_ref.shape[0]
    parts = [sm_ref[j * 128 : (j + 1) * 128, :].T for j in range(d // 128)]
    tall = jnp.concatenate(parts, 1)
    wd_ref[...] = tall[0:24, :]
    wk_ref[...] = mm(tall[32:104, :].astype(BF16), piece_rows(d), NN).astype(BF16)


def front_layout(d, half):
    cols = pieces(2 * d, 6)
    rest = [(1, (ALL, pl.ds(0, 128))), (1, (ALL, pl.ds(128, half - 128)))]
    return [(0, cols[0]), (0, cols[1]), (2, (ALL, ALL))] + [(0, c) for c in cols[2:]] + rest


def kernel_front(n, layout, *refs):
    s_ref, x_ref, cot_ref = refs[:3]
    if layout:
        sm_src, wp_src, wpt_src = refs[3:6]
        xr_ref, cotr_ref, wd_ref, wk_ref, wp_far, wpt_far = refs[6:12]
        raw, sm, *sems = refs[12:]
        plan = gathers(n, (wp_src, wpt_src, sm_src), (wp_far, wpt_far, sm), layout, sems)
    else:
        sm_src = refs[3]
        xr_ref, cotr_ref, wd_ref, wk_ref = refs[4:8]
        raw, sm = refs[8:]
        plan = None
    t, d = x_ref.shape[1:]
    nch = d // 128
    b = pl.program_id(0)
    s = s_ref[b]
    end = pl.num_programs(0) - 1
    point(b == 0, lambda: greet(n), plan, 0)
    for src, dst in ((cot_ref, cotr_ref), (x_ref, xr_ref)):
        for j in range(nch):
            col = pl.ds(j * 128, 128)
            raw[0:t, :] = src[0, :, col].astype(F32)
            raw[t : t + 128, :] = src[0, 0:128, col].astype(F32)
            dst[0, :, col] = raw[pl.ds(s, t), :].astype(BF16)

    point(b == 0, None, plan, 1)

    @pl.when(b == end)
    def _():
        if plan is not None:
            for i in range(2, plan.ticks):
                plan.tick(i)
            unpack_small(sm.reshape(d, 128), wd_ref, wk_ref)
        else:
            unpack_small(sm_src, wd_ref, wk_ref)


def stage_front(n, s, x, cot, small, wp, wpt, own):
    mb, t, d = x.shape
    half = d // 2
    sds = jax.ShapeDtypeStruct
    layout = front_layout(d, half) if own else []
    more = [wp, wpt] if own else []
    out = [((mb, t, d), BF16)] * 2
    return pl.pallas_call(
        partial(kernel_front, n, layout),
        out_shape=[sds(*o) for o in out] + [sds((24, d), F32), sds((72, half), BF16)] + gathered(n, more),
        grid_spec=pltpu.PrefetchScalarGridSpec(
            num_scalar_prefetch=1,
            grid=(mb,),
            in_specs=[per_block(t, d), per_block(t, d), ANY if own else whole(*small.shape)] + [ANY] * len(more),
            out_specs=[per_block(t, d)] * 2 + [whole(24, d), whole(72, half)] + [ANY] * len(more),
            scratch_shapes=[
                pltpu.VMEM((t + 128, 128), F32),
                pltpu.VMEM((2,) * (n.bit_length() - 1) + (PIECE, 128) if own else (8, 128), F32),
            ]
            + (gather_sems(n, layout) if own else []),
        ),
        compiler_params=params(1, 0 if own else None),
        name="front",
    )(s, x, cot, small, *more)


A_SPOTS = [block + at for block in (0.0, 16.5) for at in (0.0, 3.0, 6.0, 7.4, 8.6, 11.0, 12.3, 13.6)]


def kernel_a(n, layout, count, *refs):
    seg_ref, xr_ref, wp_ref, wd_ref, wpt_ref, wk_ref = refs[:6]
    srcs, refs = refs[6 : 6 + count], refs[6 + count :]
    q_ref, k_ref, v_ref, c_ref, depth_ref, span_ref, mixed_ref, taps_ref, conv_ref = refs[:9]
    dsts, refs = refs[9 : 9 + count], refs[9 + count :]
    xs, segb, vt, cs, lt, e_ref, texp, *sems = refs
    plan = gathers(n, srcs, dsts, layout, sems, A_SPOTS) if count else None
    t, d = xr_ref.shape[1:]
    half = d // 2
    nch = d // 128
    b = pl.program_id(0)
    end = pl.num_programs(0) - 1
    if plan is not None:
        @pl.when(b == 0)
        def _():
            greet(n)

    def spot(i, loop, every):
        for at in range(3):
            for block in range(2):
                point((b == block) & (i == at * every), None, plan, 8 * block + 2 + 3 * loop + at)

    def early(at):
        for block in range(2):
            point(b == block, None, plan, 8 * block + at)

    early(0)

    @pl.when(b == 0)
    def _():
        fill_expander(e_ref)
        cs[:, 0:8, :] = jnp.zeros((nch // 2, 8, 128), F32)
        cs[:, t + 8 : t + 16, :] = jnp.zeros((nch // 2, 8, 128), F32)
        xs[:, 0:8, :] = jnp.zeros((nch, 8, 128), F32)
        xs[:, t + 8 : t + 16, :] = jnp.zeros((nch, 8, 128), F32)

    fill_segments(seg_ref, segb, vt)
    for j in range(nch):
        xs[j, 8 : t + 8, :] = xr_ref[0, :, pl.ds(j * 128, 128)].astype(F32)

    def depth_tile(r0, masked):
        masks = mask_rows(segb, r0, 128) if masked else None
        for j in range(nch):
            acc = None
            for o in range(KERNEL):
                part = xs[j, pl.ds(8 + r0 + o - REACH, 128), :]
                w = wd_ref[o : o + 1, pl.ds(j * 128, 128)]
                part = part * (masks[o] * w) if masked else part * w
                acc = part if acc is None else acc + part
            depth_ref[0, pl.ds(r0, 128), pl.ds(j * 128, 128)] = acc.astype(BF16)

    masked_tiles(t, depth_tile, lambda: early(1))

    def proj_tile(i, carry):
        spot(i, 0, 1)
        r0 = pl.multiple_of(i * 384, 128)
        rows = pl.ds(r0, 384)
        merged = mm(xr_ref[0, rows, :], wp_ref[...]).astype(BF16)
        q = merged[:, 0:half]
        q_ref[0, rows, :] = q
        k_ref[0, rows, :] = merged[:, half : 2 * half]
        v_ref[0, rows, :] = merged[:, 2 * half : 3 * half]
        c = merged[:, 3 * half :]
        c_ref[0, rows, :] = c
        for j in range(nch // 2):
            cs[j, pl.ds(8 + r0, 384), :] = c[:, j * 128 : (j + 1) * 128].astype(F32)
        span = mm(depth_ref[0, rows, :], wpt_ref[...])
        span_ref[0, rows, :] = span
        mixed = (span * q.astype(F32)).astype(BF16)
        mixed_ref[0, rows, :] = mixed
        lt[:, rows] = mm(wk_ref[...], mixed, NT)
        return carry

    lax.fori_loop(0, t // 384, proj_tile, 0)

    logits = [lt[o * 8 : o * 8 + 8, :] for o in range(KERNEL)]
    top = logits[0]
    for o in range(1, KERNEL):
        top = jnp.maximum(top, logits[o])
    exps = [jnp.exp(v - top) for v in logits]
    total = exps[0]
    for o in range(1, KERNEL):
        total = total + exps[o]
    inv = 1.0 / total
    for o in range(KERNEL):
        tap = exps[o] * inv
        taps_ref[0, o * 8 : o * 8 + 8, :] = tap
        lt[o * 8 : o * 8 + 8, :] = tap * vt[o]

    def conv_tile(i, carry):
        spot(i, 1, 3)
        r0 = pl.multiple_of(i * 128, 128)
        rows = pl.ds(r0, 128)
        texp[...] = expand_taps(lt[:, rows], e_ref)
        for j in range(nch // 2):
            acc = None
            for o in range(KERNEL):
                part = cs[j, pl.ds(8 + r0 + o - REACH, 128), :] * texp[:, o * half + j * 128 : o * half + (j + 1) * 128]
                acc = part if acc is None else acc + part
            conv_ref[0, rows, pl.ds(j * 128, 128)] = acc.astype(BF16)
        return carry

    lax.fori_loop(0, t // 128, conv_tile, 0)
    point(b == end, None, plan, len(A_SPOTS))


def whole(*shape):
    return pl.BlockSpec(shape, lambda *_: (0,) * len(shape), pipeline_mode=pl.Buffered(1))


def per_block(*shape):
    return pl.BlockSpec((1,) + shape, lambda b, *_: (b,) + (0,) * len(shape))


def params(n, cid=None):
    more = {} if cid is None else {"collective_id": cid, "has_side_effects": True}
    return pltpu.CompilerParams(dimension_semantics=("arbitrary",) * n, vmem_limit_bytes=VMEM_CAP, **more)


def point(when, first, plan, s):
    if plan is None or not plan.plan[s]:
        return

    @pl.when(when)
    def _():
        if first is not None:
            first()
        plan.tick(s)


def stage_a(n, segr, xr, wp, wd, wpt, wk, more):
    mb, t, d = xr.shape
    half = d // 2
    sds = jax.ShapeDtypeStruct
    out = [
        ((t, half), BF16), ((t, half), BF16), ((t, half), BF16), ((t, half), BF16), ((t, d), BF16),
        ((t, half), F32), ((t, half), BF16), ((72, t), F32), ((t, half), BF16),
    ]
    layout, far = [], []
    if more:
        hid = more[1].shape[1] // 2
        layout = [(0, p) for p in pieces(d, 2)] + [(1, p) for p in pieces(hid, 2)]
        layout = [layout[i] for i in (2, 3, 0, 1)]
        far = [more[0], jax.ShapeDtypeStruct((more[1].shape[0], hid), BF16)]
    return pl.pallas_call(
        partial(kernel_a, n, layout, len(more)),
        out_shape=[sds((mb,) + sh, dt) for sh, dt in out] + gathered(n, far),
        grid=(mb,),
        in_specs=[
            pl.BlockSpec((pl.Squeezed(), 1, t), lambda b: (b, 0, 0)),
            per_block(t, d), whole(*wp.shape), whole(*wd.shape), whole(*wpt.shape), whole(*wk.shape),
        ]
        + [ANY] * len(more),
        out_specs=[per_block(*sh) for sh, _ in out] + [ANY] * len(more),
        scratch_shapes=[
            pltpu.VMEM((d // 128, t + 16, 128), F32),
            pltpu.VMEM((t + 16, 128), F32),
            pltpu.VMEM((KERNEL, 8, t), F32),
            pltpu.VMEM((half // 128, t + 16, 128), F32),
            pltpu.VMEM((72, t), F32),
            pltpu.VMEM((144, KERNEL * half), BF16),
            pltpu.VMEM((128, KERNEL * half), F32),
        ]
        + (gather_sems(n, layout) if more else []),
        compiler_params=params(1, 2 if more else None),
        name="mix_fwd",
    )(segr, xr, wp, wd, wpt, wk, *more)


QT = 1024


def seg_codes(segb, first):
    lane = lanes(segb.shape) - first
    hot = segb == lane.astype(F32)
    inside = (lane >= 0) & (lane < 24)
    return jnp.where(hot & inside, 1.0, 0.0), jnp.where(inside & ~hot, -1e30, 0.0)


def tile_points(n, plan, spots, i, tiles, h=0, heads=2):
    if plan is None:
        return
    step = pl.program_id(0) * pl.num_programs(1) + pl.program_id(1)
    for t in range(h, len(spots), heads):
        at = t // heads
        point((step == at // tiles) & (i == at % tiles), (lambda: greet(n)) if t == 0 else None, plan, t)


def end_points(plan):
    if plan is None:
        return
    last = (pl.program_id(0) == pl.num_programs(0) - 1) & (pl.program_id(1) == pl.num_programs(1) - 1)
    point(last, None, plan, plan.ticks - 1)


B_SPOTS = [5.0 * i for i in range(6)]


def kernel_b(n, layout, count, *refs):
    segt_ref, q_ref, k_ref, v_ref = refs[:4]
    srcs, (ctx_ref, lse_ref) = refs[4 : 4 + count], refs[4 + count : 6 + count]
    dsts, sems = refs[6 + count : 6 + 2 * count], refs[6 + 2 * count :]
    plan = gathers(n, srcs, dsts, layout, sems, B_SPOTS) if count else None
    t = q_ref.shape[1]
    tail = t - SEG_MOST
    low_half = lanes((1, 128)) < 64

    def finish(rows, outs, tops):
        both = jnp.where(low_half, outs[0], outs[1])
        sums = jnp.where(low_half, outs[1], outs[0])
        ctx_ref[0, rows, :] = (both / pltpu.roll(sums, 64, 1)).astype(BF16)
        lse_ref[0, rows, :] = jnp.where(low_half, tops[1], tops[0]) + jnp.log(sums)

    def one(q, k, v):
        scores = mm(q, k, NT)
        top = jnp.max(scores, -1, keepdims=True)
        return mm(jnp.exp(scores - top).astype(BF16), v), top

    k = k_ref[0, 0:SEG_MOST, :]
    v = v_ref[0, 0:SEG_MOST, :]
    one_b = jnp.ones((), BF16)
    vs = (jnp.where(low_half, v, one_b), jnp.where(low_half, one_b, v))

    def tile(i, carry):
        rows = pl.ds(pl.multiple_of(i * QT, QT), QT)
        q = q_ref[0, rows, :] * 0.125
        zero = jnp.zeros((), BF16)
        tile_points(n, plan, B_SPOTS, i, SEG_MOST // QT, heads=1)
        outs = [one(jnp.where(low_half, q, zero), k, vs[0])]
        outs.append(one(jnp.where(low_half, zero, q), k, vs[1]))
        finish(rows, [o[0] for o in outs], [o[1] for o in outs])
        return carry

    lax.fori_loop(0, SEG_MOST // QT, tile, 0)
    rows = pl.ds(SEG_MOST, tail)
    q = q_ref[0, rows, :] * 0.125
    kt = k_ref[0, rows, :]
    vt = v_ref[0, rows, :]
    segb = jnp.broadcast_to(segt_ref[...], (128, tail)).T
    outs = []
    for h in range(2):
        hot, pen = seg_codes(segb, 64 - 64 * h)
        mine = low_half if h == 0 else ~low_half
        outs.append(
            one(
                jnp.where(mine, q, pen.astype(BF16)),
                jnp.where(mine, kt, hot.astype(BF16)),
                jnp.where(mine, vt, one_b),
            )
        )
    finish(rows, [o[0] for o in outs], [o[1] for o in outs])
    end_points(plan)


def pair(t):
    return pl.BlockSpec((1, t, 128), lambda b, j: (b, 0, j))


def seg_tail(tail):
    return pl.BlockSpec((pl.Squeezed(), 1, tail), lambda b, *_: (b, 0, SEG_MOST // tail))


def stage_b(n, segt, q, k, v, more):
    mb, t, half = q.shape
    sds = jax.ShapeDtypeStruct
    layout, far = [], []
    if more:
        hid = more[0].shape[1] // 2
        cols = pieces(hid, 2)
        wide = [(0, (ALL, pl.ds(hid + i * (hid // 2), hid // 2)), p) for i, p in enumerate(cols)]
        tall = [(1, p) for p in pieces(more[1].shape[0], 4, True)]
        layout = tall[:2] + wide + tall[2:]
        far = [jax.ShapeDtypeStruct((more[0].shape[0], hid), BF16), more[1]]
    return pl.pallas_call(
        partial(kernel_b, n, layout, len(more)),
        out_shape=[sds((mb, t, half), BF16), sds((mb, t, half), F32)] + gathered(n, far),
        grid=(mb, half // 128),
        in_specs=[seg_tail(t - SEG_MOST), pair(t), pair(t), pair(t)] + [ANY] * len(more),
        out_specs=[pair(t), pair(t)] + [ANY] * len(more),
        scratch_shapes=gather_sems(n, layout) if more else [],
        compiler_params=params(2, 3 if more else None),
        name="att_fwd",
    )(segt, q, k, v, *more)


ROWS = 384


def norm_fwd(values):
    centre = values - jnp.mean(values, -1, keepdims=True)
    inv_std = lax.rsqrt(jnp.mean(centre * centre, -1, keepdims=True) + NORM_EPS)
    return centre * inv_std, inv_std


def norm_back(grad, normed, inv_std):
    one = jnp.mean(grad, -1, keepdims=True)
    two = jnp.mean(grad * normed, -1, keepdims=True)
    return inv_std * (grad - one - normed * two)


def gelu_both(x):
    cdf = 0.5 + 0.5 * lax.erf(x * 0.7071067811865476)
    bell = jnp.exp(x * (x * -0.5))
    return x * cdf, cdf + x * (bell * 0.3989422804014327)


def col_sum(v):
    return jnp.sum(v, 0, keepdims=True)


def kernel_c(
    ctx_ref, conv_ref, x_ref, cot_ref, wo_ref, wia_ref, wib_ref, wdn_ref, ln_ref,
    out_ref, dres_ref, dctx_ref, dconv_ref, gf_ref, gs_ref,
    joined, act, slope, dinner, go_ref, gi_ref, gd_ref, wi_ref,
):
    first = (pl.program_id(0) == 0) & (pl.program_id(1) == 0)
    last = (pl.program_id(0) == pl.num_programs(0) - 1) & (pl.program_id(1) == pl.num_programs(1) - 1)
    d = x_ref.shape[-1]
    half = d // 2
    hid = wi_ref.shape[1]

    @pl.when(first)
    def _():
        wi_ref[:, 0 : hid // 2] = wia_ref[...]
        wi_ref[:, hid // 2 :] = wib_ref[...]
        go_ref[...] = jnp.zeros_like(go_ref)
        gi_ref[...] = jnp.zeros_like(gi_ref)
        gd_ref[...] = jnp.zeros_like(gd_ref)
        gs_ref[...] = jnp.zeros_like(gs_ref)

    joined[:, 0:half] = ctx_ref[0]
    joined[:, half:] = conv_ref[0]
    gain1, shift1, gain2, shift2 = (ln_ref[16 + i : 17 + i, :] for i in range(4))
    normed1, inv1 = norm_fwd(mm(joined[...], wo_ref[...]) + x_ref[0].astype(F32))
    hidden = normed1 * gain1 + shift1
    hidden_low = hidden.astype(BF16)
    outers = []
    for g in range(2):
        cols = pl.ds(g * hid, hid)
        inner = mm(hidden_low[:, g * half : (g + 1) * half], wi_ref[g * half : (g + 1) * half, :])
        value, deriv = gelu_both(inner)
        act[:, cols] = value.astype(BF16)
        slope[:, cols] = deriv
        outers.append(mm(act[:, cols], wdn_ref[g * hid : (g + 1) * hid, :]))
    normed2, inv2 = norm_fwd(jnp.concatenate(outers, 1) + hidden)
    out_ref[0] = (normed2 * gain2 + shift2).astype(BF16)
    cot = cot_ref[0].astype(F32)
    gs_ref[2:3, :] += col_sum(cot * normed2)
    gs_ref[3:4, :] += col_sum(cot)
    d_sum = norm_back(cot * gain2, normed2, inv2)
    d_outer = d_sum.astype(BF16)
    d_hid = []
    for g in range(2):
        cols = pl.ds(g * hid, hid)
        mine = d_outer[:, g * half : (g + 1) * half]
        d_act = mm(mine, wdn_ref[g * hid : (g + 1) * hid, :], NT)
        gd_ref[:, cols] += mm(mine, act[:, cols], TN)
        dinner[:, cols] = (d_act * slope[:, cols]).astype(BF16)
        d_hid.append(mm(dinner[:, cols], wi_ref[g * half : (g + 1) * half, :], NT))
        gi_ref[g * half : (g + 1) * half, :] += mm(hidden_low[:, g * half : (g + 1) * half], dinner[:, cols], TN)
    d_hidden = jnp.concatenate(d_hid, 1) + d_sum
    gs_ref[0:1, :] += col_sum(d_hidden * normed1)
    gs_ref[1:2, :] += col_sum(d_hidden)
    d_res = norm_back(d_hidden * gain1, normed1, inv1)
    dres_ref[0] = d_res
    d_attn = d_res.astype(BF16)
    d_joined = mm(d_attn, wo_ref[...], NT)
    dctx_ref[0] = d_joined[:, 0:half].astype(BF16)
    dconv_ref[0] = d_joined[:, half:]
    go_ref[...] += mm(joined[...], d_attn, TN)

    @pl.when(last)
    def _():
        n, _, _ = gf_ref.shape
        rows = d // n
        tall = 2 * hid // n

        def emit(p, c):
            at = pl.ds(pl.multiple_of(p * rows, 8), rows)
            gi = gi_ref[at, :]
            go = go_ref[at, :]
            parts = [gi[:, j * half : (j + 1) * half] for j in range(hid // half)] + [go[:, 0:half], go[:, half:]]
            gf_ref[p, tall : tall + rows * len(parts), :] = jnp.concatenate(parts, 0).astype(BF16)
            return c

        lax.fori_loop(0, n, emit, 0)

        step = 4
        wide = step * tall

        def emit_down(i, c):
            block = gd_ref[:, pl.ds(pl.multiple_of(i * wide, 128), wide)].T.astype(BF16)
            for j in range(step):
                gf_ref[i * step + j, 0:tall, :] = block[j * tall : (j + 1) * tall, :]
            return c

        lax.fori_loop(0, n // step, emit_down, 0)


def stage_c(n, ctx, conv, x, cot, wo, wi_a, wi_b, wdn, ln):
    mb, t, d = x.shape
    half = d // 2
    hid = 2 * wi_a.shape[1]
    packed = (d * d + d * hid + 2 * hid * half) // (n * half)
    sds = jax.ShapeDtypeStruct

    def tile(cols):
        return pl.BlockSpec((1, ROWS, cols), lambda b, i: (b, i, 0))

    return pl.pallas_call(
        kernel_c,
        out_shape=[
            sds((mb, t, d), BF16), sds((mb, t, d), F32), sds((mb, t, half), BF16), sds((mb, t, half), F32),
            sds((n, packed, half), BF16), sds((8, d), F32),
        ],
        grid=(mb, t // ROWS),
        in_specs=[
            tile(half), tile(half), tile(d), tile(d),
            whole(*wo.shape), whole(*wi_a.shape), whole(*wi_b.shape), whole(*wdn.shape), whole(*ln.shape),
        ],
        out_specs=[
            tile(d), tile(d), tile(half), tile(half),
            whole(n, packed, half), whole(8, d),
        ],
        scratch_shapes=[
            pltpu.VMEM((ROWS, d), BF16),
            pltpu.VMEM((ROWS, 2 * hid), BF16),
            pltpu.VMEM((ROWS, 2 * hid), F32),
            pltpu.VMEM((ROWS, 2 * hid), BF16),
            pltpu.VMEM((d, d), F32),
            pltpu.VMEM((d, hid), F32),
            pltpu.VMEM((half, 2 * hid), F32),
            pltpu.VMEM((d, hid), BF16),
        ],
        compiler_params=params(2),
        name="ffn",
    )(ctx, conv, x, cot, wo, wi_a, wi_b, wdn, ln)


KT = 512
D_SPOTS = [1.9 * i for i in range(24)]


def kernel_d(n, cuts, *refs):
    count = 1 if cuts else 0
    segt_ref, q_ref, k_ref, v_ref, ctx_ref, lse_ref, do_ref = refs[:7]
    srcs, refs = refs[7 : 7 + count], refs[7 + count :]
    dq_ref, dk_ref, dv_ref = refs[:3]
    outs, refs = refs[3 : 3 + count], refs[3 + count :]
    qa, da, dqt, *rest = refs
    plan = scatters(n, cuts, srcs, outs, rest, D_SPOTS) if count else None
    t = q_ref.shape[1]
    tail = t - SEG_MOST
    lane = lanes((1, 128))
    low_half = lane < 64
    one_b = jnp.ones((), BF16)
    zero_b = jnp.zeros((), BF16)

    r = lax.broadcasted_iota(jnp.int32, (256, 128), 0) % 128
    c = lax.broadcasted_iota(jnp.int32, (256, 128), 1)
    swap = jnp.where((r < 64) != (c < 64), 1.0, 0.0).astype(BF16)
    prod = do_ref[0].astype(F32) * ctx_ref[0].astype(F32)
    hi, lo = split2(prod)
    dsum = mm(jnp.concatenate([hi, lo], 1), swap)
    q8 = q_ref[0] * 0.125
    do = do_ref[0]
    for stat, src, dst in ((lse_ref[0], q8, qa), (dsum, do, da)):
        pieces = split3(-stat)
        code = jnp.where(
            (lane & 63) == 0, pieces[0], jnp.where((lane & 63) == 1, pieces[1], jnp.where((lane & 63) == 2, pieces[2], zero_b))
        )
        dst[0] = jnp.where(low_half, src, code)
        dst[1] = jnp.where(low_half, code, src)

    def run(key_rows, q_rows, h, codes):
        mark = (lane & 63) < 3
        mine = low_half if h == 0 else ~low_half
        k = k_ref[0, key_rows, :]
        v = v_ref[0, key_rows, :]
        ka = jnp.where(mine, k, jnp.where(mark, one_b, zero_b))
        va = jnp.where(mine, v, jnp.where(mark, one_b, zero_b))
        qh = qa[h, q_rows, :]
        if codes is not None:
            hot, pen = codes
            qh = qh + pen
            ka = ka + hot
        p = jnp.exp(mm(ka, qh, NT))
        dp = mm(va, da[h, q_rows, :], NT)
        ds = (p * dp).astype(BF16)
        dv = mm(p.astype(BF16), do_ref[0, q_rows, :])
        dk = mm(ds, q_ref[0, q_rows, :] * 0.125)
        return ds, dk, dv, k

    main = pl.ds(0, SEG_MOST)

    def tile(i, carry):
        rows = pl.ds(pl.multiple_of(i * KT, KT), KT)
        halves = []
        for h in range(2):
            tile_points(n, plan, D_SPOTS, i, SEG_MOST // KT, h)
            ds, dk, dv, k = run(rows, main, h, None)
            part = mm(k[:, 64 * h : 64 * h + 64], ds, TN)
            dqt[64 * h : 64 * h + 64, :] = jnp.where(i == 0, part, dqt[64 * h : 64 * h + 64, :] + part)
            halves.append((dk, dv))
        dk_ref[0, rows, :] = jnp.where(low_half, halves[0][0], halves[1][0]).astype(BF16)
        dv_ref[0, rows, :] = jnp.where(low_half, halves[0][1], halves[1][1]).astype(BF16)
        return carry

    dqt[...] = jnp.zeros_like(dqt)
    lax.fori_loop(0, SEG_MOST // KT, tile, 0)
    dq_ref[0, main, :] = dqt[...].T * 0.125

    rows = pl.ds(SEG_MOST, tail)
    segb = jnp.broadcast_to(segt_ref[...], (128, tail)).T
    halves = []
    for h in range(2):
        hot, pen = seg_codes(segb, 64 - 64 * h + 8)
        ds, dk, dv, k = run(rows, rows, h, (hot.astype(BF16), pen.astype(BF16)))
        halves.append((dk, dv, mm(ds, k, TN)))
    for ref, i in ((dk_ref, 0), (dv_ref, 1)):
        ref[0, rows, :] = jnp.where(low_half, halves[0][i], halves[1][i]).astype(BF16)
    dq_ref[0, rows, :] = jnp.where(low_half, halves[0][2], halves[1][2]) * 0.125
    end_points(plan)


def stage_d(n, segt, q, k, v, ctx, lse, dctx, more):
    mb, t, half = q.shape
    cuts = scatter_cuts(more, 4)
    sds = jax.ShapeDtypeStruct
    return pl.pallas_call(
        partial(kernel_d, n, cuts),
        out_shape=[sds((mb, t, half), F32), sds((mb, t, half), BF16), sds((mb, t, half), BF16)]
        + [sds(w.shape[1:], F32) for w in more],
        grid=(mb, half // 128),
        in_specs=[seg_tail(t - SEG_MOST)] + [pair(t)] * 6 + [ANY] * len(more),
        out_specs=[pair(t)] * 3 + [whole(*w.shape[1:]) for w in more],
        scratch_shapes=[
            pltpu.VMEM((2, t, 128), BF16), pltpu.VMEM((2, t, 128), BF16), pltpu.VMEM((128, SEG_MOST), F32),
        ]
        + (scatter_scratch(n, cuts, more) if more else []),
        compiler_params=params(2, 4 if more else None),
        name="att_bwd",
    )(segt, q, k, v, ctx, lse, dctx, *more)


def kernel_e(
    s_ref, seg_ref, c_far, dconv_far, taps_far, mixed_far, q_far, dq_far, span_far, dk_far, dv_far, depth_far,
    x_far, dres_far, outr_far, wp_ref, wd_ref, wpt_ref, wk_ref, gs_ref,
    gx_far, out_far, gm_ref,
    pad, xs, segb, vt, dcs, dts, e_ref, er_ref, texp, dlt, rt, dm, dl, gacc, gp_ref, gpt_ref, gk_ref, small,
    c_ref, dconv_ref, taps_ref, mixed_ref, q_ref, dq_ref, span_ref, dk_ref, dv_ref, depth_ref,
    x_ref, dres_ref, out_ref_in, gx_ref, out_ref, in_sem, out_sem,
):
    t, d = x_ref.shape[1:]
    far = (
        c_far, dconv_far, taps_far, mixed_far, q_far, dq_far, span_far, dk_far, dv_far, depth_far,
        x_far, dres_far, outr_far,
    )
    near = (
        c_ref, dconv_ref, taps_ref, mixed_ref, q_ref, dq_ref, span_ref, dk_ref, dv_ref, depth_ref,
        x_ref, dres_ref, out_ref_in,
    )

    def fetch(i, block):
        return pltpu.make_async_copy(far[i].at[pl.ds(block, 1)], near[i], in_sem.at[i])

    def arrived(*which):
        for i in which:
            fetch(i, b).wait()

    def done_with(*which):
        @pl.when(b + 1 < pl.num_programs(0))
        def _():
            for i in which:
                fetch(i, b + 1).start()

    def put_back(j, block):
        cols = pl.ds(j * 128, 128)
        return [
            pltpu.make_async_copy(src.at[:, :, cols], dst.at[pl.ds(block, 1), :, cols], out_sem.at[k, j])
            for k, (src, dst) in enumerate(((gx_ref, gx_far), (out_ref, out_far)))
        ]

    half = d // 2
    nch = d // 128
    b = pl.program_id(0)
    s = s_ref[b]

    @pl.when(b == 0)
    def _():
        for i in range(len(far)):
            fetch(i, 0).start()
        fill_expander(e_ref)
        col = lanes((128, 128))
        upper = jnp.where(lax.broadcasted_iota(jnp.int32, (128, 128), 0) >= 64, 1, 0)
        for o in range(KERNEL):
            for j in range(half // 128):
                one = jnp.where(col == upper + (o * 8 + 2 * j), 1.0, 0.0).astype(BF16)
                er_ref[pl.ds(o * half + j * 128, 128), :] = one
        for ref in (xs, dts, dcs):
            n = ref.shape[0]
            ref[:, 0:8, :] = jnp.zeros((n, 8, 128), F32)
            ref[:, t + 8 : t + 16, :] = jnp.zeros((n, 8, 128), F32)
        gp_ref[...] = jnp.zeros_like(gp_ref)
        gpt_ref[...] = jnp.zeros_like(gpt_ref)
        gk_ref[...] = jnp.zeros_like(gk_ref)
        gacc[...] = jnp.zeros_like(gacc)

    fill_segments(seg_ref, segb, vt)
    arrived(0, 1)
    cw = xs
    for j in range(nch // 2):
        cols = pl.ds(j * 128, 128)
        cw[j, 8 : t + 8, :] = c_ref[0, :, cols].astype(F32)
        dcs[j, 8 : t + 8, :] = dconv_ref[0, :, cols]
    done_with(0, 1)

    def dtap_tile(i, carry):
        r0 = pl.multiple_of(i * 128, 128)
        rows = pl.ds(r0, 128)
        acc = None
        for o in range(KERNEL):
            prods = [
                (cw[j, pl.ds(8 + r0 + o - REACH, 128), :] * dcs[j, pl.ds(8 + r0, 128), :]).astype(BF16)
                for j in range(nch // 2)
            ]
            part = mm(jnp.concatenate(prods, 1), er_ref[o * half : (o + 1) * half, :])
            acc = part if acc is None else acc + part
        dlt[:, rows] = acc.T[0:72, :]
        return carry

    lax.fori_loop(0, t // 128, dtap_tile, 0)

    arrived(2)
    taps = [taps_ref[0, o * 8 : o * 8 + 8, :] for o in range(KERNEL)]
    dtaps = [dlt[o * 8 : o * 8 + 8, :] * vt[o] for o in range(KERNEL)]
    mean = taps[0] * dtaps[0]
    for o in range(1, KERNEL):
        mean = mean + taps[o] * dtaps[o]
    for o in range(KERNEL):
        dl[o * 8 : o * 8 + 8, :] = taps[o] * (dtaps[o] - mean)
        tv = taps[o] * vt[o]
        move = (o - REACH) % t
        rt[o * 8 : o * 8 + 8, :] = pltpu.roll(tv, move, 1) if move else tv

    done_with(2)
    arrived(*range(3, 10))

    def point_tile(i, carry):
        r0 = pl.multiple_of(i * 384, 128)
        rows = pl.ds(r0, 384)
        dlog = dl[:, rows].astype(BF16)
        d_mixed = mm(dlog, wk_ref[...], TN)
        gk_ref[...] += mm(dlog, mixed_ref[0, rows, :])
        d_span = (d_mixed * q_ref[0, rows, :].astype(F32)).astype(BF16)
        dm[rows, 0:half] = (dq_ref[0, rows, :] + d_mixed * span_ref[0, rows, :]).astype(BF16)
        dm[rows, half : 2 * half] = dk_ref[0, rows, :]
        dm[rows, 2 * half : 3 * half] = dv_ref[0, rows, :]
        gpt_ref[...] += mm(depth_ref[0, rows, :], d_span, TN)
        d_depth = mm(d_span, wpt_ref[...], NT)
        for j in range(nch):
            dts[j, pl.ds(8 + r0, 384), :] = d_depth[:, j * 128 : (j + 1) * 128]
        return carry

    lax.fori_loop(0, t // 384, point_tile, 0)
    done_with(*range(3, 10))

    def dc_tile(i, carry):
        r0 = pl.multiple_of(i * 128, 128)
        rows = pl.ds(r0, 128)
        texp[...] = expand_taps(rt[:, rows], e_ref)
        for j in range(nch // 2):
            acc = None
            for o in range(KERNEL):
                part = dcs[j, pl.ds(8 + r0 - o + REACH, 128), :] * texp[:, o * half + j * 128 : o * half + (j + 1) * 128]
                acc = part if acc is None else acc + part
            dm[rows, pl.ds(3 * half + j * 128, 128)] = acc.astype(BF16)
        return carry

    lax.fori_loop(0, t // 128, dc_tile, 0)

    arrived(10, 11)
    for j in range(nch):
        xs[j, 8 : t + 8, :] = x_ref[0, :, pl.ds(j * 128, 128)].astype(F32)

    def proj_tile(i, carry):
        r0 = pl.multiple_of(i * 384, 128)
        rows = pl.ds(r0, 384)
        gp_ref[...] += mm(x_ref[0, rows, :], dm[rows, :], TN)
        gx = mm(dm[rows, :], wp_ref[...], NT) + dres_ref[0, rows, :]
        for j in range(nch):
            pad[j, pl.ds(r0, 384), :] = gx[:, j * 128 : (j + 1) * 128]
        return carry

    lax.fori_loop(0, t // 384, proj_tile, 0)

    done_with(10, 11)

    def depth_tile(r0, masked):
        masks = mask_rows(segb, r0, 128) if masked else None
        for j in range(nch):
            acc = pad[j, pl.ds(r0, 128), :]
            own = dts[j, pl.ds(8 + r0, 128), :]
            for o in range(KERNEL):
                w = wd_ref[KERNEL - 1 - o : KERNEL - o, pl.ds(j * 128, 128)]
                near = dts[j, pl.ds(8 + r0 + o - REACH, 128), :]
                xw = xs[j, pl.ds(8 + r0 + o - REACH, 128), :]
                if masked:
                    near = near * masks[o]
                    xw = xw * masks[o]
                acc = acc + near * w
                term = (own * xw).reshape(16, 8, 128)
                gacc[o, :, pl.ds(j * 128, 128)] += jnp.sum(term, 0)
            pad[j, pl.ds(r0, 128), :] = acc

    masked_tiles(t, depth_tile)

    arrived(12)

    @pl.when(b > 0)
    def _():
        for j in range(nch):
            for copy in put_back(j, b - 1):
                copy.wait()

    for j in range(nch):
        cols = pl.ds(j * 128, 128)
        pad[j, pl.ds(t, 128), :] = pad[j, 0:128, :]
        back = t - s
        first = pl.ds(back, 128)
        gx_ref[0, :, cols] = xs[j, 8 : t + 8, :]
        xs[j, 0:128, :] = pad[j, first, :]
        gx_ref[0, 0:128, cols] = xs[j, 0:128, :]
        gx_ref[0, 128:, cols] = pad[j, pl.ds(128 - s, t - 128), :]
        pad[j, 0:t, :] = out_ref_in[0, :, cols].astype(F32)
        pad[j, pl.ds(t, 128), :] = pad[j, 0:128, :]
        out_ref[0, 0:128, cols] = pad[j, first, :].astype(BF16)
        out_ref[0, 128:, cols] = pad[j, pl.ds(128 - s, t - 128), :].astype(BF16)
        for copy in put_back(j, b):
            copy.start()
    done_with(12)

    @pl.when(b == pl.num_programs(0) - 1)
    def _():
        n = gm_ref.shape[0]
        rows = d // n
        small[...] = jnp.zeros_like(small)
        for o in range(KERNEL):
            small[o : o + 1, :] = jnp.sum(gacc[o], 0, keepdims=True)
        small[16:24, :] = gs_ref[...]
        row = lax.broadcasted_iota(jnp.int32, (128, 72), 0)
        col = lax.broadcasted_iota(jnp.int32, (128, 72), 1)
        order = jnp.where((row < HEADS * KERNEL) & (row % KERNEL * 8 + row // KERNEL == col), 1.0, 0.0).astype(BF16)
        gk = mm(order, gk_ref[...].astype(BF16)).astype(BF16)
        gk = mm(gk, piece_rows(d), NT)
        for j in range(nch):
            cols = pl.ds(j * 128, 128)
            pad[0, cols, :] = small[:, cols].T
            pad[1, cols, :] = gk[:, j * 128 : (j + 1) * 128].T

        def emit(p, c):
            at = pl.ds(pl.multiple_of(p * rows, 8), rows)
            gp = gp_ref[at, :]
            parts = [gp[:, j * half : (j + 1) * half] for j in range(gp.shape[1] // half)] + [gpt_ref[at, :]]
            parts.append(jnp.concatenate([pad[0, at, :], pad[1, at, :], jnp.zeros((rows, half - 256), F32)], 1))
            gm_ref[p] = jnp.concatenate(parts, 0).astype(BF16)
            return c

        lax.fori_loop(0, n, emit, 0)
        for j in range(nch):
            for copy in put_back(j, b):
                copy.wait()


def stage_e(n, s, segr, x, out_r, dres, dconv, dq, dk, dv, q, c, depth, span, mixed, taps, wp, wd, wpt, wk, gs):
    mb, t, d = x.shape
    half = d // 2
    packed = (d * 2 * d + d * half) // (n * half) + d // n
    sds = jax.ShapeDtypeStruct

    blocks = (c, dconv, taps, mixed, q, dq, span, dk, dv, depth, x, dres, out_r)
    return pl.pallas_call(
        kernel_e,
        out_shape=[
            sds((mb, t, d), F32), sds((mb, t, d), BF16), sds((n, packed, half), BF16),
        ],
        grid_spec=pltpu.PrefetchScalarGridSpec(
            num_scalar_prefetch=1,
            grid=(mb,),
            in_specs=[pl.BlockSpec((pl.Squeezed(), 1, t), lambda b, *_: (b, 0, 0))]
            + [ANY] * len(blocks)
            + [whole(*w.shape) for w in (wp, wd, wpt, wk, gs)],
            out_specs=[ANY, ANY, whole(n, packed, half)],
            scratch_shapes=[
                pltpu.VMEM((d // 128, t + 128, 128), F32),
                pltpu.VMEM((d // 128, t + 16, 128), F32),
                pltpu.VMEM((t + 16, 128), F32),
                pltpu.VMEM((KERNEL, 8, t), F32),
                pltpu.VMEM((half // 128, t + 16, 128), F32),
                pltpu.VMEM((d // 128, t + 16, 128), F32),
                pltpu.VMEM((144, KERNEL * half), BF16),
                pltpu.VMEM((KERNEL * half, 128), BF16),
                pltpu.VMEM((128, KERNEL * half), F32),
                pltpu.VMEM((72, t), F32),
                pltpu.VMEM((72, t), F32),
                pltpu.VMEM((t, 2 * d), BF16),
                pltpu.VMEM((72, t), F32),
                pltpu.VMEM((KERNEL, 8, d), F32),
                pltpu.VMEM(wp.shape, F32),
                pltpu.VMEM(wpt.shape, F32),
                pltpu.VMEM((72, half), F32),
                pltpu.VMEM((128, d), F32),
            ]
            + [pltpu.VMEM((1,) + v.shape[1:], v.dtype) for v in blocks]
            + [
                pltpu.VMEM((1, t, d), F32),
                pltpu.VMEM((1, t, d), BF16),
                pltpu.SemaphoreType.DMA((len(blocks),)),
                pltpu.SemaphoreType.DMA((2, d // 128)),
            ],
        ),
        compiler_params=params(1),
        name="mix_bwd",
    )(s, segr, *blocks, wp, wd, wpt, wk, gs)


def prep_kernel(seg_ref, wd_ref, wk_ref, norm_ref, s_ref, segr_ref, small_ref, flip):
    mb, t = seg_ref.shape
    span = t - SEG_MOST + 1
    pos = lanes((1, t))
    for b in range(mb):
        row = seg_ref[b : b + 1, :].astype(F32)
        later = pltpu.roll(jnp.broadcast_to(row, (8, t)), t - (SEG_MOST - 1), 1)
        hit = (later[0:1, :] == row) & (pos < span)
        s = jnp.sum(jnp.where(hit, pos.astype(F32), 0.0)).astype(jnp.int32)
        s_ref[b] = s
        segr_ref[b] = pltpu.roll(jnp.broadcast_to(row, (8, t)), t - s, 1)[0:1, :]
    flip[...] = jnp.zeros_like(flip)
    rows = wd_ref.shape[1]
    flip[0:KERNEL, 0:rows] = wd_ref[...].astype(F32)
    flip[16:20, 0:rows] = norm_ref[...].astype(F32)
    row = lax.broadcasted_iota(jnp.int32, (8 * KERNEL, HEADS * KERNEL), 0)
    col = lanes((8 * KERNEL, HEADS * KERNEL))
    order = jnp.where(col % KERNEL * 8 + col // KERNEL == row, 1.0, 0.0).astype(BF16)
    heads = mm(order, wk_ref[...]).astype(BF16)
    flip[32 : 32 + 8 * KERNEL, 0:rows] = mm(heads, piece_rows(rows), NT)
    small_ref[...] = flip[...].T[0:rows, :]


def prep(segments, w_depth, w_kernel, norms):
    mb, t = segments.shape
    rows = w_depth.shape[0]
    sds = jax.ShapeDtypeStruct
    vmem = pl.BlockSpec(memory_space=pltpu.VMEM)
    return pl.pallas_call(
        prep_kernel,
        out_shape=[sds((mb,), jnp.int32), sds((mb, 1, t), F32), sds((rows, 128), F32)],
        in_specs=[vmem] * 4,
        out_specs=[pl.BlockSpec(memory_space=pltpu.SMEM), vmem, vmem],
        scratch_shapes=[pltpu.VMEM((128, -(-rows // 128) * 128), F32)],
        name="prep",
    )(segments, w_depth.T, w_kernel.T, norms)


def finish_kernel(f_ref, m_ref, gp_ref, gdep_ref, gpt_ref, gk_ref, go_ref, gi_ref, gd_ref, gs_ref, flip):
    half = f_ref.shape[1]
    rows = gp_ref.shape[0]
    tall = gd_ref.shape[0]
    gd_ref[...] = f_ref[0:tall, :]
    for j in range(gi_ref.shape[1] // half):
        gi_ref[:, j * half : (j + 1) * half] = f_ref[tall + j * rows : tall + (j + 1) * rows, :]
    tall = tall + rows * (gi_ref.shape[1] // half)
    for j in range(2):
        go_ref[:, j * half : (j + 1) * half] = f_ref[tall + j * rows : tall + (j + 1) * rows, :]
    wide = gp_ref.shape[1] // half
    for j in range(wide):
        gp_ref[:, j * half : (j + 1) * half] = m_ref[j * rows : (j + 1) * rows, :]
    gpt_ref[...] = m_ref[wide * rows : (wide + 1) * rows, :]
    flip[...] = jnp.zeros_like(flip)
    flip[0:rows, :] = m_ref[(wide + 1) * rows : (wide + 2) * rows, 0:256]
    first = flip[:, 0:128].T
    gdep_ref[...] = first[0:KERNEL, 0:rows]
    gs_ref[...] = first[16:24, 0:rows]
    gk_ref[...] = flip[:, 128:256].T[0 : HEADS * KERNEL, 0 : rows // 2]


def finish(n, d, hid, f, m):
    half = d // 2
    sds = jax.ShapeDtypeStruct
    rows = d // n
    return pl.pallas_call(
        finish_kernel,
        out_shape=[
            sds((rows, 2 * d), F32), sds((KERNEL, rows), F32), sds((rows, half), F32), sds((HEADS * KERNEL, half // n), F32),
            sds((rows, d), F32), sds((rows, hid), F32), sds((2 * hid // n, half), F32), sds((8, rows), F32),
        ],
        scratch_shapes=[pltpu.VMEM((128, 256), F32)],
        name="finish",
    )(f, m)


def side_by_side(block, parts):
    units, _, cols = block.shape
    return block.reshape(units, parts, PIECE, cols).transpose(0, 2, 1, 3).reshape(units * PIECE, parts * cols)


def native_sums(gf, gm, d, hid):
    gf, gm = gf.astype(F32), gm.astype(F32)
    half = d // 2
    tall = 2 * hid * PIECE // d
    wide = hid // half * PIECE
    many_p = 2 * d // half
    g_down = gf[:, :tall].reshape(-1, half)
    g_in = side_by_side(gf[:, tall : tall + wide], hid // half)
    g_out = side_by_side(gf[:, tall + wide :], 2)
    g_proj = side_by_side(gm[:, : many_p * PIECE], many_p)
    g_point = gm[:, many_p * PIECE : (many_p + 1) * PIECE].reshape(-1, half)
    small = gm[:, (many_p + 1) * PIECE :]
    g_kernel = small[:, : PIECE // 2, 128 : 128 + HEADS * KERNEL].reshape(half, -1)
    small = small[:, :, 0:24].reshape(d, -1)
    grads = [g_proj, small[:, :KERNEL], g_point, g_kernel, g_out, g_in, g_down, small[:, 16:]]
    return [lax.psum_scatter(g, "tok", scatter_dimension=0, tiled=True) for g in grads]


def rows_of(w):
    return w.reshape(-1, w.shape[-1])


def shards(n, tokens, segments, cotangent, w_proj, w_depth, w_point, w_kernel, w_out, g1, b1, w_in, w_down, g2, b2):
    d = tokens.shape[-1]
    hid = w_in.shape[1]
    units = d // PIECE
    own = n == units
    norms = [g1, b1, g2, b2]
    if own:
        more_a, more_b = [w_out, w_in], [w_in, w_down]
    else:
        given = [w_proj, w_in, w_down, w_point, w_out, w_depth, w_kernel] + norms
        wp, wi, wdn, wpt, wo, w_depth, w_kernel, *norms = [lax.all_gather(w, "tok", axis=0, tiled=True) for w in given]
        more_a = more_b = []
    s, segr, small = prep(segments[:, 0], w_depth, w_kernel, jnp.stack(norms))
    xr, cotr, wd_rows, wk_rows, *got = stage_front(n, s, tokens, cotangent, small, w_proj, w_point, own)
    if own:
        wp, wpt = (rows_of(w) for w in got)
    q, k, v, c, depth, span, mixed, taps, conv, *got_a = stage_a(n, segr, xr, wp, wd_rows, wpt, wk_rows, more_a)
    ctx, lse, *got_b = stage_b(n, segr, q, k, v, more_b)
    if own:
        wo, wi_a, wi_b, wdn = (rows_of(w) for w in got_a + got_b)
    else:
        wi_a, wi_b = jnp.split(wi, 2, 1)
    out_r, dres, dctx, dconv, gf, g_small = stage_c(units, ctx, conv, xr, cotr, wo, wi_a, wi_b, wdn, wd_rows)
    dq, dk, dv, *sums = stage_d(n, segr, q, k, v, ctx, lse, dctx, [gf] if own else [])
    gx, out, gm = stage_e(
        units, s, segr, xr, out_r, dres, dconv, dq, dk, dv, q, c, depth, span, mixed, taps, wp, wd_rows, wpt, wk_rows,
        g_small,
    )
    if own:
        sums = finish(n, d, hid, sums[0], scatter_all(n, 1, [gm], 6)[0])
        sums = [v.T if i in (1, 3, 7) else v for i, v in enumerate(sums)]
    else:
        sums = native_sums(gf, gm, d, hid)
    g_proj, g_depth, g_point, g_kernel, g_out, g_in, g_down, g_vec = sums
    return (
        out, gx, g_proj, g_depth, g_point, g_kernel, g_out, g_vec[:, 0], g_vec[:, 1], g_in, g_down,
        g_vec[:, 2], g_vec[:, 3],
    )


def solution(mesh):
    rows, vec, act = P("tok", None), P("tok"), P(None, "tok", None)
    in_specs = (act, act, act, rows, rows, rows, rows, rows, vec, vec, rows, rows, vec, vec)
    out_specs = (act, act, rows, rows, rows, rows, rows, vec, vec, rows, rows, vec, vec)
    run = partial(shards, mesh.shape["tok"])
    return jax.shard_map(run, mesh=mesh, in_specs=in_specs, out_specs=out_specs, check_vma=False)
```
